32 devices in a mesh: dp: 4 (over x, core), ctx: 2 (over y), tensor: 4 (over z).
Axes of the slice: x: 2, y: 2, z: 4, core: 2. Of those that a mesh axis runs over, the one named last changes fastest.
Arguments:
- tokens: bfloat16 [4096, 2048], P(('dp', 'ctx')), may hold values from -6 to 6
- cotangent: bfloat16 [4096, 2048], P(('dp', 'ctx')), may hold values from -6 to 6
- first_gain: bfloat16 [2048], P('dp'), may hold values from 0.5 to 1.5
- query_weight: bfloat16 [2048, 2048], P('dp', 'tensor'), may hold values from -0.5 to 0.5
- key_weight: bfloat16 [2048, 512], P('dp', 'tensor'), may hold values from -0.5 to 0.5
- value_weight: bfloat16 [2048, 512], P('dp', 'tensor'), may hold values from -0.125 to 0.125
- output_weight: bfloat16 [2048, 2048], P('tensor', 'dp'), may hold values from -4 to 4
- second_gain: bfloat16 [2048], P('dp'), may hold values from 0.5 to 1.5
- gate_weight: bfloat16 [2048, 8192], P('dp', 'tensor'), may hold values from -0.125 to 0.125
- up_weight: bfloat16 [2048, 8192], P('dp', 'tensor'), may hold values from -0.125 to 0.125
- down_weight: bfloat16 [8192, 2048], P('tensor', 'dp'), may hold values from -0.5 to 0.5
- block_order: int32 [4, 4], P('dp'), may hold values from 0 to 3, each once within a row
- prefix_seen: int32 [4, 1], P('dp'), may hold values from 1 to 512, as said below
Outputs:
- layer_out: bfloat16 [4096, 2048], P(('dp', 'ctx'))
- tokens_grad: bfloat16 [4096, 2048], P(('dp', 'ctx'))
- first_gain_grad: float32 [2048], P('dp')
- query_grad: float32 [2048, 2048], P('dp', 'tensor')
- key_grad: float32 [2048, 512], P('dp', 'tensor')
- value_grad: float32 [2048, 512], P('dp', 'tensor')
- output_grad: float32 [2048, 2048], P('tensor', 'dp')
- second_gain_grad: float32 [2048], P('dp')
- gate_grad: float32 [2048, 8192], P('dp', 'tensor')
- up_grad: float32 [2048, 8192], P('dp', 'tensor')
- down_grad: float32 [8192, 2048], P('tensor', 'dp')
The draws below stay inside these ranges and needn't reach their ends.
Inputs may be any that keep to these rules, and one draw needn't show every extreme that they name: Each row is a permutation. A group's sequences are its prompt of 512 tokens followed by 1 continuations of 512 tokens; block_order[g, b] names which block of 256 tokens of them rows b * 256 to (b + 1) * 256 - 1 of group g hold. Continuation c of group g follows the first prefix_seen[g, c] tokens of the group's prompt. The largest value over all groups is exactly 512.
All inputs are finite; a program needn't handle non-finite values.
Results may differ from the reference program's by a relative error of at most 0.023.
Values may be sent and summed in bfloat16 or wider, within the bound.
No kernel may reach another device: no remote copies, remote signals or barrier semaphores. Data moves between devices by JAX's collectives and lax.ppermute only.
A program may use at most 192 MiB of HBM per device.

```python
import jax
import jax.numpy as jnp
from jax import lax

D = 2048
H = 32
KVH = 8
HD = 64
FF = 8192
CLEN = 512
GROUPS = 4
GROUP = 1024
PROMPT = 512
CONTS = 1
BLK = 256
NBLK = 4
TOKENS = 4096
N_DP = 4


def draw_prefix_seen(key, part):
    values = jax.random.randint(key, (GROUPS, CONTS), 1, PROMPT + 1, dtype=jnp.int32)
    return values.at[0, 0].set(PROMPT)


def spiked(entries, own_key, source, target, blocks, factor):
    owner, partner = [(jnp.arange(entries.shape[position]) // (entries.shape[position] // blocks)).reshape([-1 if axis == position else 1 for axis in range(entries.ndim)]) for position in (source, target)]
    chosen = jax.random.permutation(own_key, blocks)[partner]
    strong = (owner == chosen) | (owner == (partner + blocks // 2) % blocks)
    return jnp.where(strong, factor * entries, entries)


def block_scale(rng, shape, split, smallest, high):
    def one(axis_at, shards_of):
        heights = jax.random.uniform(jax.random.fold_in(jax.random.fold_in(rng, 6), axis_at), (shards_of,), jnp.float32, smallest / len(split), high / len(split))
        return jnp.repeat(jnp.exp(heights), shape[axis_at] // shards_of).reshape((-1,) + (1,) * (len(shape) - axis_at - 1))

    factor_of = one(*split[0])
    for cut in split[1:]:
        factor_of = factor_of * one(*cut)
    return factor_of


def gaussian(stream_key, extent, spread, most, shards=(), kind=jnp.bfloat16):
    level = block_scale(stream_key, extent, shards, -0.22, 0.18) if shards else 1.0
    array = jax.random.normal(stream_key, extent, jnp.float32) * spread * level
    return jnp.minimum(jnp.maximum(array, -most), most).astype(kind)


def gaussian_with(own_key, dims, scale, most, split, heavy, kind=jnp.bfloat16):
    drawn = scale * jax.random.normal(own_key, dims, jnp.float32)
    if split:
        drawn = drawn * block_scale(own_key, dims, split, -0.22, 0.18)
    return jnp.clip(spiked(drawn, jax.random.fold_in(own_key, 3), *heavy), -most, most).astype(kind)


def setup_inputs(seed: int = 0) -> dict:
    splits = jax.random.split(jax.random.key(seed), 14)
    return {
        "tokens": gaussian_with(splits[0], (TOKENS, D), 1.0, 6.0, ((0, 8),), (0, 1, 8, 2.0)),
        "cotangent": gaussian_with(splits[1], (TOKENS, D), 1.0, 6.0, ((0, 8),), (0, 1, 8, 2.0)),
        "first_gain": jnp.clip(1.0 + 0.1 * jax.random.normal(splits[2], (D,), jnp.float32), 0.5, 1.5).astype(jnp.bfloat16),
        "query_weight": gaussian(splits[3], (D, H * HD), (D // 16) ** -0.5, 0.5, ((0, 4), (1, 4))),
        "key_weight": gaussian(splits[4], (D, KVH * HD), (D // 16) ** -0.5, 0.5, ((0, 4), (1, 4))),
        "value_weight": gaussian(splits[5], (D, KVH * HD), D ** -0.5, 0.125, ((0, 4), (1, 4))),
        "output_weight": gaussian(splits[6], (H * HD, D), (max(H * HD // 1024, 1)) ** -0.5, 4.0, ((0, 4), (1, 4))),
        "second_gain": jnp.clip(1.0 + 0.1 * jax.random.normal(splits[7], (D,), jnp.float32), 0.5, 1.5).astype(jnp.bfloat16),
        "gate_weight": gaussian(splits[8], (D, FF), D ** -0.5, 0.125, ((0, 4), (1, 4))),
        "up_weight": gaussian(splits[9], (D, FF), D ** -0.5, 0.125, ((0, 4), (1, 4))),
        "down_weight": gaussian(splits[10], (FF, D), (FF // 64) ** -0.5, 0.5, ((0, 4), (1, 4))),
        "block_order": jax.vmap(lambda own: jax.random.permutation(own, NBLK))(jax.random.split(splits[11], GROUPS)).reshape((GROUPS, NBLK)).astype(jnp.int32),
        "prefix_seen": draw_prefix_seen(jax.random.fold_in(splits[13], 71), 0),
    }


EPSILON = 1e-05
ROPE_BASE = 10000000.0
ATTN_SCALE = 0.015625
RESIDUAL = 0.22
NEGATIVE = -1e+30
HIGHEST = lax.Precision.HIGHEST

@jax.custom_vjp
def low(v):
    return lax.optimization_barrier(v.astype(jnp.bfloat16)).astype(jnp.float32)

@jax.custom_vjp
def low_back(v):
    return v

def low_keep(v):
    return (low(v), None)

def low_pass(kept, grad):
    return (grad,)

def back_keep(v):
    return (v, None)

def back_low(kept, grad):
    return (low(grad),)
low.defvjp(low_keep, low_pass)
low_back.defvjp(back_keep, back_low)

def product(left, right):
    return jnp.dot(left, right, precision=HIGHEST, preferred_element_type=jnp.float32)

def normalize(values, gain):
    return values * lax.rsqrt(lax.optimization_barrier(jnp.mean(values * values, axis=-1, keepdims=True)) + EPSILON) * gain

def rotate(values, places, sign):
    head_count = values.shape[1] // HD
    half_size = HD // 2
    freq = ROPE_BASE ** (-(jnp.arange(half_size, dtype=jnp.float32) * 2.0) / HD)
    angle = places.astype(jnp.float32)[:, None] * freq[None, :]
    cosine = jnp.cos(angle)[:, None]
    sine = (jnp.sin(angle) * sign)[:, None]
    shaped = values.reshape(values.shape[0], head_count, 2, half_size)
    first = shaped[:, :, 0]
    second = shaped[:, :, 1]
    out_first = first * cosine - second * sine
    out_second = second * cosine + first * sine
    return jnp.stack([out_first, out_second], axis=2).reshape(values.shape)

def token_places(row_ids, order_row, seen_row, prompt_len, block_rows, cont_len):
    block_total = order_row.shape[0]
    block_pick = (row_ids // block_rows)[:, None] == jnp.arange(block_total, dtype=jnp.int32)[None, :]
    chosen = lax.optimization_barrier(jnp.sum(jnp.where(block_pick, order_row[None, :], 0), axis=1)).astype(jnp.int32)
    global_ids = (chosen * block_rows + row_ids % block_rows).astype(jnp.int32)
    in_prompt = global_ids < prompt_len
    segment = jnp.where(in_prompt, 0, 1 + (global_ids - prompt_len) // cont_len).astype(jnp.int32)
    cont_count = seen_row.shape[0]
    which_cont = (segment - 1)[:, None] == jnp.arange(cont_count, dtype=jnp.int32)[None, :]
    limit = lax.optimization_barrier(jnp.sum(jnp.where(which_cont, seen_row[None, :], 0), axis=1)).astype(jnp.int32)
    places = jnp.where(in_prompt, global_ids, limit + (global_ids - prompt_len) % cont_len).astype(jnp.int32)
    return (segment, places, limit)

def visible(query_seg, query_pos, query_lim, key_seg, key_pos):
    same_seq = (query_seg[:, None] == key_seg[None, :]) & (key_pos[None, :] <= query_pos[:, None])
    shared = (key_seg[None, :] == 0) & (key_pos[None, :] < query_lim[:, None])
    return same_seq | shared

def group_attention(queries, keys_rot, values_low, seg_row, pos_row, lim_row):
    block_len = min(512, GROUP)
    block_count = GROUP // block_len
    key_heads = keys_rot.reshape(GROUP, KVH, HD)
    value_heads = values_low.reshape(GROUP, KVH, HD)

    def one_block(parts):
        query_block, seg_block, pos_block, lim_block = parts
        heads = query_block.reshape(block_len, KVH, H // KVH, HD)
        scores = jnp.einsum('qgrd,tgd->grqt', heads, key_heads, precision=HIGHEST) * ATTN_SCALE
        scores = low_back(scores)
        mask = visible(seg_block, pos_block, lim_block, seg_row, pos_row)
        scores = jnp.where(mask[None, None], scores, NEGATIVE)
        probs = low(jax.nn.softmax(scores, axis=-1))
        mixed = jnp.einsum('grqt,tgd->qgrd', probs, value_heads, precision=HIGHEST)
        return mixed.reshape(block_len, H * HD)
    blocks = lax.map(jax.checkpoint(one_block), (queries.reshape(block_count, block_len, H * HD), seg_row.reshape(block_count, block_len), pos_row.reshape(block_count, block_len), lim_row.reshape(block_count, block_len)))
    return blocks.reshape(GROUP, H * HD)

def reference(tokens, cotangent, first_gain, query_weight, key_weight, value_weight, output_weight, second_gain, gate_weight, up_weight, down_weight, block_order, prefix_seen):
    row_ids = jnp.arange(GROUP, dtype=jnp.int32)

    def places_of(order_row, seen_row):
        return token_places(row_ids, order_row, seen_row, PROMPT, BLK, CLEN)
    seg_all, pos_all, lim_all = jax.vmap(places_of)(block_order, prefix_seen)
    flat_pos = pos_all.reshape(TOKENS)

    def forward(inputs, gain_one, query_w, key_w, value_w, output_w, gain_two, gate_w, up_w, down_w):
        normed = low(normalize(inputs, gain_one))
        queries = low(rotate(low_back(product(normed, query_w)), flat_pos, 1.0))
        keys_rot = low(rotate(low_back(product(normed, key_w)), flat_pos, 1.0))
        values_low = low(low_back(product(normed, value_w)))

        def per_group(parts):
            return group_attention(*parts)
        mixed = lax.map(per_group, (queries.reshape(N_DP, GROUP, H * HD), keys_rot.reshape(N_DP, GROUP, KVH * HD), values_low.reshape(N_DP, GROUP, KVH * HD), seg_all, pos_all, lim_all))
        attended = low(low_back(mixed.reshape(TOKENS, H * HD)))
        branch = low_back(product(attended, output_w))
        middle = inputs + RESIDUAL * branch
        normed_two = low(normalize(middle, gain_two))
        gate = low_back(product(normed_two, gate_w))
        upper = low_back(product(normed_two, up_w))
        hidden = low(jax.nn.silu(gate) * upper)
        branch_two = low_back(product(hidden, down_w))
        return middle + RESIDUAL * branch_two
    floats = (tokens.astype(jnp.float32), first_gain.astype(jnp.float32), query_weight.astype(jnp.float32), key_weight.astype(jnp.float32), value_weight.astype(jnp.float32), output_weight.astype(jnp.float32), second_gain.astype(jnp.float32), gate_weight.astype(jnp.float32), up_weight.astype(jnp.float32), down_weight.astype(jnp.float32))
    result, pullback = jax.vjp(forward, *floats)
    grads = pullback(cotangent.astype(jnp.float32))
    return (result.astype(jnp.bfloat16), grads[0].astype(jnp.bfloat16), grads[1], grads[2], grads[3], grads[4], grads[5], grads[6], grads[7], grads[8], grads[9])
```

```python
import jax
import jax.numpy as jnp
from jax import lax
from jax.sharding import PartitionSpec as P

H = 32
KVH = 8
HD = 64
CLEN = 512

EPSILON = 1e-05
ROPE_BASE = 10000000.0
ATTN_SCALE = 0.015625
RESIDUAL = 0.22
NEGATIVE = -1e30
BF = jnp.bfloat16
F32 = jnp.float32


def matmul(left, right):
    return jnp.dot(left, right, preferred_element_type=F32)


def inner_rows(left, right):
    return lax.dot_general(left, right, (((0,), (0,)), ((), ())), preferred_element_type=F32)


def inner_cols(left, right):
    return lax.dot_general(left, right, (((1,), (1,)), ((), ())), preferred_element_type=F32)


def swap_core(value):
    return lax.ppermute(value, "dp", [(i, i ^ 1) for i in range(4)])


def swap_x(value):
    return lax.ppermute(value, "dp", [(i, i ^ 2) for i in range(4)])


def swap_ctx(value):
    return lax.ppermute(value, "ctx", [(0, 1), (1, 0)])


def gather_plain(shard):
    far = swap_x(shard)
    return [shard, swap_core(shard), far, swap_core(far)]


def gather_split(shard):
    if lax.axis_size("ctx") != 2:
        return gather_plain(shard)
    half = shard.shape[0] // 2
    mine = lax.axis_index("ctx")
    got = swap_x(lax.dynamic_slice_in_dim(shard, mine * half, half))
    other = swap_ctx(got)
    first = mine == 0
    far = jnp.concatenate([jnp.where(first, got, other), jnp.where(first, other, got)], axis=0)
    return [shard, swap_core(shard), far, swap_core(far)]


def reduce_blocks(blocks):
    near = swap_core(blocks[1].astype(BF))
    far = swap_core(blocks[3].astype(BF))
    sent = swap_x((blocks[2] + far.astype(F32)).astype(BF))
    total = blocks[0] + near.astype(F32) + sent.astype(F32)
    if lax.axis_size("ctx") == 2:
        low = total.astype(BF)
        return low.astype(F32) + swap_ctx(low).astype(F32)
    return lax.psum(total.astype(BF), "ctx").astype(F32)


def relative(value, axis):
    size = value.shape[axis] // 4
    mine = lax.axis_index("dp")
    return jnp.concatenate(
        [lax.dynamic_slice_in_dim(value, (mine ^ r) * size, size, axis) for r in range(4)], axis
    )


def split4(value, axis):
    size = value.shape[axis] // 4
    return [lax.slice_in_dim(value, r * size, (r + 1) * size, axis=axis) for r in range(4)]


def rotation(places):
    half_size = HD // 2
    freq = ROPE_BASE ** (-(jnp.arange(half_size, dtype=F32) * 2.0) / HD)
    angle = places.astype(F32)[:, None] * freq[None, :]
    return jnp.cos(angle), jnp.sin(angle)


def rotate(values, cosine, sine):
    head_count = values.shape[1] // HD
    shaped = values.reshape(values.shape[0], head_count, 2, HD // 2)
    first = shaped[:, :, 0]
    second = shaped[:, :, 1]
    cosine = cosine[:, None]
    sine = sine[:, None]
    out_first = first * cosine - second * sine
    out_second = second * cosine + first * sine
    return jnp.stack([out_first, out_second], axis=2).reshape(values.shape)


def token_places(row_ids, order_row, seen_row, prompt_len, block_rows, cont_len):
    block_total = order_row.shape[0]
    block_pick = (row_ids // block_rows)[:, None] == jnp.arange(block_total, dtype=jnp.int32)[
        None, :
    ]
    chosen = jnp.sum(jnp.where(block_pick, order_row[None, :], 0), axis=1)
    global_ids = chosen * block_rows + row_ids % block_rows
    in_prompt = global_ids < prompt_len
    segment = jnp.where(in_prompt, 0, 1 + (global_ids - prompt_len) // cont_len)
    cont_count = seen_row.shape[0]
    which_cont = (segment - 1)[:, None] == jnp.arange(cont_count, dtype=jnp.int32)[None, :]
    limit = jnp.sum(jnp.where(which_cont, seen_row[None, :], 0), axis=1)
    places = jnp.where(in_prompt, global_ids, limit + (global_ids - prompt_len) % cont_len)
    return (segment, places, limit)


def visible(query_seg, query_pos, query_lim, key_seg, key_pos):
    same_seq = (query_seg[:, None] == key_seg[None, :]) & (key_pos[None, :] <= query_pos[:, None])
    shared = (key_seg[None, :] == 0) & (key_pos[None, :] < query_lim[:, None])
    return same_seq | shared


def head_scores(query_heads, key_block, mask):
    key_heads = key_block.reshape(key_block.shape[0], -1, HD)
    scores = (
        jnp.einsum("qgrd,tgd->grqt", query_heads, key_heads, preferred_element_type=jnp.float32)
        * ATTN_SCALE
    )
    return jnp.where(mask[None, None], scores, NEGATIVE)


def probabilities(query_heads, key_block, mask, log_total):
    scores = head_scores(query_heads, key_block, mask)
    return jnp.where(mask[None, None], jnp.exp(scores - log_total[..., None]), 0.0)


def attend_forward(query_heads, key_blocks, value_blocks, seg_blocks, pos_blocks, query_info):
    local_rows, heads_kv, repeat = (
        query_heads.shape[0],
        query_heads.shape[1],
        query_heads.shape[2],
    )
    start_top = jnp.full((heads_kv, repeat, local_rows), NEGATIVE, jnp.float32)
    start_total = jnp.zeros((heads_kv, repeat, local_rows), jnp.float32)

    def stats_step(carry, inputs):
        running_top, running_total = carry
        key_block, seg_block, pos_block = inputs
        mask = visible(query_info[0], query_info[1], query_info[2], seg_block, pos_block)
        scores = head_scores(query_heads, key_block, mask)
        new_top = jnp.maximum(running_top, jnp.max(scores, axis=-1))
        weights = jnp.where(mask[None, None], jnp.exp(scores - new_top[..., None]), 0.0)
        new_total = running_total * jnp.exp(running_top - new_top) + jnp.sum(weights, axis=-1)
        return ((new_top, new_total), None)

    stats, unused = lax.scan(
        stats_step, (start_top, start_total), (key_blocks, seg_blocks, pos_blocks)
    )
    log_total = stats[0] + jnp.log(stats[1])

    def output_step(carry, inputs):
        key_block, value_block, seg_block, pos_block = inputs
        mask = visible(query_info[0], query_info[1], query_info[2], seg_block, pos_block)
        probs = probabilities(query_heads, key_block, mask, log_total).astype(jnp.bfloat16)
        value_heads = value_block.reshape(value_block.shape[0], heads_kv, HD)
        return (
            carry
            + jnp.einsum("grqt,tgd->qgrd", probs, value_heads, preferred_element_type=jnp.float32),
            None,
        )

    start_out = jnp.zeros((local_rows, heads_kv, repeat, HD), jnp.float32)
    mixed, unused = lax.scan(
        output_step, start_out, (key_blocks, value_blocks, seg_blocks, pos_blocks)
    )
    return (mixed, log_total)


def attend_backward(
    query_heads, grad_heads, key_blocks, value_blocks, seg_blocks, pos_blocks, query_info, log_total
):
    local_rows, heads_kv, repeat = (
        query_heads.shape[0],
        query_heads.shape[1],
        query_heads.shape[2],
    )

    def delta_step(carry, inputs):
        key_block, value_block, seg_block, pos_block = inputs
        mask = visible(query_info[0], query_info[1], query_info[2], seg_block, pos_block)
        probs = probabilities(query_heads, key_block, mask, log_total)
        value_heads = value_block.reshape(value_block.shape[0], heads_kv, HD)
        grad_probs = jnp.einsum(
            "qgrd,tgd->grqt", grad_heads, value_heads, preferred_element_type=jnp.float32
        )
        return (carry + jnp.sum(probs * grad_probs, axis=-1), None)

    start_delta = jnp.zeros((heads_kv, repeat, local_rows), jnp.float32)
    delta, unused = lax.scan(
        delta_step, start_delta, (key_blocks, value_blocks, seg_blocks, pos_blocks)
    )

    def grad_step(carry, inputs):
        key_block, value_block, seg_block, pos_block = inputs
        mask = visible(query_info[0], query_info[1], query_info[2], seg_block, pos_block)
        probs = probabilities(query_heads, key_block, mask, log_total)
        key_heads = key_block.reshape(key_block.shape[0], heads_kv, HD)
        value_heads = value_block.reshape(value_block.shape[0], heads_kv, HD)
        grad_probs = jnp.einsum(
            "qgrd,tgd->grqt", grad_heads, value_heads, preferred_element_type=jnp.float32
        )
        scores_grad = (probs * (grad_probs - delta[..., None])).astype(jnp.bfloat16)
        new_carry = carry + jnp.einsum(
            "grqt,tgd->qgrd", scores_grad, key_heads, preferred_element_type=jnp.float32
        )
        key_part = jnp.einsum(
            "grqt,qgrd->tgd", scores_grad, query_heads, preferred_element_type=jnp.float32
        )
        value_part = jnp.einsum(
            "grqt,qgrd->tgd",
            probs.astype(jnp.bfloat16),
            grad_heads,
            preferred_element_type=jnp.float32,
        )
        return (new_carry, (key_part, value_part))

    start_query = jnp.zeros((local_rows, heads_kv, repeat, HD), jnp.float32)
    query_part, key_value = lax.scan(
        grad_step, start_query, (key_blocks, value_blocks, seg_blocks, pos_blocks)
    )
    return (query_part, key_value[0], key_value[1])


def norm_scale(values):
    return lax.rsqrt(jnp.mean(values * values, axis=-1, keepdims=True) + EPSILON)


def norm_back(values, scale, gain, grad):
    weighted = gain * grad
    inner = jnp.mean(weighted * values, axis=-1, keepdims=True)
    return scale * weighted - values * (scale * scale * scale) * inner


def psum_tensor(value):
    return lax.psum(value.astype(BF), "tensor").astype(F32)


def shards(
    tokens,
    cotangent,
    first_gain,
    query_weight,
    key_weight,
    value_weight,
    output_weight,
    second_gain,
    gate_weight,
    up_weight,
    down_weight,
    block_order,
    prefix_seen,
):
    ctx_size = lax.axis_size("ctx")
    local_rows = tokens.shape[0]
    group_rows = local_rows * ctx_size
    offset = lax.axis_index("ctx") * local_rows
    width_q = query_weight.shape[1]
    width_kv = key_weight.shape[1]
    block_d = query_weight.shape[0]

    gains = jnp.pad(jnp.stack([first_gain, second_gain]), ((0, 30), (0, width_q + 2 * width_kv - block_d)))
    qkv_shard = jnp.concatenate(
        [jnp.concatenate([query_weight, key_weight, value_weight], axis=1), gains], axis=0
    )
    qkv_pieces = gather_plain(qkv_shard)
    out_pieces = gather_plain(output_weight)
    qkv_full = jnp.concatenate([p[:block_d] for p in qkv_pieces], axis=0)
    gain_one = jnp.concatenate([p[block_d, :block_d] for p in qkv_pieces]).astype(F32)
    gain_two = jnp.concatenate([p[block_d + 1, :block_d] for p in qkv_pieces]).astype(F32)
    output_full = jnp.concatenate(out_pieces, axis=1)
    gate_full = jnp.concatenate(gather_split(gate_weight), axis=0)
    up_full = jnp.concatenate(gather_split(up_weight), axis=0)
    down_full = jnp.concatenate(gather_split(down_weight), axis=1)

    all_ids = jnp.arange(group_rows, dtype=jnp.int32)
    key_seg, key_pos, key_lim = token_places(
        all_ids, block_order[0], prefix_seen[0], group_rows // 2, local_rows // 2, CLEN
    )
    query_seg = lax.dynamic_slice_in_dim(key_seg, offset, local_rows)
    query_pos = lax.dynamic_slice_in_dim(key_pos, offset, local_rows)
    query_lim = lax.dynamic_slice_in_dim(key_lim, offset, local_rows)
    query_info = (query_seg, query_pos, query_lim)
    key_len = min(512, group_rows)
    block_count = group_rows // key_len
    seg_blocks = key_seg.reshape(block_count, key_len)
    pos_blocks = key_pos.reshape(block_count, key_len)
    cosine, sine = rotation(query_pos)

    inputs = relative(tokens, 1).astype(F32)
    grad_out = relative(cotangent, 1).astype(F32)
    scale_one = norm_scale(inputs)
    normed = (inputs * scale_one * gain_one).astype(BF)
    proj = matmul(normed, qkv_full)
    rotated = rotate(proj[:, : width_q + width_kv], cosine, sine).astype(BF)
    queries = rotated[:, :width_q]
    key_value = jnp.concatenate(
        [rotated[:, width_q:], proj[:, width_q + width_kv :].astype(BF)], axis=1
    )
    key_value_all = lax.all_gather(key_value, "ctx", axis=0, tiled=True)
    heads_kv = width_kv // HD
    repeat = H // KVH
    query_heads = queries.reshape(local_rows, heads_kv, repeat, HD)
    key_blocks = key_value_all[:, :width_kv].reshape(block_count, key_len, width_kv)
    value_blocks = key_value_all[:, width_kv:].reshape(block_count, key_len, width_kv)
    mixed, log_total = attend_forward(
        query_heads, key_blocks, value_blocks, seg_blocks, pos_blocks, query_info
    )
    attended = mixed.reshape(local_rows, -1).astype(BF)
    middle = inputs + RESIDUAL * psum_tensor(matmul(attended, output_full))

    scale_two = norm_scale(middle)
    normed_two = (middle * scale_two * gain_two).astype(BF)
    gate = matmul(normed_two, gate_full)
    upper = matmul(normed_two, up_full)
    sigma = jax.nn.sigmoid(gate)
    active = gate * sigma
    hidden = (active * upper).astype(BF)
    grad_mlp = (RESIDUAL * grad_out).astype(BF)
    grad_hidden = inner_cols(grad_mlp, down_full)
    grad_gate = (grad_hidden * upper * sigma * (1.0 + gate * (1.0 - sigma))).astype(BF)
    grad_up = (grad_hidden * active).astype(BF)
    grad_two = psum_tensor(inner_cols(grad_gate, gate_full) + inner_cols(grad_up, up_full))
    mlp_sum = psum_tensor(matmul(hidden, down_full))
    layer_out = relative((middle + RESIDUAL * mlp_sum).astype(BF), 1)

    down_grad = reduce_blocks([inner_rows(hidden, g) for g in split4(grad_mlp, 1)])
    gate_grad = reduce_blocks([inner_rows(h, grad_gate) for h in split4(normed_two, 1)])
    up_grad = reduce_blocks([inner_rows(h, grad_up) for h in split4(normed_two, 1)])

    gain_two_part = jnp.sum(grad_two * middle * scale_two, axis=0)
    grad_middle = grad_out + norm_back(middle, scale_two, gain_two, grad_two)
    grad_branch = (RESIDUAL * grad_middle).astype(BF)
    output_grad = reduce_blocks([inner_rows(attended, g) for g in split4(grad_branch, 1)])
    grad_attended = inner_cols(grad_branch, output_full).astype(BF)
    grad_heads = grad_attended.reshape(local_rows, heads_kv, repeat, HD)
    query_acc, key_parts, value_parts = attend_backward(
        query_heads,
        grad_heads,
        key_blocks,
        value_blocks,
        seg_blocks,
        pos_blocks,
        query_info,
        log_total,
    )
    key_value_parts = jnp.concatenate(
        [key_parts.reshape(group_rows, width_kv), value_parts.reshape(group_rows, width_kv)], axis=1
    )
    if ctx_size == 2:
        kept = lax.dynamic_slice_in_dim(key_value_parts, offset, local_rows)
        sent = lax.dynamic_slice_in_dim(key_value_parts, local_rows - offset, local_rows)
        key_value_sums = kept + swap_ctx(sent.astype(BF)).astype(F32)
    else:
        key_value_sums = lax.psum_scatter(
            key_value_parts.astype(BF), "ctx", scatter_dimension=0, tiled=True
        ).astype(F32)
    query_key = jnp.concatenate(
        [query_acc.reshape(local_rows, -1), key_value_sums[:, :width_kv]], axis=1
    )
    query_key_low = rotate(query_key * ATTN_SCALE, cosine, -sine).astype(BF)
    qkv_low = jnp.concatenate([query_key_low, key_value_sums[:, width_kv:].astype(BF)], axis=1)
    grad_one = psum_tensor(inner_cols(qkv_low, qkv_full))
    qkv_grad = reduce_blocks([inner_rows(h, qkv_low) for h in split4(normed, 1)])
    gain_one_part = jnp.sum(grad_one * inputs * scale_one, axis=0)
    tokens_grad = relative(
        (grad_middle + norm_back(inputs, scale_one, gain_one, grad_one)).astype(BF), 1
    )
    gain_blocks = split4(jnp.stack([gain_one_part, gain_two_part]), 1)
    gain_grad = reduce_blocks(gain_blocks)
    return (
        layer_out,
        tokens_grad,
        gain_grad[0],
        qkv_grad[:, :width_q],
        qkv_grad[:, width_q : width_q + width_kv],
        qkv_grad[:, width_q + width_kv :],
        output_grad,
        gain_grad[1],
        gate_grad,
        up_grad,
        down_grad,
    )


def solution(mesh):
    return jax.shard_map(
        shards,
        mesh=mesh,
        in_specs=(
            P(("dp", "ctx"), None),
            P(("dp", "ctx"), None),
            P("dp"),
            P("dp", "tensor"),
            P("dp", "tensor"),
            P("dp", "tensor"),
            P("tensor", "dp"),
            P("dp"),
            P("dp", "tensor"),
            P("dp", "tensor"),
            P("tensor", "dp"),
            P("dp", None),
            P("dp", None),
        ),
        out_specs=(
            P(("dp", "ctx"), None),
            P(("dp", "ctx"), None),
            P("dp"),
            P("dp", "tensor"),
            P("dp", "tensor"),
            P("dp", "tensor"),
            P("tensor", "dp"),
            P("dp"),
            P("dp", "tensor"),
            P("dp", "tensor"),
            P("tensor", "dp"),
        ),
        check_vma=False,
    )
```

```python
import functools

import jax
import jax.numpy as jnp
from jax import lax
from jax.experimental import pallas as pl
from jax.experimental.pallas import tpu as pltpu
from jax.sharding import PartitionSpec as P

HD = 64
CLEN = 512

EPSILON = 1e-05
ROPE_BASE = 10000000.0
ATTN_SCALE = 0.015625
RESIDUAL = 0.22
NEGATIVE = -1e30
SEGMENT_STEP = 1 << 16
BF = jnp.bfloat16
F32 = jnp.float32
LIGHT = pl.CostEstimate(flops=1, bytes_accessed=1, transcendentals=0)


def dot_nt(a, b):
    return lax.dot_general(a, b, (((1,), (1,)), ((), ())), preferred_element_type=F32)

def dot_nn(a, b):
    return lax.dot_general(a, b, (((1,), (0,)), ((), ())), preferred_element_type=F32)

def fill_bias(bias, key_code, query_codes):
    code = key_code[...]
    below = code < query_codes[0:1, :]
    own = (code >= query_codes[1:2, :]) & (code <= query_codes[2:3, :])
    bias[...] = jnp.where(below | own, 0.0, NEGATIVE)

def fill_padded(padded, source, lane0):
    block = source[:, lane0 : lane0 + 2 * HD]
    lane = lax.broadcasted_iota(jnp.int32, block.shape, 1)
    low = jnp.where(lane < HD, block, jnp.zeros_like(block))
    high = jnp.where(lane < HD, jnp.zeros_like(block), block)
    padded[0, 0] = low
    padded[0, 1] = pltpu.roll(low.astype(F32), HD, 1).astype(BF)
    padded[1, 0] = pltpu.roll(high.astype(F32), HD, 1).astype(BF)
    padded[1, 1] = high

def forward_kernel(chunk, q_ref, kv_ref, vt_ref, code_ref, codes_ref, o0, o1, o2, o3, out_ref, lse_ref, branch_ref, bias, keys):
    total = kv_ref.shape[0]
    rows = q_ref.shape[0]
    fill_bias(bias, code_ref, codes_ref)
    fill_padded(keys, kv_ref, 0)

    def pair_step(pair, unused):
        group = pair // 2
        lanes = pl.ds(pl.multiple_of(pair * 128, 128), 128)
        q_pair = q_ref[:, lanes]
        mixed = []
        for side in range(2):
            def chunk_step(part, carry):
                top, norm, acc = carry
                at = pl.ds(pl.multiple_of(part * chunk, chunk), chunk)
                scores = dot_nt(keys[group, side, at, :], q_pair) + bias[at, :]
                new_top = jnp.maximum(top, jnp.max(scores, axis=0, keepdims=True))
                weights = jnp.exp(scores - new_top)
                shrink = jnp.exp(top - new_top)
                norm = norm * shrink + jnp.sum(weights, axis=0, keepdims=True)
                values = vt_ref[pl.ds(pl.multiple_of(group * HD, HD), HD), at]
                acc = acc * shrink + dot_nn(values, weights.astype(BF))
                return new_top, norm, acc

            carry = (jnp.full((1, rows), NEGATIVE, F32), jnp.zeros((1, rows), F32), jnp.zeros((HD, rows), F32))
            if total == chunk:
                carry = chunk_step(0, carry)
            else:
                carry = lax.fori_loop(0, total // chunk, chunk_step, carry)
            top, norm, acc = carry
            mixed.append(acc / norm)
            lse_ref[pl.ds(pair * 2 + side, 1), :] = top + jnp.log(norm)
        out_ref[:, lanes] = jnp.concatenate(mixed, axis=0).T.astype(BF)
        return unused

    lax.fori_loop(0, q_ref.shape[1] // 128, pair_step, 0)
    block = o0.shape[1]
    for r, piece in enumerate((o0, o1, o2, o3)):
        branch_ref[:, r * block : (r + 1) * block] = dot_nn(out_ref[...], piece[...]).astype(BF)


def attend_forward(queries, key_value, values_t, key_code, query_codes, out_pieces):
    rows, width = queries.shape
    total = key_value.shape[0]
    chunk = min(total, 1024)
    return pl.pallas_call(
        functools.partial(forward_kernel, chunk),
        out_shape=(
            jax.ShapeDtypeStruct((rows, width), BF),
            jax.ShapeDtypeStruct((width // HD, rows), F32),
            jax.ShapeDtypeStruct((rows, 4 * out_pieces[0].shape[1]), BF),
        ),
        scratch_shapes=[pltpu.VMEM((total, rows), F32), pltpu.VMEM((2, 2, total, 128), BF)],
        compiler_params=pltpu.CompilerParams(vmem_limit_bytes=(32 if total <= 1024 else 58) << 20),
        cost_estimate=LIGHT,
        name="attend_forward",
    )(queries, key_value, values_t, key_code, query_codes, *out_pieces)

def backward_kernel(chunk, q_ref, kv_ref, kt_ref, code_ref, codes_ref, att_ref, branch_ref, lse_ref, rot_ref,
                    o0, o1, o2, o3, dq_ref, dkv_ref, grad_ref, bias, keys, values, delta, dk_acc, dv_acc):
    total = kv_ref.shape[0]
    rows = q_ref.shape[0]
    width = q_ref.shape[1]
    heads = width // HD
    fill_bias(bias, code_ref, codes_ref)
    fill_padded(keys, kv_ref, 0)
    fill_padded(values, kv_ref, 128)
    block = o0.shape[1]
    grad = jnp.zeros((rows, width), F32)
    for r, piece in enumerate((o0, o1, o2, o3)):
        grad += dot_nt(branch_ref[:, r * block : (r + 1) * block], piece[...])
    grad_ref[...] = grad.astype(BF)
    owner = lax.broadcasted_iota(jnp.int32, (heads, width), 1) // HD
    member = jnp.where(owner == lax.broadcasted_iota(jnp.int32, (heads, width), 0), 1.0, 0.0)
    product = att_ref[...].astype(F32) * grad_ref[...].astype(F32)
    delta[...] = lax.dot_general(member, product, (((1,), (1,)), ((), ())), precision=lax.Precision.HIGHEST, preferred_element_type=F32)
    dk_acc[...] = jnp.zeros_like(dk_acc)
    dv_acc[...] = jnp.zeros_like(dv_acc)
    half = HD // 2

    def pair_step(pair, unused):
        group = pair // 2
        lanes = pl.ds(pl.multiple_of(pair * 128, 128), 128)
        q_pair = q_ref[:, lanes]
        g_pair = grad_ref[:, lanes]
        turned = []
        for side in range(2):
            head = pl.ds(pair * 2 + side, 1)
            lse = lse_ref[head, :]
            dlt = delta[head, :]
            def chunk_step(part, acc):
                at = pl.ds(pl.multiple_of(part * chunk, chunk), chunk)
                scores = dot_nt(keys[group, side, at, :], q_pair) + bias[at, :]
                probs = jnp.exp(scores - lse)
                dprobs = dot_nt(values[group, side, at, :], g_pair)
                dscores = (probs * (dprobs - dlt)).astype(BF)
                dv_acc[group, side, at, :] += dot_nn(probs.astype(BF), g_pair)
                dk_acc[group, side, at, :] += dot_nn(dscores, q_pair)
                kt = kt_ref[pl.ds(pl.multiple_of(group * HD, HD), HD), at]
                return acc + dot_nn(kt, dscores)
            acc = jnp.zeros((HD, rows), F32)
            if total == chunk:
                acc = chunk_step(0, acc)
            else:
                acc = lax.fori_loop(0, total // chunk, chunk_step, acc)
            acc = acc * (1.0 / HD)
            first, second = acc[:half], acc[half:]
            cosine, sine = rot_ref[:half, :], rot_ref[half:, :]
            turned.append(first * cosine + second * sine)
            turned.append(second * cosine - first * sine)
        dq_ref[:, lanes] = jnp.concatenate(turned, axis=0).T.astype(BF)
        return unused

    lax.fori_loop(0, width // 128, pair_step, 0)
    lane = lax.broadcasted_iota(jnp.int32, (total, 128), 1)
    for which, acc in ((0, dk_acc), (1, dv_acc)):
        zero = acc[0, 0] + pltpu.roll(acc[0, 1], HD, 1)
        one = pltpu.roll(acc[1, 0], HD, 1) + acc[1, 1]
        dkv_ref[:, which * 128 : (which + 1) * 128] = jnp.where(lane < HD, zero, one)

def attend_backward(queries, key_value, keys_t, key_code, query_codes, attended, grad_branch, lse, turn, out_pieces):
    rows, width = queries.shape
    total = key_value.shape[0]
    chunk = min(total, 1024)
    return pl.pallas_call(
        functools.partial(backward_kernel, chunk),
        out_shape=(jax.ShapeDtypeStruct((rows, width), BF), jax.ShapeDtypeStruct((total, 256), F32)),
        scratch_shapes=[
            pltpu.VMEM((rows, width), BF),
            pltpu.VMEM((total, rows), F32),
            pltpu.VMEM((2, 2, total, 128), BF),
            pltpu.VMEM((2, 2, total, 128), BF),
            pltpu.VMEM((width // HD, rows), F32),
            pltpu.VMEM((2, 2, total, 128), F32),
            pltpu.VMEM((2, 2, total, 128), F32),
        ],
        compiler_params=pltpu.CompilerParams(vmem_limit_bytes=(32 if total <= 1024 else 58) << 20),
        cost_estimate=LIGHT,
        name="attend_backward",
    )(queries, key_value, keys_t, key_code, query_codes, attended, grad_branch, lse, turn, *out_pieces)


def rows_at(index, size):
    return pl.ds(pl.multiple_of(index * size, size), size)


def half_turn(block):
    lane = lax.broadcasted_iota(jnp.int32, block.shape, 1)
    return jnp.where(lane % HD < HD // 2, pltpu.roll(block, 128 - HD // 2, 1), pltpu.roll(block, HD // 2, 1))


def project_kernel(width_q, x_ref, cos_ref, sin_ref, p0, p1, p2, p3, normed_ref, q_ref, kv_ref):
    block = x_ref.shape[1] // 4
    width = p0.shape[1]
    total = jnp.zeros((x_ref.shape[0], width), F32)
    for r, piece in enumerate((p0, p1, p2, p3)):
        lanes = slice(r * block, (r + 1) * block)
        gain = piece[block : block + 1, :block].astype(F32)
        low = (x_ref[:, lanes] * gain).astype(BF)
        normed_ref[:, lanes] = low
        total += dot_nn(low, piece[:block, :])
    cosine, sine = cos_ref[...], sin_ref[...]
    turned_width = width_q + (width - width_q) // 2
    for at in range(0, width, 128):
        part = total[:, at : at + 128]
        if at < turned_width:
            part = part * cosine + half_turn(part) * sine
        low = part.astype(BF)
        if at < width_q:
            q_ref[:, at : at + 128] = low * jnp.asarray(ATTN_SCALE, BF)
        else:
            kv_ref[:, at - width_q : at - width_q + 128] = low


def project(scaled, cos_table, sin_table, pieces, width_q):
    rows, model = scaled.shape
    width = pieces[0].shape[1]
    return pl.pallas_call(
        functools.partial(project_kernel, width_q),
        out_shape=(
            jax.ShapeDtypeStruct((rows, model), BF),
            jax.ShapeDtypeStruct((rows, width_q), BF),
            jax.ShapeDtypeStruct((rows, width - width_q), BF),
        ),
        compiler_params=pltpu.CompilerParams(vmem_limit_bytes=24 << 20),
        cost_estimate=LIGHT,
        name="project",
    )(scaled, cos_table, sin_table, *pieces)


def mlp_kernel(h_ref, g_ref, *refs):
    gates, ups, downs = refs[:4], refs[4:8], refs[8:12]
    hidden_ref, dgate_ref, dup_ref, dh_ref, acc = refs[12:]
    step = pl.program_id(0)
    block = h_ref.shape[1] // 4
    gate = up = dhid = None
    for r in range(4):
        lanes = slice(r * block, (r + 1) * block)
        h = h_ref[:, lanes]
        terms = (dot_nn(h, gates[r][...]), dot_nn(h, ups[r][...]), dot_nt(g_ref[:, lanes], downs[r][...]))
        gate, up, dhid = terms if r == 0 else (gate + terms[0], up + terms[1], dhid + terms[2])
    sigma = jax.nn.sigmoid(gate)
    active = gate * sigma
    hidden_ref[...] = (active * up).astype(BF)
    dgate = (dhid * up * sigma * (1.0 + gate * (1.0 - sigma))).astype(BF)
    dup = (dhid * active).astype(BF)
    dgate_ref[...] = dgate
    dup_ref[...] = dup
    for r in range(4):
        lanes = slice(r * block, (r + 1) * block)
        term = dot_nt(dgate, gates[r][...]) + dot_nt(dup, ups[r][...])

        @pl.when(step == 0)
        def _():
            acc[:, lanes] = term

        @pl.when(step != 0)
        def _():
            acc[:, lanes] += term

    @pl.when(step == pl.num_programs(0) - 1)
    def _():
        dh_ref[...] = acc[...].astype(BF)


def mlp(normed, grad, gates, ups, downs):
    rows, model = normed.shape
    block, hidden = gates[0].shape
    tile = 512
    whole = pl.BlockSpec((rows, model), lambda j: (0, 0))
    wide = pl.BlockSpec((block, tile), lambda j: (0, j))
    tall = pl.BlockSpec((tile, block), lambda j: (j, 0))
    out = pl.BlockSpec((rows, tile), lambda j: (0, j))
    return pl.pallas_call(
        mlp_kernel,
        grid=(hidden // tile,),
        in_specs=[whole] * 2 + [wide] * 8 + [tall] * 4,
        out_specs=[out] * 3 + [whole],
        out_shape=[jax.ShapeDtypeStruct((rows, hidden), BF)] * 3
        + [jax.ShapeDtypeStruct((rows, model), BF)],
        scratch_shapes=[pltpu.VMEM((rows, model), F32)],
        compiler_params=pltpu.CompilerParams(vmem_limit_bytes=40 << 20),
        cost_estimate=LIGHT,
        name="mlp",
    )(normed, grad, *gates, *ups, *downs)


def entry_kernel(dq_ref, own_ref, got_ref, cos_ref, sin_ref, p0, p1, p2, p3, low_ref, dh_ref):
    block = dh_ref.shape[1] // 4
    width_q = dq_ref.shape[1]
    low_ref[:, :width_q] = dq_ref[...]
    sums = own_ref[...] + got_ref[...].astype(F32)
    dk = sums[:, :128]
    low_ref[:, width_q : width_q + 128] = (dk * cos_ref[...] - half_turn(dk) * sin_ref[...]).astype(BF)
    low_ref[:, width_q + 128 :] = sums[:, 128:].astype(BF)
    low = low_ref[...]
    for r, piece in enumerate((p0, p1, p2, p3)):
        dh_ref[:, r * block : (r + 1) * block] = dot_nt(low, piece[:block, :]).astype(BF)


def entry_grad(dq_low, own, got, cos_table, sin_table, pieces):
    rows, width_q = dq_low.shape
    block = pieces[0].shape[0] - 32
    width = pieces[0].shape[1]
    return pl.pallas_call(
        entry_kernel,
        out_shape=(
            jax.ShapeDtypeStruct((rows, width), BF),
            jax.ShapeDtypeStruct((rows, 4 * block), BF),
        ),
        compiler_params=pltpu.CompilerParams(vmem_limit_bytes=24 << 20),
        cost_estimate=LIGHT,
        name="entry_grad",
    )(dq_low, own, got, cos_table, sin_table, *pieces)


def outer_kernel(n_adds, a_ref, b_ref, *refs):
    total = lax.dot_general(
        a_ref[...], b_ref[...], (((0,), (0,)), ((), ())), preferred_element_type=F32
    )
    for add in refs[:n_adds]:
        total += add[...].astype(F32)
    refs[n_adds][...] = total.astype(BF)


def outer(left, right, left_blocks, right_blocks, adds, name):
    rows = left.shape[0]
    size_m, size_n = left.shape[1] // 4, right.shape[1] // 4
    first_m, count_m = left_blocks
    first_n, count_n = right_blocks
    cut_rows = count_m < 4
    wide = size_n * count_n
    in_specs = [
        pl.BlockSpec((rows, size_m), lambda i: (0, first_m + i)),
        pl.BlockSpec((rows, wide), lambda i: (0, first_n // count_n)),
    ]
    for array, first in adds:
        if cut_rows:
            in_specs.append(pl.BlockSpec((size_m, wide), lambda i, first=first: (first + i, 0)))
        else:
            in_specs.append(pl.BlockSpec((size_m, wide), lambda i, first=first: (i, first)))
    return pl.pallas_call(
        functools.partial(outer_kernel, len(adds)),
        grid=(count_m,),
        in_specs=in_specs,
        out_specs=pl.BlockSpec((size_m, wide), lambda i: (i, 0)),
        out_shape=jax.ShapeDtypeStruct((size_m * count_m, wide), BF),
        compiler_params=pltpu.CompilerParams(vmem_limit_bytes=32 << 20),
        cost_estimate=LIGHT,
        name=name,
    )(left, right, *[array for array, unused in adds])


def lift_kernel(hidden_ref, d0, d1, d2, d3, out_ref, acc):
    step = pl.program_id(0)
    block = d0.shape[1]
    for r, piece in enumerate((d0, d1, d2, d3)):
        lanes = slice(r * block, (r + 1) * block)
        term = dot_nn(hidden_ref[...], piece[...])

        @pl.when(step == 0)
        def _():
            acc[:, lanes] = term

        @pl.when(step != 0)
        def _():
            acc[:, lanes] += term

    @pl.when(step == pl.num_programs(0) - 1)
    def _():
        out_ref[...] = acc[...].astype(BF)


def lift(hidden, downs):
    rows, width = hidden.shape
    block = downs[0].shape[1]
    tile = 512
    return pl.pallas_call(
        lift_kernel,
        grid=(width // tile,),
        in_specs=[pl.BlockSpec((rows, tile), lambda j: (0, j))]
        + [pl.BlockSpec((tile, block), lambda j: (j, 0))] * 4,
        out_specs=pl.BlockSpec((rows, 4 * block), lambda j: (0, 0)),
        out_shape=jax.ShapeDtypeStruct((rows, 4 * block), BF),
        scratch_shapes=[pltpu.VMEM((rows, 4 * block), F32)],
        compiler_params=pltpu.CompilerParams(vmem_limit_bytes=32 << 20),
        cost_estimate=LIGHT,
        name="lift",
    )(hidden, *downs)


def entry_outer_kernel(n_adds, attended_ref, branch_ref, normed_ref, low_ref, *refs):
    out_ref = refs[n_adds]
    width = attended_ref.shape[1]
    head = lax.dot_general(
        attended_ref[...], branch_ref[...], (((0,), (0,)), ((), ())), preferred_element_type=F32
    )
    tail = lax.dot_general(
        normed_ref[...], low_ref[...], (((0,), (0,)), ((), ())), preferred_element_type=F32
    )
    for add in refs[:n_adds]:
        head += add[:, : head.shape[1]].astype(F32)
        tail += add[:, head.shape[1] :].astype(F32)
    out_ref[:, : head.shape[1]] = head.astype(BF)
    out_ref[:, head.shape[1] :] = tail.astype(BF)


def entry_outer(attended, branch, normed, low, first, count, adds):
    rows, heads = attended.shape
    block = branch.shape[1] // 4
    width = block + low.shape[1]
    column = pl.BlockSpec((rows, block), lambda i: (0, first + i))
    in_specs = [
        pl.BlockSpec((rows, heads), lambda i: (0, 0)),
        column,
        column,
        pl.BlockSpec(low.shape, lambda i: (0, 0)),
    ]
    for array, at in adds:
        in_specs.append(pl.BlockSpec((block, width), lambda i, at=at: (at + i, 0)))
    return pl.pallas_call(
        functools.partial(entry_outer_kernel, len(adds)),
        grid=(count,),
        in_specs=in_specs,
        out_specs=pl.BlockSpec((block, width), lambda i: (i, 0)),
        out_shape=jax.ShapeDtypeStruct((block * count, width), BF),
        compiler_params=pltpu.CompilerParams(vmem_limit_bytes=24 << 20),
        cost_estimate=LIGHT,
        name="entry_outer",
    )(attended, branch, normed, low, *[array for array, unused in adds])


def after(value, *others):
    if not others:
        return value
    return lax.optimization_barrier((value, *others))[0]


def sealed(step, *values):
    skipped = lambda *v: jax.tree.map(lambda a: jnp.zeros(a.shape, a.dtype), jax.eval_shape(step, *v))
    return lax.cond(lax.optimization_barrier(jnp.asarray(True)), step, skipped, *values)


def swap_core(value):
    return lax.ppermute(value, "dp", [(i, i ^ 1) for i in range(4)])


def swap_x(value):
    return lax.ppermute(value, "dp", [(i, i ^ 2) for i in range(4)])


def swap_both(value):
    return lax.ppermute(value, "dp", [(i, i ^ 3) for i in range(4)])


def swap_ctx(value):
    return lax.ppermute(value, "ctx", [(0, 1), (1, 0)])


def two_ctx():
    return lax.axis_size("ctx") == 2


def sum_ctx(total):
    low = total.astype(BF)
    if two_ctx():
        return low.astype(F32) + swap_ctx(low).astype(F32)
    return lax.psum(low, "ctx").astype(F32)


def far_halves(one, two, wait):
    if not two_ctx():
        return swap_x(after(jnp.concatenate([one, two]), wait))
    half = one.shape[0] // 2
    at = lax.axis_index("ctx") * half
    mine = [lax.dynamic_slice_in_dim(v, at, half) for v in (one, two)]
    return swap_x(after(jnp.concatenate(mine), wait))


def far_wholes(got):
    if not two_ctx():
        return jnp.split(got, 2)
    other = swap_ctx(got)
    half = got.shape[0] // 2
    first = lax.axis_index("ctx") == 0
    return [
        jnp.concatenate([jnp.where(first, a, b), jnp.where(first, b, a)])
        for a, b in ((got[:half], other[:half]), (got[half:], other[half:]))
    ]


def psum_tensor(value):
    return lax.psum(value, "tensor")


def swap_bits(index):
    return ((index & 1) << 1) | (index >> 1)


def take_blocks(value, indices):
    size = value.shape[1] // 4
    return jnp.concatenate(
        [lax.dynamic_slice_in_dim(value, i * size, size, 1) for i in indices], axis=1
    )


def relative(value):
    mine = lax.axis_index("dp")
    return take_blocks(value, [mine ^ k for k in (0, 2, 1, 3)])


def absolute(value):
    mine = lax.axis_index("dp")
    return take_blocks(value, [swap_bits(mine ^ k) for k in range(4)])


def split4(value, axis):
    size = value.shape[axis] // 4
    return [lax.slice_in_dim(value, r * size, (r + 1) * size, axis=axis) for r in range(4)]


def token_places(row_ids, order_row, seen_row, prompt_len, block_rows, cont_len):
    block_total = order_row.shape[0]
    block_pick = (row_ids // block_rows)[:, None] == jnp.arange(block_total, dtype=jnp.int32)[
        None, :
    ]
    chosen = jnp.sum(jnp.where(block_pick, order_row[None, :], 0), axis=1)
    global_ids = chosen * block_rows + row_ids % block_rows
    in_prompt = global_ids < prompt_len
    segment = jnp.where(in_prompt, 0, 1 + (global_ids - prompt_len) // cont_len)
    cont_count = seen_row.shape[0]
    which_cont = (segment - 1)[:, None] == jnp.arange(cont_count, dtype=jnp.int32)[None, :]
    limit = jnp.sum(jnp.where(which_cont, seen_row[None, :], 0), axis=1)
    places = jnp.where(in_prompt, global_ids, limit + (global_ids - prompt_len) % cont_len)
    return (segment, places, limit)


def norm_scale(values):
    return lax.rsqrt(jnp.mean(values * values, axis=-1, keepdims=True) + EPSILON)


def norm_back(values, scale, gain, grad):
    weighted = gain * grad
    inner = jnp.mean(weighted * values, axis=-1, keepdims=True)
    return scale * weighted - values * (scale * scale * scale) * inner


def combine(low, peer):
    if two_ctx():
        return low.astype(F32) + peer.astype(F32)
    return peer.astype(F32)


class BlockSum:
    def __init__(self, term):
        self.term = term

    def begin(self):
        other = swap_core(self.term(2, 2, ()))
        return other, self.term(1, 1, ((other, 1),))

    def cross(self, begun, *wait):
        self.other, self.sent = begun
        self.got = swap_x(after(self.sent, *wait))
        return self

    def joined(self, other, got):
        self.other, self.got = other, got
        return self

    def fold(self, *wait):
        self.low = self.term(0, 1, ((self.other, 0), (after(self.got, *wait), 0)))
        return self

    def swap(self, *wait):
        low = after(self.low, *wait)
        self.peer = swap_ctx(low) if two_ctx() else lax.psum(low, "ctx")
        return self

    def result(self):
        return combine(self.low, self.peer)


def outer_sum(left, right, cut_left, name):
    def term(k, n, adds):
        cut, whole = (k, n), (0, 4)
        if cut_left:
            return outer(left, right, cut, whole, adds, name)
        return outer(left, right, whole, cut, adds, name)

    return BlockSum(term)


def shards(
    tokens,
    cotangent,
    first_gain,
    query_weight,
    key_weight,
    value_weight,
    output_weight,
    second_gain,
    gate_weight,
    up_weight,
    down_weight,
    block_order,
    prefix_seen,
):
    ctx_size = lax.axis_size("ctx")
    local_rows = tokens.shape[0]
    group_rows = local_rows * ctx_size
    offset = lax.axis_index("ctx") * local_rows
    width_q = query_weight.shape[1]
    width_kv = key_weight.shape[1]
    block_d = query_weight.shape[0]

    gains = jnp.pad(
        jnp.stack([first_gain, second_gain]), ((0, 30), (0, width_q + 2 * width_kv - block_d))
    )
    qkv_shard = jnp.concatenate(
        [jnp.concatenate([query_weight, key_weight, value_weight], axis=1), gains], axis=0
    )
    qkv_far = swap_x(qkv_shard)
    qkv_near = swap_core(qkv_shard)
    out_far = swap_x(after(output_weight, qkv_near))
    out_near = swap_core(after(output_weight, qkv_near))
    wide_got = far_halves(gate_weight, up_weight, out_near)

    tokens, cotangent, block_order = (
        after(v, qkv_near) for v in (tokens, cotangent, block_order)
    )
    all_ids = jnp.arange(group_rows, dtype=jnp.int32)
    if two_ctx():
        all_ids = jnp.where(all_ids < local_rows, all_ids + offset, all_ids - offset)
    key_seg, key_pos, key_lim = token_places(
        all_ids, block_order[0], prefix_seen[0], group_rows // 2, local_rows // 2, CLEN
    )
    if two_ctx():
        query_seg, query_pos, query_lim = key_seg[:local_rows], key_pos[:local_rows], key_lim[:local_rows]
    else:
        query_seg = lax.dynamic_slice_in_dim(key_seg, offset, local_rows)
        query_pos = lax.dynamic_slice_in_dim(key_pos, offset, local_rows)
        query_lim = lax.dynamic_slice_in_dim(key_lim, offset, local_rows)
    key_code = (key_seg * SEGMENT_STEP + key_pos)[:, None]
    in_prompt = query_seg == 0
    below = jnp.where(in_prompt, query_pos + 1, query_lim)
    low_code = jnp.where(in_prompt, 1, query_seg * SEGMENT_STEP)
    high_code = jnp.where(in_prompt, 0, query_seg * SEGMENT_STEP + query_pos)
    query_codes = jnp.stack([below, low_code, high_code] + [below] * 5)
    half_size = HD // 2
    freq = ROPE_BASE ** (-(jnp.arange(half_size, dtype=F32) * 2.0) / HD)
    angle_t = freq[:, None] * query_pos.astype(F32)[None, :]
    turn = jnp.concatenate([jnp.cos(angle_t), jnp.sin(angle_t)], axis=0)
    cosine, sine = turn[:half_size].T, turn[half_size:].T
    cos_table = jnp.concatenate([cosine] * 4, axis=1)
    sin_table = jnp.concatenate([-sine, sine] * 2, axis=1)

    inputs = relative(tokens).astype(F32)
    grad_out = relative(cotangent).astype(F32)
    grad_mlp = (RESIDUAL * grad_out).astype(BF)
    scale_one = norm_scale(inputs)
    scaled = inputs * scale_one
    qkv_pieces = [qkv_shard, qkv_far, qkv_near, swap_core(qkv_far)]
    gain_one = jnp.concatenate([p[block_d, :block_d] for p in qkv_pieces]).astype(F32)
    gain_two = jnp.concatenate([p[block_d + 1, :block_d] for p in qkv_pieces]).astype(F32)
    normed, queries, key_value = project(scaled, cos_table, sin_table, qkv_pieces, width_q)
    out_far = after(out_far, queries)
    out_pieces = [output_weight, out_far, out_near, swap_core(out_far)]
    if two_ctx():
        key_value_all = jnp.concatenate([key_value, swap_ctx(key_value)], axis=0)
    else:
        key_value_all = lax.all_gather(key_value, "ctx", axis=0, tiled=True)
    attended, log_total, branch = attend_forward(
        queries, key_value_all, key_value_all[:, width_kv:].T, key_code, query_codes, out_pieces
    )
    branch = psum_tensor(branch)

    def spread_wide(got, gate, up):
        return *far_wholes(got), swap_core(gate), swap_core(up)

    def spread_last(*values):
        return tuple(swap_core(v) for v in values)

    down_far = swap_x(after(down_weight, log_total))
    gate_far, up_far, gate_near, up_near = sealed(
        spread_wide, after(wide_got, log_total), gate_weight, up_weight
    )
    gate_last, up_last, down_near, down_last = sealed(
        spread_last, gate_far, up_far, down_weight, down_far
    )
    gates = [gate_weight, gate_far, gate_near, gate_last]
    ups = [up_weight, up_far, up_near, up_last]
    downs = [down_weight, down_far, down_near, down_last]
    wait = down_last
    branch = after(branch, wait)
    middle = inputs + RESIDUAL * branch.astype(F32)

    scale_two = norm_scale(middle)
    normed_two = (middle * scale_two * gain_two).astype(BF)
    hidden, grad_gate, grad_up, grad_two = mlp(normed_two, grad_mlp, gates, ups, downs)
    grad_two = psum_tensor(grad_two)

    def begin_down(hidden, grad_mlp):
        return outer_sum(hidden, grad_mlp, False, "down_outer").begin()

    def begin_rest(hidden, normed_two, grad_gate, grad_up, *downs):
        return (
            outer_sum(normed_two, grad_gate, True, "gate_outer").begin(),
            outer_sum(normed_two, grad_up, True, "up_outer").begin(),
            lift(hidden, downs),
        )

    begun = sealed(begin_down, hidden, grad_mlp)
    down_sum = outer_sum(hidden, grad_mlp, False, "down_outer").cross(begun)
    begun_gate, begun_up, mlp_part = sealed(
        begin_rest, after(hidden, begun[1]), normed_two, grad_gate, grad_up, *downs
    )
    gate_sum = outer_sum(normed_two, grad_gate, True, "gate_outer").cross(begun_gate)
    up_sum = outer_sum(normed_two, grad_up, True, "up_outer").cross(begun_up, down_sum.got)
    grad_two = after(grad_two, down_sum.sent, gate_sum.sent, up_sum.sent, mlp_part)
    down_sum.fold(grad_two).swap()
    mlp_sum = psum_tensor(after(mlp_part, grad_two))
    grad_two = grad_two.astype(F32)

    gain_two_part = jnp.sum(grad_two * middle * scale_two, axis=0)
    grad_middle = grad_out + norm_back(middle, scale_two, gain_two, grad_two)
    grad_branch = after((RESIDUAL * grad_middle).astype(BF), down_sum.low)
    query_low, key_value_parts = attend_backward(
        queries,
        key_value_all,
        key_value_all[:, :width_kv].T,
        key_code,
        query_codes,
        attended,
        grad_branch,
        log_total,
        turn,
        out_pieces,
    )
    if two_ctx():
        own_part = key_value_parts[:local_rows]
        got_part = swap_ctx(key_value_parts[local_rows:].astype(BF))
    else:
        own_part = lax.psum_scatter(
            key_value_parts.astype(BF), "ctx", scatter_dimension=0, tiled=True
        ).astype(F32)
        got_part = jnp.zeros(own_part.shape, BF)
    qkv_low, grad_one = entry_grad(
        query_low, own_part, got_part, cos_table, sin_table, qkv_pieces
    )
    gate_sum.fold(query_low)
    gate_sum.swap(got_part)

    def entry_term(attended, grad_branch, normed, qkv_low):
        return BlockSum(
            lambda k, n, adds: entry_outer(attended, grad_branch, normed, qkv_low, k, n, adds)
        )

    entry_inputs = (attended, grad_branch, normed, qkv_low)
    begun = sealed(lambda *v: entry_term(*v).begin(), *entry_inputs)
    entry_sum = entry_term(*entry_inputs).cross(begun, gate_sum.low)
    mlp_sum = after(mlp_sum, qkv_low, down_sum.peer, gate_sum.low, up_sum.fold(qkv_low).low, entry_sum.sent)
    grad_one = psum_tensor(after(grad_one, mlp_sum))


    def finish_wide(up_low, *pairs):
        peer = swap_ctx(up_low) if two_ctx() else lax.psum(up_low, "ctx")
        totals = [combine(low, other) for low, other in zip(pairs[::2], pairs[1::2], strict=True)]
        return combine(up_low, peer), *totals

    up_grad, gate_grad, down_grad = sealed(
        finish_wide,
        after(up_sum.low, mlp_sum),
        gate_sum.low,
        gate_sum.peer,
        down_sum.low,
        down_sum.peer,
    )
    entry_total = sealed(
        lambda *v: entry_term(*v[:4]).joined(v[4], v[5]).fold().swap().result(),
        after(attended, up_grad),
        *entry_inputs[1:],
        entry_sum.other,
        entry_sum.got,
    )
    layer_out = absolute((middle + RESIDUAL * mlp_sum.astype(F32)).astype(BF))
    grad_one = after(grad_one, entry_total, layer_out)
    output_grad, qkv_grad = entry_total[:, :block_d], entry_total[:, block_d:]
    grad_one = grad_one.astype(F32)
    gain_one_part = jnp.sum(grad_one * inputs * scale_one, axis=0)
    tokens_grad = absolute(
        (grad_middle + norm_back(inputs, scale_one, gain_one, grad_one)).astype(BF)
    )
    gain_blocks = split4(jnp.stack([gain_one_part, gain_two_part]), 1)
    gain_grad = sum_ctx(
        gain_blocks[0]
        + swap_x(gain_blocks[1])
        + swap_core(gain_blocks[2])
        + swap_both(gain_blocks[3])
    )
    return (
        layer_out,
        tokens_grad,
        gain_grad[0],
        qkv_grad[:, :width_q],
        qkv_grad[:, width_q : width_q + width_kv],
        qkv_grad[:, width_q + width_kv :],
        output_grad,
        gain_grad[1],
        gate_grad,
        up_grad,
        down_grad,
    )


def solution(mesh):
    return jax.shard_map(
        shards,
        mesh=mesh,
        in_specs=(
            P(("dp", "ctx"), None),
            P(("dp", "ctx"), None),
            P("dp"),
            P("dp", "tensor"),
            P("dp", "tensor"),
            P("dp", "tensor"),
            P("tensor", "dp"),
            P("dp"),
            P("dp", "tensor"),
            P("dp", "tensor"),
            P("tensor", "dp"),
            P("dp", None),
            P("dp", None),
        ),
        out_specs=(
            P(("dp", "ctx"), None),
            P(("dp", "ctx"), None),
            P("dp"),
            P("dp", "tensor"),
            P("dp", "tensor"),
            P("dp", "tensor"),
            P("tensor", "dp"),
            P("dp"),
            P("dp", "tensor"),
            P("dp", "tensor"),
            P("tensor", "dp"),
        ),
        check_vma=False,
    )
```

```python
import functools

import jax
import jax.numpy as jnp
from jax import lax
from jax.experimental import pallas as pl
from jax.experimental.pallas import tpu as pltpu
from jax.sharding import PartitionSpec as P

HD = 64
CLEN = 512

EPSILON = 1e-05
ROPE_BASE = 10000000.0
ATTN_SCALE = 0.015625
RESIDUAL = 0.22
NEGATIVE = -1e30
SEGMENT_STEP = 1 << 16
BF = jnp.bfloat16
F32 = jnp.float32
LIGHT = pl.CostEstimate(flops=1, bytes_accessed=1, transcendentals=0)


def dot_nt(a, b):
    return lax.dot_general(a, b, (((1,), (1,)), ((), ())), preferred_element_type=F32)

def dot_nn(a, b):
    return lax.dot_general(a, b, (((1,), (0,)), ((), ())), preferred_element_type=F32)

def fill_bias(bias, key_code, query_codes):
    code = key_code[...]
    below = code < query_codes[0:1, :]
    own = (code >= query_codes[1:2, :]) & (code <= query_codes[2:3, :])
    bias[...] = jnp.where(below | own, 0.0, NEGATIVE)

def fill_padded(padded, sources, lane0):
    block = jnp.concatenate([v[:, lane0 : lane0 + 2 * HD] for v in sources], axis=0)
    lane = lax.broadcasted_iota(jnp.int32, block.shape, 1)
    low = jnp.where(lane < HD, block, jnp.zeros_like(block))
    high = jnp.where(lane < HD, jnp.zeros_like(block), block)
    padded[0, 0] = low
    padded[0, 1] = pltpu.roll(low.astype(F32), HD, 1).astype(BF)
    padded[1, 0] = pltpu.roll(high.astype(F32), HD, 1).astype(BF)
    padded[1, 1] = high

def fill_turned(turned, sources, lane0):
    at = 0
    for v in sources:
        turned[:, at : at + v.shape[0]] = v[:, lane0 : lane0 + 2 * HD].astype(F32).T.astype(BF)
        at += v.shape[0]


def forward_kernel(chunk, parts, q_ref, code_ref, codes_ref, *refs):
    kv_refs = refs[:parts]
    out_ref, lse_ref, bias, keys, vt_ref = refs[parts:]
    total = code_ref.shape[0]
    rows = q_ref.shape[0]
    fill_turned(vt_ref, kv_refs, 2 * HD)
    fill_bias(bias, code_ref, codes_ref)
    fill_padded(keys, kv_refs, 0)

    def pair_step(pair, unused):
        group = pair // 2
        lanes = pl.ds(pl.multiple_of(pair * 128, 128), 128)
        q_pair = q_ref[:, lanes]
        mixed = []
        for side in range(2):
            def chunk_step(part, carry):
                top, norm, acc = carry
                at = pl.ds(pl.multiple_of(part * chunk, chunk), chunk)
                scores = dot_nt(keys[group, side, at, :], q_pair) + bias[at, :]
                new_top = jnp.maximum(top, jnp.max(scores, axis=0, keepdims=True))
                weights = jnp.exp(scores - new_top)
                shrink = jnp.exp(top - new_top)
                norm = norm * shrink + jnp.sum(weights, axis=0, keepdims=True)
                values = vt_ref[pl.ds(pl.multiple_of(group * HD, HD), HD), at]
                acc = acc * shrink + dot_nn(values, weights.astype(BF))
                return new_top, norm, acc

            carry = (jnp.full((1, rows), NEGATIVE, F32), jnp.zeros((1, rows), F32), jnp.zeros((HD, rows), F32))
            if total == chunk:
                carry = chunk_step(0, carry)
            else:
                carry = lax.fori_loop(0, total // chunk, chunk_step, carry)
            top, norm, acc = carry
            mixed.append(acc / norm)
            lse_ref[pl.ds(pair * 2 + side, 1), :] = top + jnp.log(norm)
        out_ref[:, lanes] = jnp.concatenate(mixed, axis=0).T.astype(BF)
        return unused

    lax.fori_loop(0, q_ref.shape[1] // 128, pair_step, 0)


def attend_forward(queries, key_values, key_code, query_codes):
    rows, width = queries.shape
    total = key_code.shape[0]
    chunk = min(total, 1024)
    return pl.pallas_call(
        functools.partial(forward_kernel, chunk, len(key_values)),
        out_shape=(
            jax.ShapeDtypeStruct((rows, width), BF),
            jax.ShapeDtypeStruct((width // HD, rows), F32),
        ),
        scratch_shapes=[
            pltpu.VMEM((total, rows), F32),
            pltpu.VMEM((2, 2, total, 128), BF),
            pltpu.VMEM((128, total), BF),
        ],
        compiler_params=pltpu.CompilerParams(vmem_limit_bytes=(32 if total <= 1024 else 58) << 20),
        cost_estimate=LIGHT,
        name="attend_forward",
    )(queries, key_code, query_codes, *key_values)

def backward_kernel(
    chunk, parts, q_ref, code_ref, codes_ref, att_ref, branch_ref, lse_ref, rot_ref, o0, o1, o2, o3, *refs
):
    kv_refs = refs[:parts]
    dq_ref, dkv_ref, grad_ref, bias, keys, values, kt_ref, delta, dk_acc, dv_acc = refs[parts:]
    total = code_ref.shape[0]
    rows = q_ref.shape[0]
    width = q_ref.shape[1]
    heads = width // HD
    fill_turned(kt_ref, kv_refs, 0)
    fill_bias(bias, code_ref, codes_ref)
    fill_padded(keys, kv_refs, 0)
    fill_padded(values, kv_refs, 128)
    block = o0.shape[1]
    grad = jnp.zeros((rows, width), F32)
    for r, piece in enumerate((o0, o1, o2, o3)):
        grad += dot_nt(branch_ref[:, r * block : (r + 1) * block], piece[...])
    grad_ref[...] = grad.astype(BF)
    owner = lax.broadcasted_iota(jnp.int32, (heads, width), 1) // HD
    member = jnp.where(owner == lax.broadcasted_iota(jnp.int32, (heads, width), 0), 1.0, 0.0)
    product = att_ref[...].astype(F32) * grad_ref[...].astype(F32)
    delta[...] = lax.dot_general(member, product, (((1,), (1,)), ((), ())), precision=lax.Precision.HIGHEST, preferred_element_type=F32)
    dk_acc[...] = jnp.zeros_like(dk_acc)
    dv_acc[...] = jnp.zeros_like(dv_acc)
    half = HD // 2

    def pair_step(pair, unused):
        group = pair // 2
        lanes = pl.ds(pl.multiple_of(pair * 128, 128), 128)
        q_pair = q_ref[:, lanes]
        g_pair = grad_ref[:, lanes]
        turned = []
        for side in range(2):
            head = pl.ds(pair * 2 + side, 1)
            lse = lse_ref[head, :]
            dlt = delta[head, :]
            def chunk_step(part, acc):
                at = pl.ds(pl.multiple_of(part * chunk, chunk), chunk)
                scores = dot_nt(keys[group, side, at, :], q_pair) + bias[at, :]
                probs = jnp.exp(scores - lse)
                dprobs = dot_nt(values[group, side, at, :], g_pair)
                dscores = (probs * (dprobs - dlt)).astype(BF)
                dv_acc[group, side, at, :] += dot_nn(probs.astype(BF), g_pair)
                dk_acc[group, side, at, :] += dot_nn(dscores, q_pair)
                kt = kt_ref[pl.ds(pl.multiple_of(group * HD, HD), HD), at]
                return acc + dot_nn(kt, dscores)
            acc = jnp.zeros((HD, rows), F32)
            if total == chunk:
                acc = chunk_step(0, acc)
            else:
                acc = lax.fori_loop(0, total // chunk, chunk_step, acc)
            acc = acc * (1.0 / HD)
            first, second = acc[:half], acc[half:]
            cosine, sine = rot_ref[:half, :], rot_ref[half:, :]
            turned.append(first * cosine + second * sine)
            turned.append(second * cosine - first * sine)
        dq_ref[:, lanes] = jnp.concatenate(turned, axis=0).T.astype(BF)
        return unused

    lax.fori_loop(0, width // 128, pair_step, 0)
    lane = lax.broadcasted_iota(jnp.int32, (total, 128), 1)
    for which, acc in ((0, dk_acc), (1, dv_acc)):
        zero = acc[0, 0] + pltpu.roll(acc[0, 1], HD, 1)
        one = pltpu.roll(acc[1, 0], HD, 1) + acc[1, 1]
        dkv_ref[:, which * 128 : (which + 1) * 128] = jnp.where(lane < HD, zero, one)

def attend_backward(
    queries, key_values, key_code, query_codes, attended, grad_branch, lse, turn, out_pieces
):
    rows, width = queries.shape
    total = key_code.shape[0]
    chunk = min(total, 1024)
    return pl.pallas_call(
        functools.partial(backward_kernel, chunk, len(key_values)),
        out_shape=(jax.ShapeDtypeStruct((rows, width), BF), jax.ShapeDtypeStruct((total, 256), F32)),
        scratch_shapes=[
            pltpu.VMEM((rows, width), BF),
            pltpu.VMEM((total, rows), F32),
            pltpu.VMEM((2, 2, total, 128), BF),
            pltpu.VMEM((2, 2, total, 128), BF),
            pltpu.VMEM((128, total), BF),
            pltpu.VMEM((width // HD, rows), F32),
            pltpu.VMEM((2, 2, total, 128), F32),
            pltpu.VMEM((2, 2, total, 128), F32),
        ],
        compiler_params=pltpu.CompilerParams(vmem_limit_bytes=(32 if total <= 1024 else 58) << 20),
        cost_estimate=LIGHT,
        name="attend_backward",
    )(queries, key_code, query_codes, attended, grad_branch, lse, turn, *out_pieces, *key_values)


def out_kernel(attended_ref, o0, o1, o2, o3, branch_ref):
    block = o0.shape[1]
    for r, piece in enumerate((o0, o1, o2, o3)):
        branch_ref[:, r * block : (r + 1) * block] = dot_nn(attended_ref[...], piece[...]).astype(BF)


def out_project(attended, out_pieces):
    return pl.pallas_call(
        out_kernel,
        out_shape=jax.ShapeDtypeStruct((attended.shape[0], 4 * out_pieces[0].shape[1]), BF),
        compiler_params=pltpu.CompilerParams(vmem_limit_bytes=16 << 20),
        cost_estimate=LIGHT,
        name="out_project",
    )(attended, *out_pieces)


def rows_at(index, size):
    return pl.ds(pl.multiple_of(index * size, size), size)


def half_turn(block):
    lane = lax.broadcasted_iota(jnp.int32, block.shape, 1)
    return jnp.where(lane % HD < HD // 2, pltpu.roll(block, 128 - HD // 2, 1), pltpu.roll(block, HD // 2, 1))


def project_kv_kernel(x_ref, scale_ref, cos_ref, sin_ref, p0, p1, p2, p3, normed_ref, kv_ref):
    block = x_ref.shape[1] // 4
    total = jnp.zeros(kv_ref.shape, F32)
    for r, piece in enumerate((p0, p1, p2, p3)):
        lanes = slice(r * block, (r + 1) * block)
        rows = block // piece.shape[1]
        gain = jnp.concatenate([piece[block + i : block + i + 1, :] for i in range(rows)], axis=1)
        low = (x_ref[:, lanes].astype(F32) * scale_ref[...] * gain.astype(F32)).astype(BF)
        normed_ref[:, lanes] = low
        total += dot_nn(low, piece[:block, :])
    keys = total[:, :128]
    kv_ref[:, :128] = (keys * cos_ref[...] + half_turn(keys) * sin_ref[...]).astype(BF)
    kv_ref[:, 128:] = total[:, 128:].astype(BF)


def project_kv(tokens, scale, cos_table, sin_table, pieces):
    rows, model = tokens.shape
    return pl.pallas_call(
        project_kv_kernel,
        out_shape=(
            jax.ShapeDtypeStruct((rows, model), BF),
            jax.ShapeDtypeStruct((rows, pieces[0].shape[1]), BF),
        ),
        compiler_params=pltpu.CompilerParams(vmem_limit_bytes=24 << 20),
        cost_estimate=LIGHT,
        name="project_kv",
    )(tokens, scale, cos_table, sin_table, *pieces)


def project_q_kernel(normed_ref, cos_ref, sin_ref, p0, p1, p2, p3, q_ref):
    block = p0.shape[0]
    total = jnp.zeros(q_ref.shape, F32)
    for r, piece in enumerate((p0, p1, p2, p3)):
        total += dot_nn(normed_ref[:, r * block : (r + 1) * block], piece[...])
    for at in range(0, q_ref.shape[1], 128):
        part = total[:, at : at + 128]
        part = part * cos_ref[...] + half_turn(part) * sin_ref[...]
        q_ref[:, at : at + 128] = part.astype(BF) * jnp.asarray(ATTN_SCALE, BF)


def project_q(normed, cos_table, sin_table, pieces):
    return pl.pallas_call(
        project_q_kernel,
        out_shape=jax.ShapeDtypeStruct((normed.shape[0], pieces[0].shape[1]), BF),
        compiler_params=pltpu.CompilerParams(vmem_limit_bytes=24 << 20),
        cost_estimate=LIGHT,
        name="project_q",
    )(normed, cos_table, sin_table, *pieces)


def mlp_kernel(halves, index_ref, h_ref, g_ref, *refs):
    count = 6 if halves else 4
    given, downs = (refs[:count], refs[count : 2 * count]), refs[2 * count : 2 * count + 4]
    hidden_ref, dgate_ref, dup_ref, dh_ref, acc, joined = refs[2 * count + 4 :]
    step = pl.program_id(0)
    block = h_ref.shape[1] // 4
    sides = []
    for which, pieces in enumerate(given):
        if halves:
            half = block // 2
            first = pl.multiple_of(index_ref[0] * half, half)
            second = pl.multiple_of((1 - index_ref[0]) * half, half)
            for far in range(2):
                joined[which, far, pl.ds(first, half), :] = pieces[3 * far + 1][...]
                joined[which, far, pl.ds(second, half), :] = pieces[3 * far + 2][...]
            pieces = (pieces[0], joined.at[which, 0], pieces[3], joined.at[which, 1])
        sides.append(pieces)
    gates, ups = sides
    gate = up = dhid = None
    for r in range(4):
        lanes = slice(r * block, (r + 1) * block)
        h = h_ref[:, lanes]
        terms = (
            dot_nn(h, gates[r][...]),
            dot_nn(h, ups[r][...]),
            dot_nt(g_ref[:, lanes], downs[r][...]),
        )
        gate, up, dhid = terms if r == 0 else (gate + terms[0], up + terms[1], dhid + terms[2])
    sigma = jax.nn.sigmoid(gate)
    active = gate * sigma
    hidden_ref[...] = (active * up).astype(BF)
    dgate = (dhid * up * sigma * (1.0 + gate * (1.0 - sigma))).astype(BF)
    dup = (dhid * active).astype(BF)
    dgate_ref[...] = dgate
    dup_ref[...] = dup
    for r in range(4):
        lanes = slice(r * block, (r + 1) * block)
        term = dot_nt(dgate, gates[r][...]) + dot_nt(dup, ups[r][...])

        @pl.when(step == 0)
        def _():
            acc[:, lanes] = term

        @pl.when(step != 0)
        def _():
            acc[:, lanes] += term

    @pl.when(step == pl.num_programs(0) - 1)
    def _():
        dh_ref[...] = acc[...].astype(BF)


def mlp(normed, grad, index, gates, ups, downs):
    rows, model = normed.shape
    hidden = downs[0].shape[0]
    tile = 512
    whole = pl.BlockSpec((rows, model), lambda j, s: (0, 0))
    wide = [pl.BlockSpec((size, tile), lambda j, s, at=at: (at, j)) for unused, size, at in gates + ups]
    tall = pl.BlockSpec((tile, downs[0].shape[1]), lambda j, s: (j, 0))
    out = pl.BlockSpec((rows, tile), lambda j, s: (0, j))
    return pl.pallas_call(
        functools.partial(mlp_kernel, len(gates) > 4),
        grid_spec=pltpu.PrefetchScalarGridSpec(
            num_scalar_prefetch=1,
            grid=(hidden // tile,),
            in_specs=[whole] * 2 + wide + [tall] * 4,
            out_specs=[out] * 3 + [whole],
            scratch_shapes=[
                pltpu.VMEM((rows, model), F32),
                pltpu.VMEM((2, 2, model // 4, tile), BF),
            ],
        ),
        out_shape=[jax.ShapeDtypeStruct((rows, hidden), BF)] * 3
        + [jax.ShapeDtypeStruct((rows, model), BF)],
        compiler_params=pltpu.CompilerParams(vmem_limit_bytes=44 << 20),
        cost_estimate=LIGHT,
        name="mlp",
    )(index, normed, grad, *[v[0] for v in gates + ups], *downs)


def entry_kernel(dq_ref, own_ref, got_ref, cos_ref, sin_ref, *refs):
    queries, keys, (low_ref, dh_ref) = refs[:4], refs[4:8], refs[8:]
    block = dh_ref.shape[1] // 4
    width_q = dq_ref.shape[1]
    low_ref[:, :width_q] = dq_ref[...]
    sums = own_ref[...] + got_ref[...].astype(F32)
    dk = sums[:, :128]
    low_ref[:, width_q : width_q + 128] = (dk * cos_ref[...] - half_turn(dk) * sin_ref[...]).astype(BF)
    low_ref[:, width_q + 128 :] = sums[:, 128:].astype(BF)
    low = low_ref[:, width_q:]
    for r in range(4):
        term = dot_nt(dq_ref[...], queries[r][...]) + dot_nt(low, keys[r][:block, :])
        dh_ref[:, r * block : (r + 1) * block] = term.astype(BF)


def entry_grad(dq_low, own, got, cos_table, sin_table, query_pieces, key_pieces):
    rows, width_q = dq_low.shape
    block = query_pieces[0].shape[0]
    return pl.pallas_call(
        entry_kernel,
        out_shape=(
            jax.ShapeDtypeStruct((rows, width_q + key_pieces[0].shape[1]), BF),
            jax.ShapeDtypeStruct((rows, 4 * block), BF),
        ),
        compiler_params=pltpu.CompilerParams(vmem_limit_bytes=24 << 20),
        cost_estimate=LIGHT,
        name="entry_grad",
    )(dq_low, own, got, cos_table, sin_table, *query_pieces, *key_pieces)


def outer_kernel(n_adds, a_ref, b_ref, *refs):
    total = lax.dot_general(
        a_ref[...], b_ref[...], (((0,), (0,)), ((), ())), preferred_element_type=F32
    )
    for add in refs[:n_adds]:
        total += add[...].astype(F32)
    refs[n_adds][...] = total.astype(BF)


def outer(left, right, left_blocks, right_blocks, adds, name):
    rows = left.shape[0]
    size_m, size_n = left.shape[1] // 4, right.shape[1] // 4
    first_m, count_m = left_blocks
    first_n, count_n = right_blocks
    cut_rows = count_m < 4
    wide = size_n * count_n
    in_specs = [
        pl.BlockSpec((rows, size_m), lambda i: (0, first_m + i)),
        pl.BlockSpec((rows, wide), lambda i: (0, first_n // count_n)),
    ]
    for array, first in adds:
        if cut_rows:
            in_specs.append(pl.BlockSpec((size_m, wide), lambda i, first=first: (first + i, 0)))
        else:
            in_specs.append(pl.BlockSpec((size_m, wide), lambda i, first=first: (i, first)))
    return pl.pallas_call(
        functools.partial(outer_kernel, len(adds)),
        grid=(count_m,),
        in_specs=in_specs,
        out_specs=pl.BlockSpec((size_m, wide), lambda i: (i, 0)),
        out_shape=jax.ShapeDtypeStruct((size_m * count_m, wide), BF),
        compiler_params=pltpu.CompilerParams(vmem_limit_bytes=32 << 20),
        cost_estimate=LIGHT,
        name=name,
    )(left, right, *[array for array, unused in adds])


def lift_kernel(hidden_ref, d0, d1, d2, d3, out_ref, acc):
    step = pl.program_id(0)
    block = d0.shape[1]
    for r, piece in enumerate((d0, d1, d2, d3)):
        lanes = slice(r * block, (r + 1) * block)
        term = dot_nn(hidden_ref[...], piece[...])

        @pl.when(step == 0)
        def _():
            acc[:, lanes] = term

        @pl.when(step != 0)
        def _():
            acc[:, lanes] += term

    @pl.when(step == pl.num_programs(0) - 1)
    def _():
        out_ref[...] = acc[...].astype(BF)


def lift(hidden, downs):
    rows, width = hidden.shape
    block = downs[0].shape[1]
    tile = 512
    return pl.pallas_call(
        lift_kernel,
        grid=(width // tile,),
        in_specs=[pl.BlockSpec((rows, tile), lambda j: (0, j))]
        + [pl.BlockSpec((tile, block), lambda j: (j, 0))] * 4,
        out_specs=pl.BlockSpec((rows, 4 * block), lambda j: (0, 0)),
        out_shape=jax.ShapeDtypeStruct((rows, 4 * block), BF),
        scratch_shapes=[pltpu.VMEM((rows, 4 * block), F32)],
        compiler_params=pltpu.CompilerParams(vmem_limit_bytes=32 << 20),
        cost_estimate=LIGHT,
        name="lift",
    )(hidden, *downs)


def entry_outer_kernel(n_adds, attended_ref, branch_ref, normed_ref, low_ref, *refs):
    out_ref = refs[n_adds]
    width = attended_ref.shape[1]
    head = lax.dot_general(
        attended_ref[...], branch_ref[...], (((0,), (0,)), ((), ())), preferred_element_type=F32
    )
    tail = lax.dot_general(
        normed_ref[...], low_ref[...], (((0,), (0,)), ((), ())), preferred_element_type=F32
    )
    for add in refs[:n_adds]:
        head += add[:, : head.shape[1]].astype(F32)
        tail += add[:, head.shape[1] :].astype(F32)
    out_ref[:, : head.shape[1]] = head.astype(BF)
    out_ref[:, head.shape[1] :] = tail.astype(BF)


def entry_outer(attended, branch, normed, low, first, count, adds):
    rows, heads = attended.shape
    block = branch.shape[1] // 4
    width = block + low.shape[1]
    column = pl.BlockSpec((rows, block), lambda i: (0, first + i))
    in_specs = [
        pl.BlockSpec((rows, heads), lambda i: (0, 0)),
        column,
        column,
        pl.BlockSpec(low.shape, lambda i: (0, 0)),
    ]
    for array, at in adds:
        in_specs.append(pl.BlockSpec((block, width), lambda i, at=at: (at + i, 0)))
    return pl.pallas_call(
        functools.partial(entry_outer_kernel, len(adds)),
        grid=(count,),
        in_specs=in_specs,
        out_specs=pl.BlockSpec((block, width), lambda i: (i, 0)),
        out_shape=jax.ShapeDtypeStruct((block * count, width), BF),
        compiler_params=pltpu.CompilerParams(vmem_limit_bytes=24 << 20),
        cost_estimate=LIGHT,
        name="entry_outer",
    )(attended, branch, normed, low, *[array for array, unused in adds])


def after(value, *others):
    if not others:
        return value
    return lax.optimization_barrier((value, *others))[0]


def sealed(step, *values):
    skipped = lambda *v: jax.tree.map(lambda a: jnp.zeros(a.shape, a.dtype), jax.eval_shape(step, *v))
    return lax.cond(lax.optimization_barrier(jnp.asarray(True)), step, skipped, *values)


def swap_core(value):
    return lax.ppermute(value, "dp", [(i, i ^ 1) for i in range(4)])


def swap_x(value):
    return lax.ppermute(value, "dp", [(i, i ^ 2) for i in range(4)])


def swap_both(value):
    return lax.ppermute(value, "dp", [(i, i ^ 3) for i in range(4)])


def swap_ctx(value):
    return lax.ppermute(value, "ctx", [(0, 1), (1, 0)])


def two_ctx():
    return lax.axis_size("ctx") == 2


def sum_ctx(total):
    low = total.astype(BF)
    if two_ctx():
        return low.astype(F32) + swap_ctx(low).astype(F32)
    return lax.psum(low, "ctx").astype(F32)


def far_halves(one, two, wait):
    if not two_ctx():
        return swap_x(after(jnp.concatenate([one, two]), wait))
    half = one.shape[0] // 2
    at = lax.axis_index("ctx") * half
    mine = [lax.dynamic_slice_in_dim(v, at, half) for v in (one, two)]
    return swap_x(after(jnp.concatenate(mine), wait))


def psum_tensor(value):
    return lax.psum(value, "tensor")


def swap_bits(index):
    return ((index & 1) << 1) | (index >> 1)


def take_blocks(value, indices):
    size = value.shape[1] // 4
    return jnp.concatenate(
        [lax.dynamic_slice_in_dim(value, i * size, size, 1) for i in indices], axis=1
    )


def relative(value):
    mine = lax.axis_index("dp")
    return take_blocks(value, [mine ^ k for k in (0, 2, 1, 3)])


def absolute(value):
    mine = lax.axis_index("dp")
    return take_blocks(value, [swap_bits(mine ^ k) for k in range(4)])


def split4(value, axis):
    size = value.shape[axis] // 4
    return [lax.slice_in_dim(value, r * size, (r + 1) * size, axis=axis) for r in range(4)]


def token_places(row_ids, order_row, seen_row, prompt_len, block_rows, cont_len):
    block_total = order_row.shape[0]
    block_pick = (row_ids // block_rows)[:, None] == jnp.arange(block_total, dtype=jnp.int32)[
        None, :
    ]
    chosen = jnp.sum(jnp.where(block_pick, order_row[None, :], 0), axis=1)
    global_ids = chosen * block_rows + row_ids % block_rows
    in_prompt = global_ids < prompt_len
    segment = jnp.where(in_prompt, 0, 1 + (global_ids - prompt_len) // cont_len)
    cont_count = seen_row.shape[0]
    which_cont = (segment - 1)[:, None] == jnp.arange(cont_count, dtype=jnp.int32)[None, :]
    limit = jnp.sum(jnp.where(which_cont, seen_row[None, :], 0), axis=1)
    places = jnp.where(in_prompt, global_ids, limit + (global_ids - prompt_len) % cont_len)
    return (segment, places, limit)


def norm_scale(values):
    return lax.rsqrt(jnp.mean(values * values, axis=-1, keepdims=True) + EPSILON)


def norm_back(values, scale, gain, grad):
    weighted = gain * grad
    inner = jnp.mean(weighted * values, axis=-1, keepdims=True)
    return scale * weighted - values * (scale * scale * scale) * inner


def combine(low, peer):
    if two_ctx():
        return low.astype(F32) + peer.astype(F32)
    return peer.astype(F32)


class BlockSum:
    def __init__(self, term):
        self.term = term

    def begin(self):
        other = swap_core(self.term(2, 2, ()))
        return other, self.term(1, 1, ((other, 1),))

    def cross(self, begun, *wait):
        self.other, self.sent = begun
        self.got = swap_x(after(self.sent, *wait))
        return self

    def joined(self, other, got):
        self.other, self.got = other, got
        return self

    def fold(self, *wait):
        self.low = self.term(0, 1, ((self.other, 0), (after(self.got, *wait), 0)))
        return self

    def swap(self, *wait):
        low = after(self.low, *wait)
        self.peer = swap_ctx(low) if two_ctx() else lax.psum(low, "ctx")
        return self

    def result(self):
        return combine(self.low, self.peer)


def outer_sum(left, right, cut_left, name):
    def term(k, n, adds):
        cut, whole = (k, n), (0, 4)
        if cut_left:
            return outer(left, right, cut, whole, adds, name)
        return outer(left, right, whole, cut, adds, name)

    return BlockSum(term)


def shards(
    tokens,
    cotangent,
    first_gain,
    query_weight,
    key_weight,
    value_weight,
    output_weight,
    second_gain,
    gate_weight,
    up_weight,
    down_weight,
    block_order,
    prefix_seen,
):
    ctx_size = lax.axis_size("ctx")
    local_rows = tokens.shape[0]
    group_rows = local_rows * ctx_size
    offset = lax.axis_index("ctx") * local_rows
    width_q = query_weight.shape[1]
    width_kv = key_weight.shape[1]
    block_d = query_weight.shape[0]

    query_far = swap_x(query_weight)
    query_near = swap_core(query_weight)
    gain_rows = jnp.stack([first_gain, second_gain]).reshape(-1, 2 * width_kv)
    kv_shard = jnp.concatenate(
        [
            jnp.concatenate([after(key_weight, query_near), value_weight], axis=1),
            jnp.pad(gain_rows, ((0, 32 - gain_rows.shape[0]), (0, 0))),
        ],
        axis=0,
    )
    kv_far = swap_x(kv_shard)
    kv_near = swap_core(kv_shard)
    out_far = swap_x(after(output_weight, kv_near))
    out_near = swap_core(after(output_weight, kv_near))
    wide_got = far_halves(gate_weight, up_weight, out_far)

    tokens, block_order = (after(v, query_near) for v in (tokens, block_order))
    all_ids = jnp.arange(group_rows, dtype=jnp.int32)
    if two_ctx():
        all_ids = jnp.where(all_ids < local_rows, all_ids + offset, all_ids - offset)
    key_seg, key_pos, key_lim = token_places(
        all_ids, block_order[0], prefix_seen[0], group_rows // 2, local_rows // 2, CLEN
    )
    if two_ctx():
        query_seg, query_pos, query_lim = key_seg[:local_rows], key_pos[:local_rows], key_lim[:local_rows]
    else:
        query_seg = lax.dynamic_slice_in_dim(key_seg, offset, local_rows)
        query_pos = lax.dynamic_slice_in_dim(key_pos, offset, local_rows)
        query_lim = lax.dynamic_slice_in_dim(key_lim, offset, local_rows)
    key_code = (key_seg * SEGMENT_STEP + key_pos)[:, None]
    in_prompt = query_seg == 0
    below = jnp.where(in_prompt, query_pos + 1, query_lim)
    low_code = jnp.where(in_prompt, 1, query_seg * SEGMENT_STEP)
    high_code = jnp.where(in_prompt, 0, query_seg * SEGMENT_STEP + query_pos)
    query_codes = jnp.stack([below, low_code, high_code] + [below] * 5)
    half_size = HD // 2
    freq = ROPE_BASE ** (-(jnp.arange(half_size, dtype=F32) * 2.0) / HD)
    angle_t = freq[:, None] * query_pos.astype(F32)[None, :]
    turn = jnp.concatenate([jnp.cos(angle_t), jnp.sin(angle_t)], axis=0)
    cosine, sine = turn[:half_size].T, turn[half_size:].T
    cos_table = jnp.concatenate([cosine] * 4, axis=1)
    sin_table = jnp.concatenate([-sine, sine] * 2, axis=1)

    tokens = relative(tokens)
    inputs = tokens.astype(F32)
    scale_one = norm_scale(inputs)
    kv_pieces = [kv_shard, kv_far, kv_near, swap_core(kv_far)]
    gain_at = block_d + block_d // (2 * width_kv)
    gain_one, gain_two = (
        jnp.concatenate([p[i : i + gain_at - block_d].reshape(-1) for p in kv_pieces]).astype(F32)
        for i in (block_d, gain_at)
    )
    normed, key_value = project_kv(tokens, scale_one, cos_table, sin_table, kv_pieces)
    if two_ctx():
        key_values = (key_value, swap_ctx(key_value))
    else:
        key_values = (lax.all_gather(key_value, "ctx", axis=0, tiled=True),)
    query_pieces = [query_weight, query_far, query_near, swap_core(query_far)]
    queries = project_q(normed, cos_table, sin_table, query_pieces)
    attended, log_total = attend_forward(queries, key_values, key_code, query_codes)
    out_far = after(out_far, queries)
    out_pieces = [output_weight, out_far, out_near, swap_core(out_far)]
    branch = out_project(attended, out_pieces)
    grad_out = relative(after(cotangent, log_total)).astype(F32)
    grad_mlp = (RESIDUAL * grad_out).astype(BF)
    branch = psum_tensor(branch)

    def spread_wide(got, gate, up, down):
        gate_near = swap_core(gate)
        near = gate_near, swap_core(up), swap_core(after(got, gate_near)), swap_core(after(down, gate_near))
        return swap_ctx(got) if two_ctx() else got, *near

    def spread_last(*values):
        return tuple(swap_core(v) for v in values)

    down_far = swap_x(after(down_weight, log_total))
    wide_other, gate_near, up_near, last_got, down_near = sealed(
        spread_wide, after(wide_got, log_total), gate_weight, up_weight, down_weight
    )
    last_other, down_last = sealed(spread_last, wide_other, down_far)
    downs = [down_weight, down_far, down_near, down_last]
    half = block_d // 2 if two_ctx() else block_d
    far = (wide_got, wide_other) if two_ctx() else (wide_got,)
    last = (last_got, last_other) if two_ctx() else (last_got,)
    gates, ups = (
        [(own, block_d, 0), *[(v, half, at) for v in far], (near, block_d, 0), *[(v, half, at) for v in last]]
        for own, near, at in ((gate_weight, gate_near, 0), (up_weight, up_near, 1))
    )
    wait = down_last
    branch = after(branch, wait)
    middle = inputs + RESIDUAL * branch.astype(F32)

    scale_two = norm_scale(middle)
    normed_two = (middle * scale_two * gain_two).astype(BF)
    hidden, grad_gate, grad_up, grad_two = mlp(
        normed_two, grad_mlp, lax.axis_index("ctx")[None], gates, ups, downs
    )
    grad_two = psum_tensor(grad_two)

    def begin(hidden, normed_two, grad_mlp, grad_gate, grad_up, *downs):
        down_sum = outer_sum(hidden, grad_mlp, False, "down_outer")
        down_sum.cross(down_sum.begin())
        gate_begun = outer_sum(normed_two, grad_gate, True, "gate_outer").begin()
        up_begun = outer_sum(normed_two, grad_up, True, "up_outer").begin()
        part = lift(hidden, downs)
        return down_sum.fold(gate_begun[1], up_begun[1], part).low, gate_begun, up_begun, part

    down_sum = BlockSum(None)
    down_sum.low, gate_begun, up_begun, mlp_part = sealed(
        begin, hidden, normed_two, grad_mlp, grad_gate, grad_up, *downs
    )
    down_sum.swap()
    gate_sum = outer_sum(normed_two, grad_gate, True, "gate_outer").cross(gate_begun)
    up_sum = outer_sum(normed_two, grad_up, True, "up_outer")
    grad_two = after(grad_two, down_sum.low)
    mlp_sum = psum_tensor(after(mlp_part, grad_two))
    up_sum.cross(up_begun, grad_two)
    grad_two = grad_two.astype(F32)

    gain_two_part = jnp.sum(grad_two * middle * scale_two, axis=0)
    grad_middle = grad_out + norm_back(middle, scale_two, gain_two, grad_two)
    grad_branch = (RESIDUAL * grad_middle).astype(BF)
    query_low, key_value_parts = attend_backward(
        queries,
        key_values,
        key_code,
        query_codes,
        attended,
        grad_branch,
        log_total,
        turn,
        out_pieces,
    )
    if two_ctx():
        own_part = key_value_parts[:local_rows]
        got_part = swap_ctx(key_value_parts[local_rows:].astype(BF))
    else:
        own_part = lax.psum_scatter(
            key_value_parts.astype(BF), "ctx", scatter_dimension=0, tiled=True
        ).astype(F32)
        got_part = jnp.zeros(own_part.shape, BF)
    qkv_low, grad_one = entry_grad(
        query_low, own_part, got_part, cos_table, sin_table, query_pieces, kv_pieces
    )
    gate_sum.fold(query_low)
    gate_sum.swap(got_part)

    def entry_term(attended, grad_branch, normed, qkv_low):
        return BlockSum(
            lambda k, n, adds: entry_outer(attended, grad_branch, normed, qkv_low, k, n, adds)
        )

    entry_inputs = (attended, grad_branch, normed, qkv_low)
    begun = sealed(lambda *v: entry_term(*v).begin(), *entry_inputs)
    entry_sum = entry_term(*entry_inputs).cross(begun, gate_sum.low)
    mlp_sum = after(mlp_sum, qkv_low, down_sum.peer, gate_sum.low, up_sum.fold(qkv_low).low, entry_sum.sent)
    grad_one = psum_tensor(after(grad_one, mlp_sum))


    up_sum.swap()

    def finish(middle, mlp_sum, *values):
        entry_sum = entry_term(*values[:4]).joined(*values[4:6]).fold().swap()
        layer_out = absolute((middle + RESIDUAL * mlp_sum.astype(F32)).astype(BF))
        totals = (combine(*values[i : i + 2]) for i in (6, 8, 10))
        return layer_out, *totals, entry_sum.result()

    layer_out, down_grad, gate_grad, up_grad, entry_total = sealed(
        finish,
        middle,
        mlp_sum,
        *entry_inputs,
        entry_sum.other,
        entry_sum.got,
        down_sum.low,
        down_sum.peer,
        gate_sum.low,
        gate_sum.peer,
        up_sum.low,
        up_sum.peer,
    )
    grad_one = after(grad_one, down_grad)
    output_grad, qkv_grad = entry_total[:, :block_d], entry_total[:, block_d:]
    grad_one = grad_one.astype(F32)
    gain_one_part = jnp.sum(grad_one * inputs * scale_one, axis=0)
    tokens_grad = absolute(
        (grad_middle + norm_back(inputs, scale_one, gain_one, grad_one)).astype(BF)
    )
    gain_blocks = split4(jnp.stack([gain_one_part, gain_two_part]), 1)
    gain_grad = sum_ctx(
        gain_blocks[0]
        + swap_x(gain_blocks[1])
        + swap_core(gain_blocks[2])
        + swap_both(gain_blocks[3])
    )
    return (
        layer_out,
        tokens_grad,
        gain_grad[0],
        qkv_grad[:, :width_q],
        qkv_grad[:, width_q : width_q + width_kv],
        qkv_grad[:, width_q + width_kv :],
        output_grad,
        gain_grad[1],
        gate_grad,
        up_grad,
        down_grad,
    )


def solution(mesh):
    return jax.shard_map(
        shards,
        mesh=mesh,
        in_specs=(
            P(("dp", "ctx"), None),
            P(("dp", "ctx"), None),
            P("dp"),
            P("dp", "tensor"),
            P("dp", "tensor"),
            P("dp", "tensor"),
            P("tensor", "dp"),
            P("dp"),
            P("dp", "tensor"),
            P("dp", "tensor"),
            P("tensor", "dp"),
            P("dp", None),
            P("dp", None),
        ),
        out_specs=(
            P(("dp", "ctx"), None),
            P(("dp", "ctx"), None),
            P("dp"),
            P("dp", "tensor"),
            P("dp", "tensor"),
            P("dp", "tensor"),
            P("tensor", "dp"),
            P("dp"),
            P("dp", "tensor"),
            P("dp", "tensor"),
            P("tensor", "dp"),
        ),
        check_vma=False,
    )
```

```python
import functools

import jax
import jax.numpy as jnp
from jax import lax
from jax.experimental import pallas as pl
from jax.experimental.pallas import tpu as pltpu
from jax.sharding import PartitionSpec as P

HD = 64
CLEN = 512

EPSILON = 1e-05
ROPE_BASE = 10000000.0
ATTN_SCALE = 0.015625
RESIDUAL = 0.22
NEGATIVE = -1e30
SEGMENT_STEP = 1 << 16
BF = jnp.bfloat16
F32 = jnp.float32
LIGHT = pl.CostEstimate(flops=1, bytes_accessed=1, transcendentals=0)


def dot_nt(a, b):
    return lax.dot_general(a, b, (((1,), (1,)), ((), ())), preferred_element_type=F32)

def dot_nn(a, b):
    return lax.dot_general(a, b, (((1,), (0,)), ((), ())), preferred_element_type=F32)

def fill_bias(bias, key_code, query_codes):
    code = key_code[...]
    below = code < query_codes[0:1, :]
    own = (code >= query_codes[1:2, :]) & (code <= query_codes[2:3, :])
    bias[...] = jnp.where(below | own, 0.0, NEGATIVE)

def fill_padded(padded, sources, lane0):
    block = jnp.concatenate([v[:, lane0 : lane0 + 2 * HD] for v in sources], axis=0)
    lane = lax.broadcasted_iota(jnp.int32, block.shape, 1)
    low = jnp.where(lane < HD, block, jnp.zeros_like(block))
    high = jnp.where(lane < HD, jnp.zeros_like(block), block)
    padded[0, 0] = low
    padded[0, 1] = pltpu.roll(low.astype(F32), HD, 1).astype(BF)
    padded[1, 0] = pltpu.roll(high.astype(F32), HD, 1).astype(BF)
    padded[1, 1] = high

def fill_turned(turned, sources, lane0):
    at = 0
    for v in sources:
        turned[:, at : at + v.shape[0]] = v[:, lane0 : lane0 + 2 * HD].astype(F32).T.astype(BF)
        at += v.shape[0]


def forward_kernel(chunk, parts, q_ref, code_ref, codes_ref, *refs):
    kv_refs = refs[:parts]
    out_ref, lse_ref, bias, keys, vt_ref = refs[parts:]
    total = code_ref.shape[0]
    rows = q_ref.shape[0]
    fill_turned(vt_ref, kv_refs, 2 * HD)
    fill_bias(bias, code_ref, codes_ref)
    fill_padded(keys, kv_refs, 0)

    def pair_step(pair, unused):
        group = pair // 2
        lanes = pl.ds(pl.multiple_of(pair * 128, 128), 128)
        q_pair = q_ref[:, lanes]
        mixed = []
        for side in range(2):
            def chunk_step(part, carry):
                top, norm, acc = carry
                at = pl.ds(pl.multiple_of(part * chunk, chunk), chunk)
                scores = dot_nt(keys[group, side, at, :], q_pair) + bias[at, :]
                new_top = jnp.maximum(top, jnp.max(scores, axis=0, keepdims=True))
                weights = jnp.exp(scores - new_top)
                shrink = jnp.exp(top - new_top)
                norm = norm * shrink + jnp.sum(weights, axis=0, keepdims=True)
                values = vt_ref[pl.ds(pl.multiple_of(group * HD, HD), HD), at]
                acc = acc * shrink + dot_nn(values, weights.astype(BF))
                return new_top, norm, acc

            carry = (jnp.full((1, rows), NEGATIVE, F32), jnp.zeros((1, rows), F32), jnp.zeros((HD, rows), F32))
            if total == chunk:
                carry = chunk_step(0, carry)
            else:
                carry = lax.fori_loop(0, total // chunk, chunk_step, carry)
            top, norm, acc = carry
            mixed.append(acc / norm)
            lse_ref[pl.ds(pair * 2 + side, 1), :] = top + jnp.log(norm)
        out_ref[:, lanes] = jnp.concatenate(mixed, axis=0).T.astype(BF)
        return unused

    lax.fori_loop(0, q_ref.shape[1] // 128, pair_step, 0)


def attend_forward(queries, key_values, key_code, query_codes):
    rows, width = queries.shape
    total = key_code.shape[0]
    chunk = min(total, 1024)
    return pl.pallas_call(
        functools.partial(forward_kernel, chunk, len(key_values)),
        out_shape=(
            jax.ShapeDtypeStruct((rows, width), BF),
            jax.ShapeDtypeStruct((width // HD, rows), F32),
        ),
        scratch_shapes=[
            pltpu.VMEM((total, rows), F32),
            pltpu.VMEM((2, 2, total, 128), BF),
            pltpu.VMEM((128, total), BF),
        ],
        compiler_params=pltpu.CompilerParams(vmem_limit_bytes=(32 if total <= 1024 else 58) << 20),
        cost_estimate=LIGHT,
        name="attend_forward",
    )(queries, key_code, query_codes, *key_values)

def backward_kernel(
    chunk, parts, q_ref, code_ref, codes_ref, att_ref, branch_ref, lse_ref, rot_ref, o0, o1, o2, o3, *refs
):
    kv_refs = refs[:parts]
    dq_ref, dkv_ref, grad_ref, bias, keys, values, kt_ref, delta, dk_acc, dv_acc = refs[parts:]
    total = code_ref.shape[0]
    rows = q_ref.shape[0]
    width = q_ref.shape[1]
    heads = width // HD
    fill_turned(kt_ref, kv_refs, 0)
    fill_bias(bias, code_ref, codes_ref)
    fill_padded(keys, kv_refs, 0)
    fill_padded(values, kv_refs, 128)
    block = o0.shape[1]
    grad = jnp.zeros((rows, width), F32)
    for r, piece in enumerate((o0, o1, o2, o3)):
        grad += dot_nt(branch_ref[:, r * block : (r + 1) * block], piece[...])
    grad_ref[...] = grad.astype(BF)
    owner = lax.broadcasted_iota(jnp.int32, (heads, width), 1) // HD
    member = jnp.where(owner == lax.broadcasted_iota(jnp.int32, (heads, width), 0), 1.0, 0.0)
    product = att_ref[...].astype(F32) * grad_ref[...].astype(F32)
    delta[...] = lax.dot_general(member, product, (((1,), (1,)), ((), ())), precision=lax.Precision.HIGHEST, preferred_element_type=F32)
    dk_acc[...] = jnp.zeros_like(dk_acc)
    dv_acc[...] = jnp.zeros_like(dv_acc)
    half = HD // 2

    def pair_step(pair, unused):
        group = pair // 2
        lanes = pl.ds(pl.multiple_of(pair * 128, 128), 128)
        q_pair = q_ref[:, lanes]
        g_pair = grad_ref[:, lanes]
        turned = []
        for side in range(2):
            head = pl.ds(pair * 2 + side, 1)
            lse = lse_ref[head, :]
            dlt = delta[head, :]
            def chunk_step(part, acc):
                at = pl.ds(pl.multiple_of(part * chunk, chunk), chunk)
                scores = dot_nt(keys[group, side, at, :], q_pair) + bias[at, :]
                probs = jnp.exp(scores - lse)
                dprobs = dot_nt(values[group, side, at, :], g_pair)
                dscores = (probs * (dprobs - dlt)).astype(BF)
                dv_acc[group, side, at, :] += dot_nn(probs.astype(BF), g_pair)
                dk_acc[group, side, at, :] += dot_nn(dscores, q_pair)
                kt = kt_ref[pl.ds(pl.multiple_of(group * HD, HD), HD), at]
                return acc + dot_nn(kt, dscores)
            acc = jnp.zeros((HD, rows), F32)
            if total == chunk:
                acc = chunk_step(0, acc)
            else:
                acc = lax.fori_loop(0, total // chunk, chunk_step, acc)
            acc = acc * (1.0 / HD)
            first, second = acc[:half], acc[half:]
            cosine, sine = rot_ref[:half, :], rot_ref[half:, :]
            turned.append(first * cosine + second * sine)
            turned.append(second * cosine - first * sine)
        dq_ref[:, lanes] = jnp.concatenate(turned, axis=0).T.astype(BF)
        return unused

    lax.fori_loop(0, width // 128, pair_step, 0)
    lane = lax.broadcasted_iota(jnp.int32, (total, 128), 1)
    for which, acc in ((0, dk_acc), (1, dv_acc)):
        zero = acc[0, 0] + pltpu.roll(acc[0, 1], HD, 1)
        one = pltpu.roll(acc[1, 0], HD, 1) + acc[1, 1]
        dkv_ref[:, which * 128 : (which + 1) * 128] = jnp.where(lane < HD, zero, one)

def attend_backward(
    queries, key_values, key_code, query_codes, attended, grad_branch, lse, turn, out_pieces
):
    rows, width = queries.shape
    total = key_code.shape[0]
    chunk = min(total, 1024)
    return pl.pallas_call(
        functools.partial(backward_kernel, chunk, len(key_values)),
        out_shape=(jax.ShapeDtypeStruct((rows, width), BF), jax.ShapeDtypeStruct((total, 256), F32)),
        scratch_shapes=[
            pltpu.VMEM((rows, width), BF),
            pltpu.VMEM((total, rows), F32),
            pltpu.VMEM((2, 2, total, 128), BF),
            pltpu.VMEM((2, 2, total, 128), BF),
            pltpu.VMEM((128, total), BF),
            pltpu.VMEM((width // HD, rows), F32),
            pltpu.VMEM((2, 2, total, 128), F32),
            pltpu.VMEM((2, 2, total, 128), F32),
        ],
        compiler_params=pltpu.CompilerParams(vmem_limit_bytes=(32 if total <= 1024 else 58) << 20),
        cost_estimate=LIGHT,
        name="attend_backward",
    )(queries, key_code, query_codes, attended, grad_branch, lse, turn, *out_pieces, *key_values)


def out_kernel(attended_ref, o0, o1, o2, o3, branch_ref):
    block = o0.shape[1]
    for r, piece in enumerate((o0, o1, o2, o3)):
        branch_ref[:, r * block : (r + 1) * block] = dot_nn(attended_ref[...], piece[...]).astype(BF)


def out_project(attended, out_pieces):
    return pl.pallas_call(
        out_kernel,
        out_shape=jax.ShapeDtypeStruct((attended.shape[0], 4 * out_pieces[0].shape[1]), BF),
        compiler_params=pltpu.CompilerParams(vmem_limit_bytes=60 << 20),
        cost_estimate=LIGHT,
        name="out_project",
    )(attended, *out_pieces)


def rows_at(index, size):
    return pl.ds(pl.multiple_of(index * size, size), size)


def half_turn(block):
    lane = lax.broadcasted_iota(jnp.int32, block.shape, 1)
    return jnp.where(lane % HD < HD // 2, pltpu.roll(block, 128 - HD // 2, 1), pltpu.roll(block, HD // 2, 1))


def project_kv_kernel(x_ref, scale_ref, cos_ref, sin_ref, p0, p1, p2, p3, normed_ref, kv_ref):
    block = x_ref.shape[1] // 4
    total = jnp.zeros(kv_ref.shape, F32)
    for r, piece in enumerate((p0, p1, p2, p3)):
        lanes = slice(r * block, (r + 1) * block)
        rows = block // piece.shape[1]
        gain = jnp.concatenate([piece[block + i : block + i + 1, :] for i in range(rows)], axis=1)
        low = (x_ref[:, lanes].astype(F32) * scale_ref[...] * gain.astype(F32)).astype(BF)
        normed_ref[:, lanes] = low
        total += dot_nn(low, piece[:block, :])
    keys = total[:, :128]
    kv_ref[:, :128] = (keys * cos_ref[...] + half_turn(keys) * sin_ref[...]).astype(BF)
    kv_ref[:, 128:] = total[:, 128:].astype(BF)


def project_kv(tokens, scale, cos_table, sin_table, pieces):
    rows, model = tokens.shape
    return pl.pallas_call(
        project_kv_kernel,
        out_shape=(
            jax.ShapeDtypeStruct((rows, model), BF),
            jax.ShapeDtypeStruct((rows, pieces[0].shape[1]), BF),
        ),
        compiler_params=pltpu.CompilerParams(vmem_limit_bytes=24 << 20),
        cost_estimate=LIGHT,
        name="project_kv",
    )(tokens, scale, cos_table, sin_table, *pieces)


def project_q_kernel(normed_ref, cos_ref, sin_ref, p0, p1, p2, p3, q_ref):
    block = p0.shape[0]
    total = jnp.zeros(q_ref.shape, F32)
    for r, piece in enumerate((p0, p1, p2, p3)):
        total += dot_nn(normed_ref[:, r * block : (r + 1) * block], piece[...])
    for at in range(0, q_ref.shape[1], 128):
        part = total[:, at : at + 128]
        part = part * cos_ref[...] + half_turn(part) * sin_ref[...]
        q_ref[:, at : at + 128] = part.astype(BF) * jnp.asarray(ATTN_SCALE, BF)


def project_q(normed, cos_table, sin_table, pieces):
    return pl.pallas_call(
        project_q_kernel,
        out_shape=jax.ShapeDtypeStruct((normed.shape[0], pieces[0].shape[1]), BF),
        compiler_params=pltpu.CompilerParams(vmem_limit_bytes=24 << 20),
        cost_estimate=LIGHT,
        name="project_q",
    )(normed, cos_table, sin_table, *pieces)


def mlp_kernel(halves, index_ref, x_ref, branch_ref, gain_ref, g_ref, *refs):
    count = 6 if halves else 4
    given, downs = (refs[:count], refs[count : 2 * count]), refs[2 * count : 2 * count + 4]
    h_ref, hidden_ref, dgate_ref, dup_ref, dh_ref, acc, joined = refs[2 * count + 4 :]
    step = pl.program_id(0)
    block = h_ref.shape[1] // 4

    @pl.when(step == 0)
    def _():
        height = 128

        def norm(i, unused):
            at = rows_at(i, height)
            middle = x_ref[at, :].astype(F32) + RESIDUAL * branch_ref[at, :].astype(F32)
            square = jnp.mean(middle * middle, axis=1, keepdims=True)
            h_ref[at, :] = (middle * lax.rsqrt(square + EPSILON) * gain_ref[...]).astype(BF)
            return unused

        lax.fori_loop(0, h_ref.shape[0] // height, norm, 0)

    sides = []
    for which, pieces in enumerate(given):
        if halves:
            half = block // 2
            first = pl.multiple_of(index_ref[0] * half, half)
            second = pl.multiple_of((1 - index_ref[0]) * half, half)
            for far in range(2):
                joined[which, far, pl.ds(first, half), :] = pieces[3 * far + 1][...]
                joined[which, far, pl.ds(second, half), :] = pieces[3 * far + 2][...]
            pieces = (pieces[0], joined.at[which, 0], pieces[3], joined.at[which, 1])
        sides.append(pieces)
    gates, ups = sides
    gate = up = dhid = None
    for r in range(4):
        lanes = slice(r * block, (r + 1) * block)
        h = h_ref[:, lanes]
        terms = (
            dot_nn(h, gates[r][...]),
            dot_nn(h, ups[r][...]),
            dot_nt(g_ref[:, lanes], downs[r][...]),
        )
        gate, up, dhid = terms if r == 0 else (gate + terms[0], up + terms[1], dhid + terms[2])
    sigma = jax.nn.sigmoid(gate)
    active = gate * sigma
    hidden_ref[...] = (active * up).astype(BF)
    dgate = (dhid * up * sigma * (1.0 + gate * (1.0 - sigma))).astype(BF)
    dup = (dhid * active).astype(BF)
    dgate_ref[...] = dgate
    dup_ref[...] = dup
    for r in range(4):
        lanes = slice(r * block, (r + 1) * block)
        term = dot_nt(dgate, gates[r][...]) + dot_nt(dup, ups[r][...])

        @pl.when(step == 0)
        def _():
            acc[:, lanes] = term

        @pl.when(step != 0)
        def _():
            acc[:, lanes] += term

    @pl.when(step == pl.num_programs(0) - 1)
    def _():
        dh_ref[...] = acc[...].astype(BF)


def mlp(tokens, branch, gain, grad, index, gates, ups, downs):
    rows, model = tokens.shape
    hidden = downs[0].shape[0]
    tile = 512
    whole = pl.BlockSpec((rows, model), lambda j, s: (0, 0))
    wide = [pl.BlockSpec((size, tile), lambda j, s, at=at: (at, j)) for unused, size, at in gates + ups]
    tall = pl.BlockSpec((tile, downs[0].shape[1]), lambda j, s: (j, 0))
    out = pl.BlockSpec((rows, tile), lambda j, s: (0, j))
    return pl.pallas_call(
        functools.partial(mlp_kernel, len(gates) > 4),
        grid_spec=pltpu.PrefetchScalarGridSpec(
            num_scalar_prefetch=1,
            grid=(hidden // tile,),
            in_specs=[whole, whole, pl.BlockSpec((1, model), lambda j, s: (0, 0)), whole]
            + wide
            + [tall] * 4,
            out_specs=[whole] + [out] * 3 + [whole],
            scratch_shapes=[
                pltpu.VMEM((rows, model), F32),
                pltpu.VMEM((2, 2, model // 4, tile), BF),
            ],
        ),
        out_shape=[jax.ShapeDtypeStruct((rows, model), BF)]
        + [jax.ShapeDtypeStruct((rows, hidden), BF)] * 3
        + [jax.ShapeDtypeStruct((rows, model), BF)],
        compiler_params=pltpu.CompilerParams(vmem_limit_bytes=60 << 20),
        cost_estimate=LIGHT,
        name="mlp",
    )(index, tokens, branch, gain[None], grad, *[v[0] for v in gates + ups], *downs)


def entry_kernel(dq_ref, own_ref, got_ref, cos_ref, sin_ref, *refs):
    queries, keys, (low_ref, dh_ref) = refs[:4], refs[4:8], refs[8:]
    block = dh_ref.shape[1] // 4
    width_q = dq_ref.shape[1]
    low_ref[:, :width_q] = dq_ref[...]
    sums = own_ref[...] + got_ref[...].astype(F32)
    dk = sums[:, :128]
    low_ref[:, width_q : width_q + 128] = (dk * cos_ref[...] - half_turn(dk) * sin_ref[...]).astype(BF)
    low_ref[:, width_q + 128 :] = sums[:, 128:].astype(BF)
    low = low_ref[:, width_q:]
    for r in range(4):
        term = dot_nt(dq_ref[...], queries[r][...]) + dot_nt(low, keys[r][:block, :])
        dh_ref[:, r * block : (r + 1) * block] = term.astype(BF)


def entry_grad(dq_low, own, got, cos_table, sin_table, query_pieces, key_pieces):
    rows, width_q = dq_low.shape
    block = query_pieces[0].shape[0]
    return pl.pallas_call(
        entry_kernel,
        out_shape=(
            jax.ShapeDtypeStruct((rows, width_q + key_pieces[0].shape[1]), BF),
            jax.ShapeDtypeStruct((rows, 4 * block), BF),
        ),
        compiler_params=pltpu.CompilerParams(vmem_limit_bytes=60 << 20),
        cost_estimate=LIGHT,
        name="entry_grad",
    )(dq_low, own, got, cos_table, sin_table, *query_pieces, *key_pieces)


def outer_kernel(n_adds, a_ref, b_ref, *refs):
    total = lax.dot_general(
        a_ref[...], b_ref[...], (((0,), (0,)), ((), ())), preferred_element_type=F32
    )
    for add in refs[:n_adds]:
        total += add[...].astype(F32)
    refs[n_adds][...] = total.astype(BF)


def outer(left, right, left_blocks, right_blocks, adds, name):
    rows = left.shape[0]
    size_m, size_n = left.shape[1] // 4, right.shape[1] // 4
    first_m, count_m = left_blocks
    first_n, count_n = right_blocks
    cut_rows = count_m < 4
    wide = size_n * count_n
    in_specs = [
        pl.BlockSpec((rows, size_m), lambda i: (0, first_m + i)),
        pl.BlockSpec((rows, wide), lambda i: (0, first_n // count_n)),
    ]
    for array, first in adds:
        if cut_rows:
            in_specs.append(pl.BlockSpec((size_m, wide), lambda i, first=first: (first + i, 0)))
        else:
            in_specs.append(pl.BlockSpec((size_m, wide), lambda i, first=first: (i, first)))
    return pl.pallas_call(
        functools.partial(outer_kernel, len(adds)),
        grid=(count_m,),
        in_specs=in_specs,
        out_specs=pl.BlockSpec((size_m, wide), lambda i: (i, 0)),
        out_shape=jax.ShapeDtypeStruct((size_m * count_m, wide), BF),
        compiler_params=pltpu.CompilerParams(vmem_limit_bytes=32 << 20),
        cost_estimate=LIGHT,
        name=name,
    )(left, right, *[array for array, unused in adds])


def lift_kernel(hidden_ref, d0, d1, d2, d3, out_ref, acc):
    step = pl.program_id(0)
    block = d0.shape[1]
    for r, piece in enumerate((d0, d1, d2, d3)):
        lanes = slice(r * block, (r + 1) * block)
        term = dot_nn(hidden_ref[...], piece[...])

        @pl.when(step == 0)
        def _():
            acc[:, lanes] = term

        @pl.when(step != 0)
        def _():
            acc[:, lanes] += term

    @pl.when(step == pl.num_programs(0) - 1)
    def _():
        out_ref[...] = acc[...].astype(BF)


def lift(hidden, downs):
    rows, width = hidden.shape
    block = downs[0].shape[1]
    tile = 512
    return pl.pallas_call(
        lift_kernel,
        grid=(width // tile,),
        in_specs=[pl.BlockSpec((rows, tile), lambda j: (0, j))]
        + [pl.BlockSpec((tile, block), lambda j: (j, 0))] * 4,
        out_specs=pl.BlockSpec((rows, 4 * block), lambda j: (0, 0)),
        out_shape=jax.ShapeDtypeStruct((rows, 4 * block), BF),
        scratch_shapes=[pltpu.VMEM((rows, 4 * block), F32)],
        compiler_params=pltpu.CompilerParams(vmem_limit_bytes=32 << 20),
        cost_estimate=LIGHT,
        name="lift",
    )(hidden, *downs)


def entry_outer_kernel(n_adds, attended_ref, branch_ref, normed_ref, low_ref, *refs):
    out_ref = refs[n_adds]
    width = attended_ref.shape[1]
    head = lax.dot_general(
        attended_ref[...], branch_ref[...], (((0,), (0,)), ((), ())), preferred_element_type=F32
    )
    tail = lax.dot_general(
        normed_ref[...], low_ref[...], (((0,), (0,)), ((), ())), preferred_element_type=F32
    )
    for add in refs[:n_adds]:
        head += add[:, : head.shape[1]].astype(F32)
        tail += add[:, head.shape[1] :].astype(F32)
    out_ref[:, : head.shape[1]] = head.astype(BF)
    out_ref[:, head.shape[1] :] = tail.astype(BF)


def entry_outer(attended, branch, normed, low, first, count, adds):
    rows, heads = attended.shape
    block = branch.shape[1] // 4
    width = block + low.shape[1]
    column = pl.BlockSpec((rows, block), lambda i: (0, first + i))
    in_specs = [
        pl.BlockSpec((rows, heads), lambda i: (0, 0)),
        column,
        column,
        pl.BlockSpec(low.shape, lambda i: (0, 0)),
    ]
    for array, at in adds:
        in_specs.append(pl.BlockSpec((block, width), lambda i, at=at: (at + i, 0)))
    return pl.pallas_call(
        functools.partial(entry_outer_kernel, len(adds)),
        grid=(count,),
        in_specs=in_specs,
        out_specs=pl.BlockSpec((block, width), lambda i: (i, 0)),
        out_shape=jax.ShapeDtypeStruct((block * count, width), BF),
        compiler_params=pltpu.CompilerParams(vmem_limit_bytes=24 << 20),
        cost_estimate=LIGHT,
        name="entry_outer",
    )(attended, branch, normed, low, *[array for array, unused in adds])


def exit_kernel(index_ref, middle_ref, dh_ref, x_ref, gain_ref, out_ref):
    x = x_ref[...].astype(F32)
    scale = lax.rsqrt(jnp.mean(x * x, axis=1, keepdims=True) + EPSILON)
    weighted = gain_ref[...] * dh_ref[...].astype(F32)
    inner = jnp.mean(weighted * x, axis=1, keepdims=True)
    total = middle_ref[...] + scale * weighted - x * (scale * scale * scale * inner)
    block = x.shape[1] // 4
    for k, owner in enumerate(OWNERS):
        place = pl.multiple_of((index_ref[0] ^ owner) * block, block)
        out_ref[:, pl.ds(place, block)] = total[:, k * block : (k + 1) * block].astype(BF)


def exit_grad(index, grad_middle, grad, tokens, gain):
    rows, model = tokens.shape
    height = 128
    part = pl.BlockSpec((height, model), lambda i, s: (i, 0))
    return pl.pallas_call(
        exit_kernel,
        grid_spec=pltpu.PrefetchScalarGridSpec(
            num_scalar_prefetch=1,
            grid=(rows // height,),
            in_specs=[part, part, part, pl.BlockSpec((1, model), lambda i, s: (0, 0))],
            out_specs=part,
        ),
        out_shape=jax.ShapeDtypeStruct((rows, model), BF),
        compiler_params=pltpu.CompilerParams(vmem_limit_bytes=60 << 20),
        cost_estimate=LIGHT,
        name="exit_grad",
    )(index, grad_middle, grad, tokens, gain[None])


def after(value, *others):
    if not others:
        return value
    return lax.optimization_barrier((value, *others))[0]


def sealed(step, *values):
    skipped = lambda *v: jax.tree.map(lambda a: jnp.zeros(a.shape, a.dtype), jax.eval_shape(step, *v))
    return lax.cond(lax.optimization_barrier(jnp.asarray(True)), step, skipped, *values)


def swap_core(value):
    return lax.ppermute(value, "dp", [(i, i ^ 1) for i in range(4)])


def swap_x(value):
    return lax.ppermute(value, "dp", [(i, i ^ 2) for i in range(4)])


def swap_both(value):
    return lax.ppermute(value, "dp", [(i, i ^ 3) for i in range(4)])


def swap_ctx(value):
    return lax.ppermute(value, "ctx", [(0, 1), (1, 0)])


def two_ctx():
    return lax.axis_size("ctx") == 2


def sum_ctx(total):
    low = total.astype(BF)
    if two_ctx():
        return low.astype(F32) + swap_ctx(low).astype(F32)
    return lax.psum(low, "ctx").astype(F32)


def far_halves(one, two):
    if not two_ctx():
        return jnp.concatenate([one, two])
    half = one.shape[0] // 2
    at = lax.axis_index("ctx") * half
    return jnp.concatenate([lax.dynamic_slice_in_dim(v, at, half) for v in (one, two)])


def psum_tensor(value):
    return lax.psum(value, "tensor")


def sum_everywhere(gains):
    gains = gains + swap_ctx(gains) if two_ctx() else lax.psum(gains, "ctx")
    near, far, other, both = split4(gains, 1)
    total = near + swap_x(far)
    total = total + swap_core(after(other, total))
    total = total + swap_both(after(both, total))
    if lax.axis_size("tensor") != 4:
        return lax.psum(total, "tensor")
    for bit in (1, 2):
        total = total + lax.ppermute(total, "tensor", [(i, i ^ bit) for i in range(4)])
    return total


def swap_bits(index):
    return ((index & 1) << 1) | (index >> 1)


def take_blocks(value, indices):
    size = value.shape[1] // 4
    return jnp.concatenate(
        [lax.dynamic_slice_in_dim(value, i * size, size, 1) for i in indices], axis=1
    )


OWNERS = (0, 2, 1, 3)


def relative(value):
    mine = lax.axis_index("dp")
    return take_blocks(value, [mine ^ k for k in OWNERS])


def absolute(value):
    mine = lax.axis_index("dp")
    return take_blocks(value, [swap_bits(mine ^ k) for k in range(4)])


def split4(value, axis):
    size = value.shape[axis] // 4
    return [lax.slice_in_dim(value, r * size, (r + 1) * size, axis=axis) for r in range(4)]


def token_places(row_ids, order_row, seen_row, prompt_len, block_rows, cont_len):
    block_total = order_row.shape[0]
    block_pick = (row_ids // block_rows)[:, None] == jnp.arange(block_total, dtype=jnp.int32)[
        None, :
    ]
    chosen = jnp.sum(jnp.where(block_pick, order_row[None, :], 0), axis=1)
    global_ids = chosen * block_rows + row_ids % block_rows
    in_prompt = global_ids < prompt_len
    segment = jnp.where(in_prompt, 0, 1 + (global_ids - prompt_len) // cont_len)
    cont_count = seen_row.shape[0]
    which_cont = (segment - 1)[:, None] == jnp.arange(cont_count, dtype=jnp.int32)[None, :]
    limit = jnp.sum(jnp.where(which_cont, seen_row[None, :], 0), axis=1)
    places = jnp.where(in_prompt, global_ids, limit + (global_ids - prompt_len) % cont_len)
    return (segment, places, limit)


def norm_scale(values):
    return lax.rsqrt(jnp.mean(values * values, axis=-1, keepdims=True) + EPSILON)


def norm_back(values, scale, gain, grad):
    weighted = gain * grad
    inner = jnp.mean(weighted * values, axis=-1, keepdims=True)
    return scale * weighted - values * (scale * scale * scale) * inner


def combine(low, peer):
    if two_ctx():
        return low.astype(F32) + peer.astype(F32)
    return peer.astype(F32)


class BlockSum:
    def __init__(self, term):
        self.term = term

    def begin(self):
        other = swap_core(self.term(2, 2, ()))
        return other, self.term(1, 1, ((other, 1),))

    def cross(self, begun, *wait):
        self.other, self.sent = begun
        self.got = swap_x(after(self.sent, *wait))
        return self

    def joined(self, other, got):
        self.other, self.got = other, got
        return self

    def fold(self, *wait):
        self.low = self.term(0, 1, ((self.other, 0), (after(self.got, *wait), 0)))
        return self

    def swap(self, *wait):
        low = after(self.low, *wait)
        self.peer = swap_ctx(low) if two_ctx() else lax.psum(low, "ctx")
        return self

    def result(self):
        return combine(self.low, self.peer)


def outer_sum(left, right, cut_left, name):
    def term(k, n, adds):
        cut, whole = (k, n), (0, 4)
        if cut_left:
            return outer(left, right, cut, whole, adds, name)
        return outer(left, right, whole, cut, adds, name)

    return BlockSum(term)


def shards(
    tokens,
    cotangent,
    first_gain,
    query_weight,
    key_weight,
    value_weight,
    output_weight,
    second_gain,
    gate_weight,
    up_weight,
    down_weight,
    block_order,
    prefix_seen,
):
    ctx_size = lax.axis_size("ctx")
    local_rows = tokens.shape[0]
    group_rows = local_rows * ctx_size
    offset = lax.axis_index("ctx") * local_rows
    width_q = query_weight.shape[1]
    width_kv = key_weight.shape[1]
    block_d = query_weight.shape[0]

    query_far = swap_x(query_weight)
    query_near = swap_core(query_weight)
    gain_rows = jnp.stack([first_gain, second_gain]).reshape(-1, 2 * width_kv)
    kv_shard = jnp.concatenate(
        [
            jnp.concatenate([after(key_weight, query_near), value_weight], axis=1),
            jnp.pad(gain_rows, ((0, 32 - gain_rows.shape[0]), (0, 0))),
        ],
        axis=0,
    )
    kv_far = swap_x(kv_shard)
    kv_near = swap_core(kv_shard)
    out_far = swap_x(after(output_weight, kv_near))
    out_near = swap_core(after(output_weight, kv_near))
    wide_sent = after(far_halves(*(after(v, query_near) for v in (gate_weight, up_weight))), query_near)
    wide_got = swap_x(after(wide_sent, kv_far))

    tokens, block_order = (after(v, query_near) for v in (tokens, block_order))
    all_ids = jnp.arange(group_rows, dtype=jnp.int32)
    if two_ctx():
        all_ids = jnp.where(all_ids < local_rows, all_ids + offset, all_ids - offset)
    key_seg, key_pos, key_lim = token_places(
        all_ids, block_order[0], prefix_seen[0], group_rows // 2, local_rows // 2, CLEN
    )
    if two_ctx():
        query_seg, query_pos, query_lim = key_seg[:local_rows], key_pos[:local_rows], key_lim[:local_rows]
    else:
        query_seg = lax.dynamic_slice_in_dim(key_seg, offset, local_rows)
        query_pos = lax.dynamic_slice_in_dim(key_pos, offset, local_rows)
        query_lim = lax.dynamic_slice_in_dim(key_lim, offset, local_rows)
    key_code = (key_seg * SEGMENT_STEP + key_pos)[:, None]
    in_prompt = query_seg == 0
    below = jnp.where(in_prompt, query_pos + 1, query_lim)
    low_code = jnp.where(in_prompt, 1, query_seg * SEGMENT_STEP)
    high_code = jnp.where(in_prompt, 0, query_seg * SEGMENT_STEP + query_pos)
    query_codes = jnp.stack([below, low_code, high_code] + [below] * 5)
    half_size = HD // 2
    freq = ROPE_BASE ** (-(jnp.arange(half_size, dtype=F32) * 2.0) / HD)
    angle_t = freq[:, None] * query_pos.astype(F32)[None, :]
    turn = jnp.concatenate([jnp.cos(angle_t), jnp.sin(angle_t)], axis=0)
    cosine, sine = turn[:half_size].T, turn[half_size:].T
    cos_table = jnp.concatenate([cosine] * 4, axis=1)
    sin_table = jnp.concatenate([-sine, sine] * 2, axis=1)

    tokens = relative(tokens)
    inputs = tokens.astype(F32)
    scale_one = norm_scale(inputs)
    kv_pieces = [kv_shard, kv_far, kv_near, swap_core(kv_far)]
    gain_at = block_d + block_d // (2 * width_kv)
    gain_one, gain_two = (
        jnp.concatenate([p[i : i + gain_at - block_d].reshape(-1) for p in kv_pieces]).astype(F32)
        for i in (block_d, gain_at)
    )
    normed, key_value = project_kv(
        tokens, after(scale_one, wide_sent), cos_table, sin_table, kv_pieces
    )
    if two_ctx():
        other_kv = swap_ctx(key_value)
    else:
        other_kv = lax.all_gather(key_value, "ctx", axis=0, tiled=True)
    query_pieces = [query_weight, query_far, query_near, swap_core(query_far)]
    queries = project_q(normed, cos_table, sin_table, query_pieces)
    other_kv = after(other_kv, queries)
    key_values = (key_value, other_kv) if two_ctx() else (other_kv,)
    attended, log_total = attend_forward(queries, key_values, key_code, query_codes)
    out_far = after(out_far, queries, key_values[-1])
    out_pieces = [output_weight, out_far, out_near, swap_core(out_far)]
    branch = out_project(attended, out_pieces)
    grad_out = relative(after(cotangent, log_total)).astype(F32)
    grad_mlp = (RESIDUAL * grad_out).astype(BF)
    branch = psum_tensor(branch)

    def spread_wide(got, gate, up, down):
        gate_near = swap_core(gate)
        near = gate_near, swap_core(up), swap_core(after(got, gate_near)), swap_core(after(down, gate_near))
        return swap_ctx(got) if two_ctx() else got, *near

    def spread_last(*values):
        return tuple(swap_core(v) for v in values)

    down_far = swap_x(after(down_weight, log_total))
    wide_other, gate_near, up_near, last_got, down_near = sealed(
        spread_wide, after(wide_got, log_total), gate_weight, up_weight, down_weight
    )
    last_other, down_last = sealed(spread_last, wide_other, down_far)
    downs = [down_weight, down_far, down_near, down_last]
    half = block_d // 2 if two_ctx() else block_d
    far = (wide_got, wide_other) if two_ctx() else (wide_got,)
    last = (last_got, last_other) if two_ctx() else (last_got,)
    gates, ups = (
        [(own, block_d, 0), *[(v, half, at) for v in far], (near, block_d, 0), *[(v, half, at) for v in last]]
        for own, near, at in ((gate_weight, gate_near, 0), (up_weight, up_near, 1))
    )
    wait = down_last
    branch = after(branch, wait)
    normed_two, hidden, grad_gate, grad_up, grad_two = mlp(
        tokens, branch, gain_two, grad_mlp, lax.axis_index("ctx")[None], gates, ups, downs
    )
    two_part = grad_two
    grad_two = psum_tensor(grad_two)
    middle = inputs + RESIDUAL * after(branch, hidden).astype(F32)
    scale_two = norm_scale(middle)

    def begin(hidden, normed_two, grad_mlp, grad_gate, grad_up, *downs):
        down_sum = outer_sum(hidden, grad_mlp, False, "down_outer")
        down_sum.cross(down_sum.begin())
        gate_begun = outer_sum(normed_two, grad_gate, True, "gate_outer").begin()
        up_begun = outer_sum(normed_two, grad_up, True, "up_outer").begin()
        part = lift(hidden, downs)
        return down_sum.fold(gate_begun[1], up_begun[1], part).low, gate_begun, up_begun, part

    down_sum = BlockSum(None)
    down_sum.low, gate_begun, up_begun, mlp_part = sealed(
        begin, hidden, normed_two, grad_mlp, grad_gate, grad_up, *downs
    )
    down_sum.swap()
    gate_sum = outer_sum(normed_two, grad_gate, True, "gate_outer").cross(gate_begun)
    up_sum = outer_sum(normed_two, grad_up, True, "up_outer")
    grad_two = after(grad_two, down_sum.low)
    mlp_sum = psum_tensor(after(mlp_part, grad_two))
    up_sum.cross(up_begun, grad_two)
    grad_two = grad_two.astype(F32)

    grad_middle = grad_out + norm_back(middle, scale_two, gain_two, grad_two)
    grad_branch = (RESIDUAL * grad_middle).astype(BF)
    query_low, key_value_parts = attend_backward(
        queries,
        key_values,
        key_code,
        query_codes,
        attended,
        grad_branch,
        log_total,
        turn,
        out_pieces,
    )
    if two_ctx():
        own_part = key_value_parts[:local_rows]
        got_part = swap_ctx(key_value_parts[local_rows:].astype(BF))
    else:
        own_part = lax.psum_scatter(
            key_value_parts.astype(BF), "ctx", scatter_dimension=0, tiled=True
        ).astype(F32)
        got_part = jnp.zeros(own_part.shape, BF)
    qkv_low, grad_one = entry_grad(
        query_low, own_part, got_part, cos_table, sin_table, query_pieces, kv_pieces
    )
    gate_sum.fold(query_low)
    gate_sum.swap(got_part)

    def entry_term(attended, grad_branch, normed, qkv_low):
        return BlockSum(
            lambda k, n, adds: entry_outer(attended, grad_branch, normed, qkv_low, k, n, adds)
        )

    entry_inputs = (attended, grad_branch, normed, qkv_low)
    begun = sealed(lambda *v: entry_term(*v).begin(), *entry_inputs)
    entry_sum = entry_term(*entry_inputs).cross(begun, gate_sum.low)
    mlp_sum = after(mlp_sum, qkv_low, down_sum.peer, gate_sum.low, up_sum.fold(qkv_low).low, entry_sum.sent)
    gains = jnp.stack(
        [
            jnp.sum(grad_one.astype(F32) * inputs * scale_one, axis=0),
            jnp.sum(two_part.astype(F32) * middle * scale_two, axis=0),
        ]
    )
    grad_one = psum_tensor(after(grad_one, mlp_sum))


    up_sum.swap()

    def finish(gains, middle, mlp_sum, *values):
        gains = sum_everywhere(gains)
        entry_sum = entry_term(*values[:4]).joined(*values[4:6]).fold().swap()
        layer_out = absolute((middle + RESIDUAL * mlp_sum.astype(F32)).astype(BF))
        totals = (combine(*values[i : i + 2]) for i in (6, 8, 10))
        parts = (
            combine(entry_sum.low[:, at], entry_sum.peer[:, at])
            for at in (slice(0, block_d), slice(block_d, None))
        )
        return gains, layer_out, *totals, *parts

    gain_grad, layer_out, down_grad, gate_grad, up_grad, output_grad, qkv_grad = sealed(
        finish,
        gains,
        middle,
        mlp_sum,
        *entry_inputs,
        entry_sum.other,
        entry_sum.got,
        down_sum.low,
        down_sum.peer,
        gate_sum.low,
        gate_sum.peer,
        up_sum.low,
        up_sum.peer,
    )
    tokens_grad = exit_grad(
        lax.axis_index("dp")[None],
        grad_middle,
        after(grad_one, down_grad),
        tokens,
        gain_one,
    )
    return (
        layer_out,
        tokens_grad,
        gain_grad[0],
        qkv_grad[:, :width_q],
        qkv_grad[:, width_q : width_q + width_kv],
        qkv_grad[:, width_q + width_kv :],
        output_grad,
        gain_grad[1],
        gate_grad,
        up_grad,
        down_grad,
    )


def solution(mesh):
    return jax.shard_map(
        shards,
        mesh=mesh,
        in_specs=(
            P(("dp", "ctx"), None),
            P(("dp", "ctx"), None),
            P("dp"),
            P("dp", "tensor"),
            P("dp", "tensor"),
            P("dp", "tensor"),
            P("tensor", "dp"),
            P("dp"),
            P("dp", "tensor"),
            P("dp", "tensor"),
            P("tensor", "dp"),
            P("dp", None),
            P("dp", None),
        ),
        out_specs=(
            P(("dp", "ctx"), None),
            P(("dp", "ctx"), None),
            P("dp"),
            P("dp", "tensor"),
            P("dp", "tensor"),
            P("dp", "tensor"),
            P("tensor", "dp"),
            P("dp"),
            P("dp", "tensor"),
            P("dp", "tensor"),
            P("tensor", "dp"),
        ),
        check_vma=False,
    )
```

```python
import functools

import jax
import jax.numpy as jnp
from jax import lax
from jax.experimental import pallas as pl
from jax.experimental.pallas import tpu as pltpu
from jax.sharding import PartitionSpec as P

HD = 64
CLEN = 512

EPSILON = 1e-05
ROPE_BASE = 10000000.0
ATTN_SCALE = 0.015625
RESIDUAL = 0.22
NEGATIVE = -1e30
SEGMENT_STEP = 1 << 16
BF = jnp.bfloat16
F32 = jnp.float32
LIGHT = pl.CostEstimate(flops=1, bytes_accessed=1, transcendentals=0)


def dot_nt(a, b):
    return lax.dot_general(a, b, (((1,), (1,)), ((), ())), preferred_element_type=F32)

def dot_nn(a, b):
    return lax.dot_general(a, b, (((1,), (0,)), ((), ())), preferred_element_type=F32)

def fill_bias(bias, key_code, query_codes):
    code = key_code[...]
    below = code < query_codes[0:1, :]
    own = (code >= query_codes[1:2, :]) & (code <= query_codes[2:3, :])
    bias[...] = jnp.where(below | own, 0.0, NEGATIVE)

def fill_padded(padded, sources, lane0):
    block = jnp.concatenate([v[:, lane0 : lane0 + 2 * HD] for v in sources], axis=0)
    lane = lax.broadcasted_iota(jnp.int32, block.shape, 1)
    low = jnp.where(lane < HD, block, jnp.zeros_like(block))
    high = jnp.where(lane < HD, jnp.zeros_like(block), block)
    padded[0, 0] = low
    padded[0, 1] = pltpu.roll(low.astype(F32), HD, 1).astype(BF)
    padded[1, 0] = pltpu.roll(high.astype(F32), HD, 1).astype(BF)
    padded[1, 1] = high

def fill_turned(turned, sources, lane0):
    at = 0
    for v in sources:
        turned[:, at : at + v.shape[0]] = v[:, lane0 : lane0 + 2 * HD].astype(F32).T.astype(BF)
        at += v.shape[0]


def forward_kernel(chunk, parts, q_ref, code_ref, codes_ref, *refs):
    kv_refs = refs[:parts]
    out_ref, lse_ref, bias, keys, vt_ref = refs[parts:]
    total = code_ref.shape[0]
    rows = q_ref.shape[0]
    fill_turned(vt_ref, kv_refs, 2 * HD)
    fill_bias(bias, code_ref, codes_ref)
    fill_padded(keys, kv_refs, 0)

    def pair_step(pair, unused):
        group = pair // 2
        lanes = pl.ds(pl.multiple_of(pair * 128, 128), 128)
        q_pair = q_ref[:, lanes]
        mixed = []
        for side in range(2):
            def chunk_step(part, carry):
                top, norm, acc = carry
                at = pl.ds(pl.multiple_of(part * chunk, chunk), chunk)
                scores = dot_nt(keys[group, side, at, :], q_pair) + bias[at, :]
                new_top = jnp.maximum(top, jnp.max(scores, axis=0, keepdims=True))
                weights = jnp.exp(scores - new_top)
                shrink = jnp.exp(top - new_top)
                norm = norm * shrink + jnp.sum(weights, axis=0, keepdims=True)
                values = vt_ref[pl.ds(pl.multiple_of(group * HD, HD), HD), at]
                acc = acc * shrink + dot_nn(values, weights.astype(BF))
                return new_top, norm, acc

            carry = (jnp.full((1, rows), NEGATIVE, F32), jnp.zeros((1, rows), F32), jnp.zeros((HD, rows), F32))
            if total == chunk:
                carry = chunk_step(0, carry)
            else:
                carry = lax.fori_loop(0, total // chunk, chunk_step, carry)
            top, norm, acc = carry
            mixed.append(acc / norm)
            lse_ref[pl.ds(pair * 2 + side, 1), :] = top + jnp.log(norm)
        out_ref[:, lanes] = jnp.concatenate(mixed, axis=0).T.astype(BF)
        return unused

    lax.fori_loop(0, q_ref.shape[1] // 128, pair_step, 0)


def attend_forward(queries, key_values, key_code, query_codes):
    rows, width = queries.shape
    total = key_code.shape[0]
    chunk = min(total, 1024)
    return pl.pallas_call(
        functools.partial(forward_kernel, chunk, len(key_values)),
        out_shape=(
            jax.ShapeDtypeStruct((rows, width), BF),
            jax.ShapeDtypeStruct((width // HD, rows), F32),
        ),
        scratch_shapes=[
            pltpu.VMEM((total, rows), F32),
            pltpu.VMEM((2, 2, total, 128), BF),
            pltpu.VMEM((128, total), BF),
        ],
        compiler_params=pltpu.CompilerParams(vmem_limit_bytes=(32 if total <= 1024 else 58) << 20),
        cost_estimate=LIGHT,
        name="attend_forward",
    )(queries, key_code, query_codes, *key_values)

def backward_kernel(
    chunk, parts, q_ref, code_ref, codes_ref, att_ref, branch_ref, lse_ref, rot_ref, o0, o1, o2, o3, *refs
):
    kv_refs = refs[:parts]
    dq_ref, dkv_ref, grad_ref, bias, keys, values, kt_ref, delta, dk_acc, dv_acc = refs[parts:]
    total = code_ref.shape[0]
    rows = q_ref.shape[0]
    width = q_ref.shape[1]
    heads = width // HD
    fill_turned(kt_ref, kv_refs, 0)
    fill_bias(bias, code_ref, codes_ref)
    fill_padded(keys, kv_refs, 0)
    fill_padded(values, kv_refs, 128)
    block = o0.shape[1]
    grad = jnp.zeros((rows, width), F32)
    for r, piece in enumerate((o0, o1, o2, o3)):
        grad += dot_nt(branch_ref[:, r * block : (r + 1) * block], piece[...])
    grad_ref[...] = grad.astype(BF)
    owner = lax.broadcasted_iota(jnp.int32, (heads, width), 1) // HD
    member = jnp.where(owner == lax.broadcasted_iota(jnp.int32, (heads, width), 0), 1.0, 0.0)
    product = att_ref[...].astype(F32) * grad_ref[...].astype(F32)
    delta[...] = lax.dot_general(member, product, (((1,), (1,)), ((), ())), precision=lax.Precision.HIGHEST, preferred_element_type=F32)
    dk_acc[...] = jnp.zeros_like(dk_acc)
    dv_acc[...] = jnp.zeros_like(dv_acc)
    half = HD // 2

    def pair_step(pair, unused):
        group = pair // 2
        lanes = pl.ds(pl.multiple_of(pair * 128, 128), 128)
        q_pair = q_ref[:, lanes]
        g_pair = grad_ref[:, lanes]
        turned = []
        for side in range(2):
            head = pl.ds(pair * 2 + side, 1)
            lse = lse_ref[head, :]
            dlt = delta[head, :]
            def chunk_step(part, acc):
                at = pl.ds(pl.multiple_of(part * chunk, chunk), chunk)
                scores = dot_nt(keys[group, side, at, :], q_pair) + bias[at, :]
                probs = jnp.exp(scores - lse)
                dprobs = dot_nt(values[group, side, at, :], g_pair)
                dscores = (probs * (dprobs - dlt)).astype(BF)
                dv_acc[group, side, at, :] += dot_nn(probs.astype(BF), g_pair)
                dk_acc[group, side, at, :] += dot_nn(dscores, q_pair)
                kt = kt_ref[pl.ds(pl.multiple_of(group * HD, HD), HD), at]
                return acc + dot_nn(kt, dscores)
            acc = jnp.zeros((HD, rows), F32)
            if total == chunk:
                acc = chunk_step(0, acc)
            else:
                acc = lax.fori_loop(0, total // chunk, chunk_step, acc)
            acc = acc * (1.0 / HD)
            first, second = acc[:half], acc[half:]
            cosine, sine = rot_ref[:half, :], rot_ref[half:, :]
            turned.append(first * cosine + second * sine)
            turned.append(second * cosine - first * sine)
        dq_ref[:, lanes] = jnp.concatenate(turned, axis=0).T.astype(BF)
        return unused

    lax.fori_loop(0, width // 128, pair_step, 0)
    lane = lax.broadcasted_iota(jnp.int32, (total, 128), 1)
    for which, acc in ((0, dk_acc), (1, dv_acc)):
        zero = acc[0, 0] + pltpu.roll(acc[0, 1], HD, 1)
        one = pltpu.roll(acc[1, 0], HD, 1) + acc[1, 1]
        dkv_ref[:, which * 128 : (which + 1) * 128] = jnp.where(lane < HD, zero, one)

def attend_backward(
    queries, key_values, key_code, query_codes, attended, grad_branch, lse, turn, out_pieces
):
    rows, width = queries.shape
    total = key_code.shape[0]
    chunk = min(total, 1024)
    return pl.pallas_call(
        functools.partial(backward_kernel, chunk, len(key_values)),
        out_shape=(jax.ShapeDtypeStruct((rows, width), BF), jax.ShapeDtypeStruct((total, 256), F32)),
        scratch_shapes=[
            pltpu.VMEM((rows, width), BF),
            pltpu.VMEM((total, rows), F32),
            pltpu.VMEM((2, 2, total, 128), BF),
            pltpu.VMEM((2, 2, total, 128), BF),
            pltpu.VMEM((128, total), BF),
            pltpu.VMEM((width // HD, rows), F32),
            pltpu.VMEM((2, 2, total, 128), F32),
            pltpu.VMEM((2, 2, total, 128), F32),
        ],
        compiler_params=pltpu.CompilerParams(vmem_limit_bytes=(32 if total <= 1024 else 58) << 20),
        cost_estimate=LIGHT,
        name="attend_backward",
    )(queries, key_code, query_codes, attended, grad_branch, lse, turn, *out_pieces, *key_values)


def out_kernel(attended_ref, o0, o1, o2, o3, branch_ref):
    block = o0.shape[1]
    for r, piece in enumerate((o0, o1, o2, o3)):
        branch_ref[:, r * block : (r + 1) * block] = dot_nn(attended_ref[...], piece[...]).astype(BF)


def out_project(attended, out_pieces):
    return pl.pallas_call(
        out_kernel,
        out_shape=jax.ShapeDtypeStruct((attended.shape[0], 4 * out_pieces[0].shape[1]), BF),
        compiler_params=pltpu.CompilerParams(vmem_limit_bytes=60 << 20),
        cost_estimate=LIGHT,
        name="out_project",
    )(attended, *out_pieces)


def rows_at(index, size):
    return pl.ds(pl.multiple_of(index * size, size), size)


def half_turn(block):
    lane = lax.broadcasted_iota(jnp.int32, block.shape, 1)
    return jnp.where(lane % HD < HD // 2, pltpu.roll(block, 128 - HD // 2, 1), pltpu.roll(block, HD // 2, 1))


def project_kv_kernel(x_ref, scale_ref, cos_ref, sin_ref, p0, p1, p2, p3, normed_ref, kv_ref):
    block = x_ref.shape[1] // 4
    total = jnp.zeros(kv_ref.shape, F32)
    for r, piece in enumerate((p0, p1, p2, p3)):
        lanes = slice(r * block, (r + 1) * block)
        rows = block // piece.shape[1]
        gain = jnp.concatenate([piece[block + i : block + i + 1, :] for i in range(rows)], axis=1)
        low = (x_ref[:, lanes].astype(F32) * scale_ref[...] * gain.astype(F32)).astype(BF)
        normed_ref[:, lanes] = low
        total += dot_nn(low, piece[:block, :])
    keys = total[:, :128]
    kv_ref[:, :128] = (keys * cos_ref[...] + half_turn(keys) * sin_ref[...]).astype(BF)
    kv_ref[:, 128:] = total[:, 128:].astype(BF)


def project_kv(tokens, scale, cos_table, sin_table, pieces):
    rows, model = tokens.shape
    return pl.pallas_call(
        project_kv_kernel,
        out_shape=(
            jax.ShapeDtypeStruct((rows, model), BF),
            jax.ShapeDtypeStruct((rows, pieces[0].shape[1]), BF),
        ),
        compiler_params=pltpu.CompilerParams(vmem_limit_bytes=24 << 20),
        cost_estimate=LIGHT,
        name="project_kv",
    )(tokens, scale, cos_table, sin_table, *pieces)


def project_q_kernel(normed_ref, cos_ref, sin_ref, p0, p1, p2, p3, q_ref):
    block = p0.shape[0]
    total = jnp.zeros(q_ref.shape, F32)
    for r, piece in enumerate((p0, p1, p2, p3)):
        total += dot_nn(normed_ref[:, r * block : (r + 1) * block], piece[...])
    for at in range(0, q_ref.shape[1], 128):
        part = total[:, at : at + 128]
        part = part * cos_ref[...] + half_turn(part) * sin_ref[...]
        q_ref[:, at : at + 128] = part.astype(BF) * jnp.asarray(ATTN_SCALE, BF)


def project_q(normed, cos_table, sin_table, pieces):
    return pl.pallas_call(
        project_q_kernel,
        out_shape=jax.ShapeDtypeStruct((normed.shape[0], pieces[0].shape[1]), BF),
        compiler_params=pltpu.CompilerParams(vmem_limit_bytes=24 << 20),
        cost_estimate=LIGHT,
        name="project_q",
    )(normed, cos_table, sin_table, *pieces)


def early_kernel(g_ref, d0, d2, out_ref):
    block = d0.shape[1]
    out_ref[...] = dot_nt(g_ref[:, :block], d0[...]) + dot_nt(g_ref[:, 2 * block : 3 * block], d2[...])


def early_hidden(grad, own, near):
    rows, model = grad.shape
    hidden, block = own.shape
    tile = 512
    return pl.pallas_call(
        early_kernel,
        grid=(hidden // tile,),
        in_specs=[pl.BlockSpec((rows, model), lambda j: (0, 0))]
        + [pl.BlockSpec((tile, block), lambda j: (j, 0))] * 2,
        out_specs=pl.BlockSpec((rows, tile), lambda j: (0, j)),
        out_shape=jax.ShapeDtypeStruct((rows, hidden), F32),
        compiler_params=pltpu.CompilerParams(vmem_limit_bytes=60 << 20),
        cost_estimate=LIGHT,
        name="early_hidden",
    )(grad, own, near)


def mlp_kernel(halves, index_ref, x_ref, branch_ref, gain_ref, g_ref, early_ref, *refs):
    count = 6 if halves else 4
    given, downs = (refs[:count], refs[count : 2 * count]), refs[2 * count : 2 * count + 4]
    h_ref, hidden_ref, dgate_ref, dup_ref, dh_ref, acc, joined = refs[2 * count + 4 :]
    step = pl.program_id(0)
    block = h_ref.shape[1] // 4

    @pl.when(step == 0)
    def _():
        height = 128

        def norm(i, unused):
            at = rows_at(i, height)
            middle = x_ref[at, :].astype(F32) + RESIDUAL * branch_ref[at, :].astype(F32)
            square = jnp.mean(middle * middle, axis=1, keepdims=True)
            h_ref[at, :] = (middle * lax.rsqrt(square + EPSILON) * gain_ref[...]).astype(BF)
            return unused

        lax.fori_loop(0, h_ref.shape[0] // height, norm, 0, unroll=True)

    sides = []
    for which, pieces in enumerate(given):
        if halves:
            half = block // 2
            first = pl.multiple_of(index_ref[0] * half, half)
            second = pl.multiple_of((1 - index_ref[0]) * half, half)
            for far in range(2):
                joined[which, far, pl.ds(first, half), :] = pieces[3 * far + 1][...]
                joined[which, far, pl.ds(second, half), :] = pieces[3 * far + 2][...]
            pieces = (pieces[0], joined.at[which, 0], pieces[3], joined.at[which, 1])
        sides.append(pieces)
    gates, ups = sides
    gate = up = dhid = None
    for r in range(4):
        lanes = slice(r * block, (r + 1) * block)
        h = h_ref[:, lanes]
        terms = dot_nn(h, gates[r][...]), dot_nn(h, ups[r][...])
        gate, up = terms if r == 0 else (gate + terms[0], up + terms[1])
        if r == 0:
            dhid = early_ref[...]
        elif r != 2:
            dhid += dot_nt(g_ref[:, lanes], downs[r][...])
    sigma = jax.nn.sigmoid(gate)
    active = gate * sigma
    hidden_ref[...] = (active * up).astype(BF)
    dgate = (dhid * up * sigma * (1.0 + gate * (1.0 - sigma))).astype(BF)
    dup = (dhid * active).astype(BF)
    dgate_ref[...] = dgate
    dup_ref[...] = dup
    for r in range(4):
        lanes = slice(r * block, (r + 1) * block)
        term = dot_nt(dgate, gates[r][...]) + dot_nt(dup, ups[r][...])

        @pl.when(step == 0)
        def _():
            acc[:, lanes] = term

        @pl.when(step != 0)
        def _():
            acc[:, lanes] += term

    @pl.when(step == pl.num_programs(0) - 1)
    def _():
        dh_ref[...] = acc[...].astype(BF)


def mlp(tokens, branch, gain, grad, early, index, gates, ups, downs):
    rows, model = tokens.shape
    hidden = downs[0].shape[0]
    tile = 512
    whole = pl.BlockSpec((rows, model), lambda j, s: (0, 0))
    wide = [pl.BlockSpec((size, tile), lambda j, s, at=at: (at, j)) for unused, size, at in gates + ups]
    tall = pl.BlockSpec((tile, downs[0].shape[1]), lambda j, s: (j, 0))
    out = pl.BlockSpec((rows, tile), lambda j, s: (0, j))
    return pl.pallas_call(
        functools.partial(mlp_kernel, len(gates) > 4),
        grid_spec=pltpu.PrefetchScalarGridSpec(
            num_scalar_prefetch=1,
            grid=(hidden // tile,),
            in_specs=[whole, whole, pl.BlockSpec((1, model), lambda j, s: (0, 0)), whole, out]
            + wide
            + [tall] * 4,
            out_specs=[whole] + [out] * 3 + [whole],
            scratch_shapes=[
                pltpu.VMEM((rows, model), F32),
                pltpu.VMEM((2, 2, model // 4, tile), BF),
            ],
        ),
        out_shape=[jax.ShapeDtypeStruct((rows, model), BF)]
        + [jax.ShapeDtypeStruct((rows, hidden), BF)] * 3
        + [jax.ShapeDtypeStruct((rows, model), BF)],
        compiler_params=pltpu.CompilerParams(vmem_limit_bytes=60 << 20),
        cost_estimate=LIGHT,
        name="mlp",
    )(index, tokens, branch, gain[None], grad, early, *[v[0] for v in gates + ups], *downs)


def entry_kernel(dq_ref, own_ref, got_ref, cos_ref, sin_ref, *refs):
    queries, keys, (low_ref, dh_ref) = refs[:4], refs[4:8], refs[8:]
    block = dh_ref.shape[1] // 4
    width_q = dq_ref.shape[1]
    low_ref[:, :width_q] = dq_ref[...]
    sums = own_ref[...] + got_ref[...].astype(F32)
    dk = sums[:, :128]
    low_ref[:, width_q : width_q + 128] = (dk * cos_ref[...] - half_turn(dk) * sin_ref[...]).astype(BF)
    low_ref[:, width_q + 128 :] = sums[:, 128:].astype(BF)
    low = low_ref[:, width_q:]
    for r in range(4):
        term = dot_nt(dq_ref[...], queries[r][...]) + dot_nt(low, keys[r][:block, :])
        dh_ref[:, r * block : (r + 1) * block] = term.astype(BF)


def entry_grad(dq_low, own, got, cos_table, sin_table, query_pieces, key_pieces):
    rows, width_q = dq_low.shape
    block = query_pieces[0].shape[0]
    return pl.pallas_call(
        entry_kernel,
        out_shape=(
            jax.ShapeDtypeStruct((rows, width_q + key_pieces[0].shape[1]), BF),
            jax.ShapeDtypeStruct((rows, 4 * block), BF),
        ),
        compiler_params=pltpu.CompilerParams(vmem_limit_bytes=60 << 20),
        cost_estimate=LIGHT,
        name="entry_grad",
    )(dq_low, own, got, cos_table, sin_table, *query_pieces, *key_pieces)


def outer_kernel(n_adds, a_ref, b_ref, *refs):
    total = lax.dot_general(
        a_ref[...], b_ref[...], (((0,), (0,)), ((), ())), preferred_element_type=F32
    )
    for add in refs[:n_adds]:
        total += add[...].astype(F32)
    refs[n_adds][...] = total.astype(BF)


def outer(left, right, left_blocks, right_blocks, adds, name):
    rows = left.shape[0]
    size_m, size_n = left.shape[1] // 4, right.shape[1] // 4
    first_m, count_m = left_blocks
    first_n, count_n = right_blocks
    cut_rows = count_m < 4
    wide = size_n * count_n
    in_specs = [
        pl.BlockSpec((rows, size_m), lambda i: (0, first_m + i)),
        pl.BlockSpec((rows, wide), lambda i: (0, first_n // count_n)),
    ]
    for array, first in adds:
        if cut_rows:
            in_specs.append(pl.BlockSpec((size_m, wide), lambda i, first=first: (first + i, 0)))
        else:
            in_specs.append(pl.BlockSpec((size_m, wide), lambda i, first=first: (i, first)))
    return pl.pallas_call(
        functools.partial(outer_kernel, len(adds)),
        grid=(count_m,),
        in_specs=in_specs,
        out_specs=pl.BlockSpec((size_m, wide), lambda i: (i, 0)),
        out_shape=jax.ShapeDtypeStruct((size_m * count_m, wide), BF),
        compiler_params=pltpu.CompilerParams(vmem_limit_bytes=32 << 20),
        cost_estimate=LIGHT,
        name=name,
    )(left, right, *[array for array, unused in adds])


def lift_kernel(hidden_ref, d0, d1, d2, d3, out_ref, acc):
    step = pl.program_id(0)
    block = d0.shape[1]
    for r, piece in enumerate((d0, d1, d2, d3)):
        lanes = slice(r * block, (r + 1) * block)
        term = dot_nn(hidden_ref[...], piece[...])

        @pl.when(step == 0)
        def _():
            acc[:, lanes] = term

        @pl.when(step != 0)
        def _():
            acc[:, lanes] += term

    @pl.when(step == pl.num_programs(0) - 1)
    def _():
        out_ref[...] = acc[...].astype(BF)


def lift(hidden, downs):
    rows, width = hidden.shape
    block = downs[0].shape[1]
    tile = 512
    return pl.pallas_call(
        lift_kernel,
        grid=(width // tile,),
        in_specs=[pl.BlockSpec((rows, tile), lambda j: (0, j))]
        + [pl.BlockSpec((tile, block), lambda j: (j, 0))] * 4,
        out_specs=pl.BlockSpec((rows, 4 * block), lambda j: (0, 0)),
        out_shape=jax.ShapeDtypeStruct((rows, 4 * block), BF),
        scratch_shapes=[pltpu.VMEM((rows, 4 * block), F32)],
        compiler_params=pltpu.CompilerParams(vmem_limit_bytes=32 << 20),
        cost_estimate=LIGHT,
        name="lift",
    )(hidden, *downs)


def entry_outer_kernel(n_adds, attended_ref, branch_ref, normed_ref, low_ref, *refs):
    out_ref = refs[n_adds]
    width = attended_ref.shape[1]
    head = lax.dot_general(
        attended_ref[...], branch_ref[...], (((0,), (0,)), ((), ())), preferred_element_type=F32
    )
    tail = lax.dot_general(
        normed_ref[...], low_ref[...], (((0,), (0,)), ((), ())), preferred_element_type=F32
    )
    for add in refs[:n_adds]:
        head += add[:, : head.shape[1]].astype(F32)
        tail += add[:, head.shape[1] :].astype(F32)
    out_ref[:, : head.shape[1]] = head.astype(BF)
    out_ref[:, head.shape[1] :] = tail.astype(BF)


def entry_outer(attended, branch, normed, low, first, count, adds):
    rows, heads = attended.shape
    block = branch.shape[1] // 4
    width = block + low.shape[1]
    column = pl.BlockSpec((rows, block), lambda i: (0, first + i))
    in_specs = [
        pl.BlockSpec((rows, heads), lambda i: (0, 0)),
        column,
        column,
        pl.BlockSpec(low.shape, lambda i: (0, 0)),
    ]
    for array, at in adds:
        in_specs.append(pl.BlockSpec((block, width), lambda i, at=at: (at + i, 0)))
    return pl.pallas_call(
        functools.partial(entry_outer_kernel, len(adds)),
        grid=(count,),
        in_specs=in_specs,
        out_specs=pl.BlockSpec((block, width), lambda i: (i, 0)),
        out_shape=jax.ShapeDtypeStruct((block * count, width), BF),
        compiler_params=pltpu.CompilerParams(vmem_limit_bytes=24 << 20),
        cost_estimate=LIGHT,
        name="entry_outer",
    )(attended, branch, normed, low, *[array for array, unused in adds])


def exit_kernel(index_ref, middle_ref, dh_ref, x_ref, gain_ref, out_ref):
    x = x_ref[...].astype(F32)
    scale = lax.rsqrt(jnp.mean(x * x, axis=1, keepdims=True) + EPSILON)
    weighted = gain_ref[...] * dh_ref[...].astype(F32)
    inner = jnp.mean(weighted * x, axis=1, keepdims=True)
    total = middle_ref[...] + scale * weighted - x * (scale * scale * scale * inner)
    block = x.shape[1] // 4
    for k, owner in enumerate(OWNERS):
        place = pl.multiple_of((index_ref[0] ^ owner) * block, block)
        out_ref[:, pl.ds(place, block)] = total[:, k * block : (k + 1) * block].astype(BF)


def exit_grad(index, grad_middle, grad, tokens, gain):
    rows, model = tokens.shape
    height = 256
    part = pl.BlockSpec((height, model), lambda i, s: (i, 0))
    return pl.pallas_call(
        exit_kernel,
        grid_spec=pltpu.PrefetchScalarGridSpec(
            num_scalar_prefetch=1,
            grid=(rows // height,),
            in_specs=[part, part, part, pl.BlockSpec((1, model), lambda i, s: (0, 0))],
            out_specs=part,
        ),
        out_shape=jax.ShapeDtypeStruct((rows, model), BF),
        compiler_params=pltpu.CompilerParams(vmem_limit_bytes=60 << 20),
        cost_estimate=LIGHT,
        name="exit_grad",
    )(index, grad_middle, grad, tokens, gain[None])


def after(value, *others):
    if not others:
        return value
    return lax.optimization_barrier((value, *others))[0]


def sealed(step, *values):
    skipped = lambda *v: jax.tree.map(lambda a: jnp.zeros(a.shape, a.dtype), jax.eval_shape(step, *v))
    return lax.cond(lax.optimization_barrier(jnp.asarray(True)), step, skipped, *values)


def swap_core(value):
    return lax.ppermute(value, "dp", [(i, i ^ 1) for i in range(4)])


def swap_x(value):
    return lax.ppermute(value, "dp", [(i, i ^ 2) for i in range(4)])


def swap_both(value):
    return lax.ppermute(value, "dp", [(i, i ^ 3) for i in range(4)])


def swap_ctx(value):
    return lax.ppermute(value, "ctx", [(0, 1), (1, 0)])


def two_ctx():
    return lax.axis_size("ctx") == 2


def sum_ctx(total):
    low = total.astype(BF)
    if two_ctx():
        return low.astype(F32) + swap_ctx(low).astype(F32)
    return lax.psum(low, "ctx").astype(F32)


def far_halves(one, two):
    if not two_ctx():
        return jnp.concatenate([one, two])
    half = one.shape[0] // 2
    at = lax.axis_index("ctx") * half
    return jnp.concatenate([lax.dynamic_slice_in_dim(v, at, half) for v in (one, two)])


def psum_tensor(value):
    return lax.psum(value, "tensor")


def sum_everywhere(gains):
    gains = gains + swap_ctx(gains) if two_ctx() else lax.psum(gains, "ctx")
    near, far, other, both = split4(gains, 1)
    total = near + swap_x(far)
    total = total + swap_core(after(other, total))
    total = total + swap_both(after(both, total))
    if lax.axis_size("tensor") != 4:
        return lax.psum(total, "tensor")
    for bit in (1, 2):
        total = total + lax.ppermute(total, "tensor", [(i, i ^ bit) for i in range(4)])
    return total


def swap_bits(index):
    return ((index & 1) << 1) | (index >> 1)


def take_blocks(value, indices):
    size = value.shape[1] // 4
    return jnp.concatenate(
        [lax.dynamic_slice_in_dim(value, i * size, size, 1) for i in indices], axis=1
    )


OWNERS = (0, 2, 1, 3)


def relative(value):
    mine = lax.axis_index("dp")
    return take_blocks(value, [mine ^ k for k in OWNERS])


def absolute(value):
    mine = lax.axis_index("dp")
    return take_blocks(value, [swap_bits(mine ^ k) for k in range(4)])


def split4(value, axis):
    size = value.shape[axis] // 4
    return [lax.slice_in_dim(value, r * size, (r + 1) * size, axis=axis) for r in range(4)]


def token_places(row_ids, order_row, seen_row, prompt_len, block_rows, cont_len):
    block_total = order_row.shape[0]
    block_pick = (row_ids // block_rows)[:, None] == jnp.arange(block_total, dtype=jnp.int32)[
        None, :
    ]
    chosen = jnp.sum(jnp.where(block_pick, order_row[None, :], 0), axis=1)
    global_ids = chosen * block_rows + row_ids % block_rows
    in_prompt = global_ids < prompt_len
    segment = jnp.where(in_prompt, 0, 1 + (global_ids - prompt_len) // cont_len)
    cont_count = seen_row.shape[0]
    which_cont = (segment - 1)[:, None] == jnp.arange(cont_count, dtype=jnp.int32)[None, :]
    limit = jnp.sum(jnp.where(which_cont, seen_row[None, :], 0), axis=1)
    places = jnp.where(in_prompt, global_ids, limit + (global_ids - prompt_len) % cont_len)
    return (segment, places, limit)


def norm_scale(values):
    return lax.rsqrt(jnp.mean(values * values, axis=-1, keepdims=True) + EPSILON)


def norm_back(values, scale, gain, grad):
    weighted = gain * grad
    inner = jnp.mean(weighted * values, axis=-1, keepdims=True)
    return scale * weighted - values * (scale * scale * scale) * inner


def combine(low, peer):
    if two_ctx():
        return low.astype(F32) + peer.astype(F32)
    return peer.astype(F32)


class BlockSum:
    def __init__(self, term):
        self.term = term

    def begin(self):
        other = swap_core(self.term(2, 2, ()))
        return other, self.term(1, 1, ((other, 1),))

    def cross(self, begun, *wait):
        self.other, self.sent = begun
        self.got = swap_x(after(self.sent, *wait))
        return self

    def joined(self, other, got):
        self.other, self.got = other, got
        return self

    def fold(self, *wait):
        self.low = self.term(0, 1, ((self.other, 0), (after(self.got, *wait), 0)))
        return self

    def swap(self, *wait):
        low = after(self.low, *wait)
        self.peer = swap_ctx(low) if two_ctx() else lax.psum(low, "ctx")
        return self

    def result(self):
        return combine(self.low, self.peer)


def outer_sum(left, right, cut_left, name):
    def term(k, n, adds):
        cut, whole = (k, n), (0, 4)
        if cut_left:
            return outer(left, right, cut, whole, adds, name)
        return outer(left, right, whole, cut, adds, name)

    return BlockSum(term)


def shards(
    tokens,
    cotangent,
    first_gain,
    query_weight,
    key_weight,
    value_weight,
    output_weight,
    second_gain,
    gate_weight,
    up_weight,
    down_weight,
    block_order,
    prefix_seen,
):
    ctx_size = lax.axis_size("ctx")
    local_rows = tokens.shape[0]
    group_rows = local_rows * ctx_size
    offset = lax.axis_index("ctx") * local_rows
    width_q = query_weight.shape[1]
    width_kv = key_weight.shape[1]
    block_d = query_weight.shape[0]

    query_far = swap_x(query_weight)
    query_near = swap_core(query_weight)
    gain_rows = jnp.stack([first_gain, second_gain]).reshape(-1, 2 * width_kv)
    kv_shard = jnp.concatenate(
        [
            jnp.concatenate([after(key_weight, query_near), value_weight], axis=1),
            jnp.pad(gain_rows, ((0, 32 - gain_rows.shape[0]), (0, 0))),
        ],
        axis=0,
    )
    kv_far = swap_x(kv_shard)
    kv_near = swap_core(kv_shard)
    out_far = swap_x(after(output_weight, kv_near))
    out_near = swap_core(after(output_weight, kv_near))
    wide_sent = after(far_halves(*(after(v, query_near) for v in (gate_weight, up_weight))), query_near)
    wide_got = swap_x(after(wide_sent, kv_far))

    tokens, block_order = (after(v, query_near) for v in (tokens, block_order))
    all_ids = jnp.arange(group_rows, dtype=jnp.int32)
    if two_ctx():
        all_ids = jnp.where(all_ids < local_rows, all_ids + offset, all_ids - offset)
    key_seg, key_pos, key_lim = token_places(
        all_ids, block_order[0], prefix_seen[0], group_rows // 2, local_rows // 2, CLEN
    )
    if two_ctx():
        query_seg, query_pos, query_lim = key_seg[:local_rows], key_pos[:local_rows], key_lim[:local_rows]
    else:
        query_seg = lax.dynamic_slice_in_dim(key_seg, offset, local_rows)
        query_pos = lax.dynamic_slice_in_dim(key_pos, offset, local_rows)
        query_lim = lax.dynamic_slice_in_dim(key_lim, offset, local_rows)
    key_code = (key_seg * SEGMENT_STEP + key_pos)[:, None]
    in_prompt = query_seg == 0
    below = jnp.where(in_prompt, query_pos + 1, query_lim)
    low_code = jnp.where(in_prompt, 1, query_seg * SEGMENT_STEP)
    high_code = jnp.where(in_prompt, 0, query_seg * SEGMENT_STEP + query_pos)
    query_codes = jnp.stack([below, low_code, high_code] + [below] * 5)
    half_size = HD // 2
    freq = ROPE_BASE ** (-(jnp.arange(half_size, dtype=F32) * 2.0) / HD)
    angle_t = freq[:, None] * query_pos.astype(F32)[None, :]
    turn = jnp.concatenate([jnp.cos(angle_t), jnp.sin(angle_t)], axis=0)
    cosine, sine = turn[:half_size].T, turn[half_size:].T
    cos_table = jnp.concatenate([cosine] * 4, axis=1)
    sin_table = jnp.concatenate([-sine, sine] * 2, axis=1)

    tokens = relative(tokens)
    inputs = tokens.astype(F32)
    scale_one = norm_scale(inputs)
    kv_pieces = [kv_shard, kv_far, kv_near, swap_core(kv_far)]
    gain_at = block_d + block_d // (2 * width_kv)
    gain_one, gain_two = (
        jnp.concatenate([p[i : i + gain_at - block_d].reshape(-1) for p in kv_pieces]).astype(F32)
        for i in (block_d, gain_at)
    )
    normed, key_value = project_kv(
        tokens, after(scale_one, wide_sent), cos_table, sin_table, kv_pieces
    )
    if two_ctx():
        other_kv = swap_ctx(key_value)
    else:
        other_kv = lax.all_gather(key_value, "ctx", axis=0, tiled=True)
    query_pieces = [query_weight, query_far, query_near, swap_core(query_far)]
    queries = project_q(normed, cos_table, sin_table, query_pieces)
    other_kv = after(other_kv, queries)
    key_values = (key_value, other_kv) if two_ctx() else (other_kv,)
    attended, log_total = attend_forward(queries, key_values, key_code, query_codes)
    out_far = after(out_far, queries, key_values[-1])
    out_pieces = [output_weight, out_far, out_near, swap_core(out_far)]
    branch = out_project(attended, out_pieces)
    grad_out = relative(after(cotangent, log_total)).astype(F32)
    grad_mlp = (RESIDUAL * grad_out).astype(BF)
    branch = psum_tensor(branch)

    def spread_wide(got, gate, up, down, grad_mlp):
        gate_near = swap_core(gate)
        down_near = swap_core(after(down, gate_near))
        near = gate_near, swap_core(up), swap_core(after(got, gate_near)), down_near
        early = early_hidden(grad_mlp, down, down_near)
        return swap_ctx(got) if two_ctx() else got, *near, early

    def spread_last(*values):
        return tuple(swap_core(v) for v in values)

    down_far = swap_x(after(down_weight, log_total))
    wide_other, gate_near, up_near, last_got, down_near, early = sealed(
        spread_wide, after(wide_got, log_total), gate_weight, up_weight, down_weight, grad_mlp
    )
    last_other, down_last = sealed(spread_last, wide_other, down_far)
    downs = [down_weight, down_far, down_near, down_last]
    half = block_d // 2 if two_ctx() else block_d
    far = (wide_got, wide_other) if two_ctx() else (wide_got,)
    last = (last_got, last_other) if two_ctx() else (last_got,)
    gates, ups = (
        [(own, block_d, 0), *[(v, half, at) for v in far], (near, block_d, 0), *[(v, half, at) for v in last]]
        for own, near, at in ((gate_weight, gate_near, 0), (up_weight, up_near, 1))
    )
    wait = down_last
    branch = after(branch, wait)
    normed_two, hidden, grad_gate, grad_up, grad_two = mlp(
        tokens, branch, gain_two, grad_mlp, early, lax.axis_index("ctx")[None], gates, ups, downs
    )
    two_part = grad_two
    grad_two = psum_tensor(grad_two)
    middle = inputs + RESIDUAL * after(branch, hidden).astype(F32)
    scale_two = norm_scale(middle)

    def begin(hidden, normed_two, grad_mlp, grad_gate, grad_up, *downs):
        down_sum = outer_sum(hidden, grad_mlp, False, "down_outer")
        down_sum.cross(down_sum.begin())
        gate_begun = outer_sum(normed_two, grad_gate, True, "gate_outer").begin()
        up_begun = outer_sum(normed_two, grad_up, True, "up_outer").begin()
        part = lift(hidden, downs)
        return down_sum.fold(gate_begun[1], up_begun[1], part).low, gate_begun, up_begun, part

    down_sum = BlockSum(None)
    down_sum.low, gate_begun, up_begun, mlp_part = sealed(
        begin, hidden, normed_two, grad_mlp, grad_gate, grad_up, *downs
    )
    down_sum.swap()
    gate_sum = outer_sum(normed_two, grad_gate, True, "gate_outer").cross(gate_begun)
    up_sum = outer_sum(normed_two, grad_up, True, "up_outer")
    grad_two = after(grad_two, down_sum.low)
    mlp_sum = psum_tensor(after(mlp_part, grad_two))
    up_sum.cross(up_begun, grad_two)
    grad_two = grad_two.astype(F32)

    grad_middle = grad_out + norm_back(middle, scale_two, gain_two, grad_two)
    grad_branch = (RESIDUAL * grad_middle).astype(BF)
    query_low, key_value_parts = attend_backward(
        queries,
        key_values,
        key_code,
        query_codes,
        attended,
        grad_branch,
        log_total,
        turn,
        out_pieces,
    )
    if two_ctx():
        own_part = key_value_parts[:local_rows]
        got_part = swap_ctx(key_value_parts[local_rows:].astype(BF))
    else:
        own_part = lax.psum_scatter(
            key_value_parts.astype(BF), "ctx", scatter_dimension=0, tiled=True
        ).astype(F32)
        got_part = jnp.zeros(own_part.shape, BF)
    qkv_low, grad_one = entry_grad(
        query_low, own_part, got_part, cos_table, sin_table, query_pieces, kv_pieces
    )
    gate_sum.fold(query_low)
    gate_sum.swap(got_part)

    def entry_term(attended, grad_branch, normed, qkv_low):
        return BlockSum(
            lambda k, n, adds: entry_outer(attended, grad_branch, normed, qkv_low, k, n, adds)
        )

    entry_inputs = (attended, grad_branch, normed, qkv_low)
    begun = sealed(lambda *v: entry_term(*v).begin(), *entry_inputs)
    entry_sum = entry_term(*entry_inputs).cross(begun, gate_sum.low)
    mlp_sum = after(mlp_sum, qkv_low, down_sum.peer, gate_sum.low, up_sum.fold(qkv_low).low, entry_sum.sent)
    gains = jnp.stack(
        [
            jnp.sum(grad_one.astype(F32) * inputs * scale_one, axis=0),
            jnp.sum(two_part.astype(F32) * middle * scale_two, axis=0),
        ]
    )
    grad_one = psum_tensor(after(grad_one, mlp_sum))


    up_sum.swap()

    def finish(gains, middle, mlp_sum, *values):
        gains = sum_everywhere(gains)
        entry_sum = entry_term(*values[:4]).joined(*values[4:6]).fold().swap()
        layer_out = absolute((middle + RESIDUAL * mlp_sum.astype(F32)).astype(BF))
        totals = (combine(*values[i : i + 2]) for i in (6, 8, 10))
        parts = (
            combine(entry_sum.low[:, at], entry_sum.peer[:, at])
            for at in (slice(0, block_d), slice(block_d, None))
        )
        return gains, layer_out, *totals, *parts

    gain_grad, layer_out, down_grad, gate_grad, up_grad, output_grad, qkv_grad = sealed(
        finish,
        gains,
        middle,
        mlp_sum,
        *entry_inputs,
        entry_sum.other,
        entry_sum.got,
        down_sum.low,
        down_sum.peer,
        gate_sum.low,
        gate_sum.peer,
        up_sum.low,
        up_sum.peer,
    )
    tokens_grad = exit_grad(
        lax.axis_index("dp")[None],
        grad_middle,
        after(grad_one, down_grad),
        tokens,
        gain_one,
    )
    return (
        layer_out,
        tokens_grad,
        gain_grad[0],
        qkv_grad[:, :width_q],
        qkv_grad[:, width_q : width_q + width_kv],
        qkv_grad[:, width_q + width_kv :],
        output_grad,
        gain_grad[1],
        gate_grad,
        up_grad,
        down_grad,
    )


def solution(mesh):
    return jax.shard_map(
        shards,
        mesh=mesh,
        in_specs=(
            P(("dp", "ctx"), None),
            P(("dp", "ctx"), None),
            P("dp"),
            P("dp", "tensor"),
            P("dp", "tensor"),
            P("dp", "tensor"),
            P("tensor", "dp"),
            P("dp"),
            P("dp", "tensor"),
            P("dp", "tensor"),
            P("tensor", "dp"),
            P("dp", None),
            P("dp", None),
        ),
        out_specs=(
            P(("dp", "ctx"), None),
            P(("dp", "ctx"), None),
            P("dp"),
            P("dp", "tensor"),
            P("dp", "tensor"),
            P("dp", "tensor"),
            P("tensor", "dp"),
            P("dp"),
            P("dp", "tensor"),
            P("dp", "tensor"),
            P("tensor", "dp"),
        ),
        check_vma=False,
    )
```

```python
import functools

import jax
import jax.numpy as jnp
from jax import lax
from jax.experimental import pallas as pl
from jax.experimental.pallas import tpu as pltpu
from jax.sharding import PartitionSpec as P

HD = 64
CLEN = 512

EPSILON = 1e-05
ROPE_BASE = 10000000.0
ATTN_SCALE = 0.015625
RESIDUAL = 0.22
NEGATIVE = -1e30
SEGMENT_STEP = 1 << 16
BF = jnp.bfloat16
F32 = jnp.float32
LIGHT = pl.CostEstimate(flops=1, bytes_accessed=1, transcendentals=0)


def dot_nt(a, b):
    return lax.dot_general(a, b, (((1,), (1,)), ((), ())), preferred_element_type=F32)

def dot_nn(a, b):
    return lax.dot_general(a, b, (((1,), (0,)), ((), ())), preferred_element_type=F32)

def fill_bias(bias, key_code, query_codes):
    code = key_code[...]
    below = code < query_codes[0:1, :]
    own = (code >= query_codes[1:2, :]) & (code <= query_codes[2:3, :])
    bias[...] = jnp.where(below | own, 0.0, NEGATIVE)

def fill_padded(padded, sources, lane0):
    block = jnp.concatenate([v[:, lane0 : lane0 + 2 * HD] for v in sources], axis=0)
    lane = lax.broadcasted_iota(jnp.int32, block.shape, 1)
    low = jnp.where(lane < HD, block, jnp.zeros_like(block))
    high = jnp.where(lane < HD, jnp.zeros_like(block), block)
    padded[0, 0] = low
    padded[0, 1] = pltpu.roll(low.astype(F32), HD, 1).astype(BF)
    padded[1, 0] = pltpu.roll(high.astype(F32), HD, 1).astype(BF)
    padded[1, 1] = high

def fill_turned(turned, sources, lane0):
    at = 0
    for v in sources:
        turned[:, at : at + v.shape[0]] = v[:, lane0 : lane0 + 2 * HD].astype(F32).T.astype(BF)
        at += v.shape[0]


def forward_kernel(chunk, parts, q_ref, code_ref, codes_ref, *refs):
    kv_refs = refs[:parts]
    out_ref, lse_ref, bias, keys, vt_ref = refs[parts:]
    total = code_ref.shape[0]
    rows = q_ref.shape[0]
    fill_turned(vt_ref, kv_refs, 2 * HD)
    fill_bias(bias, code_ref, codes_ref)
    fill_padded(keys, kv_refs, 0)

    def pair_step(pair, unused):
        group = pair // 2
        lanes = pl.ds(pl.multiple_of(pair * 128, 128), 128)
        q_pair = q_ref[:, lanes]
        mixed = []
        for side in range(2):
            def chunk_step(part, carry):
                top, norm, acc = carry
                at = pl.ds(pl.multiple_of(part * chunk, chunk), chunk)
                scores = dot_nt(keys[group, side, at, :], q_pair) + bias[at, :]
                new_top = jnp.maximum(top, jnp.max(scores, axis=0, keepdims=True))
                weights = jnp.exp(scores - new_top)
                shrink = jnp.exp(top - new_top)
                norm = norm * shrink + jnp.sum(weights, axis=0, keepdims=True)
                values = vt_ref[pl.ds(pl.multiple_of(group * HD, HD), HD), at]
                acc = acc * shrink + dot_nn(values, weights.astype(BF))
                return new_top, norm, acc

            carry = (jnp.full((1, rows), NEGATIVE, F32), jnp.zeros((1, rows), F32), jnp.zeros((HD, rows), F32))
            if total == chunk:
                carry = chunk_step(0, carry)
            else:
                carry = lax.fori_loop(0, total // chunk, chunk_step, carry)
            top, norm, acc = carry
            mixed.append(acc / norm)
            lse_ref[pl.ds(pair * 2 + side, 1), :] = top + jnp.log(norm)
        out_ref[:, lanes] = jnp.concatenate(mixed, axis=0).T.astype(BF)
        return unused

    lax.fori_loop(0, q_ref.shape[1] // 128, pair_step, 0)


def attend_forward(queries, key_values, key_code, query_codes):
    rows, width = queries.shape
    total = key_code.shape[0]
    chunk = min(total, 1024)
    return pl.pallas_call(
        functools.partial(forward_kernel, chunk, len(key_values)),
        out_shape=(
            jax.ShapeDtypeStruct((rows, width), BF),
            jax.ShapeDtypeStruct((width // HD, rows), F32),
        ),
        scratch_shapes=[
            pltpu.VMEM((total, rows), F32),
            pltpu.VMEM((2, 2, total, 128), BF),
            pltpu.VMEM((128, total), BF),
        ],
        compiler_params=pltpu.CompilerParams(vmem_limit_bytes=(32 if total <= 1024 else 58) << 20),
        cost_estimate=LIGHT,
        name="attend_forward",
    )(queries, key_code, query_codes, *key_values)

def backward_kernel(
    chunk, parts, q_ref, code_ref, codes_ref, att_ref, branch_ref, lse_ref, rot_ref, o0, o1, o2, o3, *refs
):
    kv_refs = refs[:parts]
    dq_ref, dkv_ref, grad_ref, bias, keys, values, kt_ref, delta, dk_acc, dv_acc = refs[parts:]
    total = code_ref.shape[0]
    rows = q_ref.shape[0]
    width = q_ref.shape[1]
    heads = width // HD
    fill_turned(kt_ref, kv_refs, 0)
    fill_bias(bias, code_ref, codes_ref)
    fill_padded(keys, kv_refs, 0)
    fill_padded(values, kv_refs, 128)
    block = o0.shape[1]
    grad = jnp.zeros((rows, width), F32)
    for r, piece in enumerate((o0, o1, o2, o3)):
        grad += dot_nt(branch_ref[:, r * block : (r + 1) * block], piece[...])
    grad_ref[...] = grad.astype(BF)
    owner = lax.broadcasted_iota(jnp.int32, (heads, width), 1) // HD
    member = jnp.where(owner == lax.broadcasted_iota(jnp.int32, (heads, width), 0), 1.0, 0.0)
    product = att_ref[...].astype(F32) * grad_ref[...].astype(F32)
    delta[...] = lax.dot_general(member, product, (((1,), (1,)), ((), ())), precision=lax.Precision.HIGHEST, preferred_element_type=F32)
    dk_acc[...] = jnp.zeros_like(dk_acc)
    dv_acc[...] = jnp.zeros_like(dv_acc)
    half = HD // 2

    def pair_step(pair, unused):
        group = pair // 2
        lanes = pl.ds(pl.multiple_of(pair * 128, 128), 128)
        q_pair = q_ref[:, lanes]
        g_pair = grad_ref[:, lanes]
        turned = []
        for side in range(2):
            head = pl.ds(pair * 2 + side, 1)
            lse = lse_ref[head, :]
            dlt = delta[head, :]
            def chunk_step(part, acc):
                at = pl.ds(pl.multiple_of(part * chunk, chunk), chunk)
                scores = dot_nt(keys[group, side, at, :], q_pair) + bias[at, :]
                probs = jnp.exp(scores - lse)
                dprobs = dot_nt(values[group, side, at, :], g_pair)
                dscores = (probs * (dprobs - dlt)).astype(BF)
                dv_acc[group, side, at, :] += dot_nn(probs.astype(BF), g_pair)
                dk_acc[group, side, at, :] += dot_nn(dscores, q_pair)
                kt = kt_ref[pl.ds(pl.multiple_of(group * HD, HD), HD), at]
                return acc + dot_nn(kt, dscores)
            acc = jnp.zeros((HD, rows), F32)
            if total == chunk:
                acc = chunk_step(0, acc)
            else:
                acc = lax.fori_loop(0, total // chunk, chunk_step, acc)
            acc = acc * (1.0 / HD)
            first, second = acc[:half], acc[half:]
            cosine, sine = rot_ref[:half, :], rot_ref[half:, :]
            turned.append(first * cosine + second * sine)
            turned.append(second * cosine - first * sine)
        dq_ref[:, lanes] = jnp.concatenate(turned, axis=0).T.astype(BF)
        return unused

    lax.fori_loop(0, width // 128, pair_step, 0)
    lane = lax.broadcasted_iota(jnp.int32, (total, 128), 1)
    for which, acc in ((0, dk_acc), (1, dv_acc)):
        zero = acc[0, 0] + pltpu.roll(acc[0, 1], HD, 1)
        one = pltpu.roll(acc[1, 0], HD, 1) + acc[1, 1]
        dkv_ref[:, which * 128 : (which + 1) * 128] = jnp.where(lane < HD, zero, one)

def attend_backward(
    queries, key_values, key_code, query_codes, attended, grad_branch, lse, turn, out_pieces
):
    rows, width = queries.shape
    total = key_code.shape[0]
    chunk = min(total, 1024)
    return pl.pallas_call(
        functools.partial(backward_kernel, chunk, len(key_values)),
        out_shape=(jax.ShapeDtypeStruct((rows, width), BF), jax.ShapeDtypeStruct((total, 256), F32)),
        scratch_shapes=[
            pltpu.VMEM((rows, width), BF),
            pltpu.VMEM((total, rows), F32),
            pltpu.VMEM((2, 2, total, 128), BF),
            pltpu.VMEM((2, 2, total, 128), BF),
            pltpu.VMEM((128, total), BF),
            pltpu.VMEM((width // HD, rows), F32),
            pltpu.VMEM((2, 2, total, 128), F32),
            pltpu.VMEM((2, 2, total, 128), F32),
        ],
        compiler_params=pltpu.CompilerParams(vmem_limit_bytes=(32 if total <= 1024 else 58) << 20),
        cost_estimate=LIGHT,
        name="attend_backward",
    )(queries, key_code, query_codes, attended, grad_branch, lse, turn, *out_pieces, *key_values)


def out_kernel(attended_ref, o0, o1, o2, o3, branch_ref):
    block = o0.shape[1]
    for r, piece in enumerate((o0, o1, o2, o3)):
        branch_ref[:, r * block : (r + 1) * block] = dot_nn(attended_ref[...], piece[...]).astype(BF)


def out_project(attended, out_pieces):
    return pl.pallas_call(
        out_kernel,
        out_shape=jax.ShapeDtypeStruct((attended.shape[0], 4 * out_pieces[0].shape[1]), BF),
        compiler_params=pltpu.CompilerParams(vmem_limit_bytes=60 << 20),
        cost_estimate=LIGHT,
        name="out_project",
    )(attended, *out_pieces)


def rows_at(index, size):
    return pl.ds(pl.multiple_of(index * size, size), size)


def half_turn(block):
    lane = lax.broadcasted_iota(jnp.int32, block.shape, 1)
    return jnp.where(lane % HD < HD // 2, pltpu.roll(block, 128 - HD // 2, 1), pltpu.roll(block, HD // 2, 1))


def project_kv_kernel(x_ref, scale_ref, cos_ref, sin_ref, p0, p1, p2, p3, normed_ref, kv_ref):
    block = x_ref.shape[1] // 4
    total = jnp.zeros(kv_ref.shape, F32)
    for r, piece in enumerate((p0, p1, p2, p3)):
        lanes = slice(r * block, (r + 1) * block)
        rows = block // piece.shape[1]
        gain = jnp.concatenate([piece[block + i : block + i + 1, :] for i in range(rows)], axis=1)
        low = (x_ref[:, lanes].astype(F32) * scale_ref[...] * gain.astype(F32)).astype(BF)
        normed_ref[:, lanes] = low
        total += dot_nn(low, piece[:block, :])
    keys = total[:, :128]
    kv_ref[:, :128] = (keys * cos_ref[...] + half_turn(keys) * sin_ref[...]).astype(BF)
    kv_ref[:, 128:] = total[:, 128:].astype(BF)


def project_kv(tokens, scale, cos_table, sin_table, pieces):
    rows, model = tokens.shape
    return pl.pallas_call(
        project_kv_kernel,
        out_shape=(
            jax.ShapeDtypeStruct((rows, model), BF),
            jax.ShapeDtypeStruct((rows, pieces[0].shape[1]), BF),
        ),
        compiler_params=pltpu.CompilerParams(vmem_limit_bytes=24 << 20),
        cost_estimate=LIGHT,
        name="project_kv",
    )(tokens, scale, cos_table, sin_table, *pieces)


def project_q_kernel(normed_ref, cos_ref, sin_ref, p0, p1, p2, p3, q_ref):
    block = p0.shape[0]
    total = jnp.zeros(q_ref.shape, F32)
    for r, piece in enumerate((p0, p1, p2, p3)):
        total += dot_nn(normed_ref[:, r * block : (r + 1) * block], piece[...])
    for at in range(0, q_ref.shape[1], 128):
        part = total[:, at : at + 128]
        part = part * cos_ref[...] + half_turn(part) * sin_ref[...]
        q_ref[:, at : at + 128] = part.astype(BF) * jnp.asarray(ATTN_SCALE, BF)


def project_q(normed, cos_table, sin_table, pieces):
    return pl.pallas_call(
        project_q_kernel,
        out_shape=jax.ShapeDtypeStruct((normed.shape[0], pieces[0].shape[1]), BF),
        compiler_params=pltpu.CompilerParams(vmem_limit_bytes=24 << 20),
        cost_estimate=LIGHT,
        name="project_q",
    )(normed, cos_table, sin_table, *pieces)


def early_kernel(g_ref, d0, d2, out_ref):
    block = d0.shape[1]
    out_ref[...] = dot_nt(g_ref[:, :block], d0[...]) + dot_nt(g_ref[:, 2 * block : 3 * block], d2[...])


def early_hidden(grad, own, near):
    rows, model = grad.shape
    hidden, block = own.shape
    tile = 512
    return pl.pallas_call(
        early_kernel,
        grid=(hidden // tile,),
        in_specs=[pl.BlockSpec((rows, model), lambda j: (0, 0))]
        + [pl.BlockSpec((tile, block), lambda j: (j, 0))] * 2,
        out_specs=pl.BlockSpec((rows, tile), lambda j: (0, j)),
        out_shape=jax.ShapeDtypeStruct((rows, hidden), F32),
        compiler_params=pltpu.CompilerParams(vmem_limit_bytes=60 << 20),
        cost_estimate=LIGHT,
        name="early_hidden",
    )(grad, own, near)


def mlp_kernel(side_places, index_ref, x_ref, branch_ref, gain_ref, g_ref, early_ref, *refs):
    count = len(side_places[0])
    sides, downs = (refs[:count], refs[count : 2 * count]), refs[2 * count : 2 * count + 2]
    h_ref, hidden_ref, dgate_ref, dup_ref, dh_ref = refs[2 * count + 2 : 2 * count + 7]
    grad, dgates, dups, wide, tall, sems, grad_sem = refs[2 * count + 7 :]
    step, steps = pl.program_id(0), pl.num_programs(0)
    block = h_ref.shape[1] // 4
    tile = tall.shape[2]
    index = index_ref[0]

    def copies(at_step):
        columns = rows_at(at_step, tile)
        made = []
        for which, pieces in enumerate(sides):
            for piece, (first, size, base, sign) in zip(pieces, side_places[which], strict=True):
                if sign:
                    base = pl.multiple_of(base + (index if sign > 0 else 1 - index) * size, size)
                made.append((piece.at[pl.ds(first, size), columns], wide.at[which, pl.ds(base, size), columns]))
        for k, piece in enumerate(downs):
            made.append((piece.at[columns], tall.at[at_step, k]))
        return [pltpu.make_async_copy(*ends, sems.at[at_step, n]) for n, ends in enumerate(made)]

    grad_copy = pltpu.make_async_copy(g_ref, grad, grad_sem)

    @pl.when(step == 0)
    def _():
        for copy in copies(0):
            copy.start()
        grad_copy.start()

        def begin(j, unused):
            for copy in copies(j):
                copy.start()
            return unused

        lax.fori_loop(1, steps, begin, 0)

    @pl.when(step == 0)
    def _():
        height = 128

        def norm(i, unused):
            at = rows_at(i, height)
            middle = x_ref[at, :].astype(F32) + RESIDUAL * branch_ref[at, :].astype(F32)
            square = jnp.mean(middle * middle, axis=1, keepdims=True)
            h_ref[at, :] = (middle * lax.rsqrt(square + EPSILON) * gain_ref[...]).astype(BF)
            return unused

        lax.fori_loop(0, h_ref.shape[0] // height, norm, 0, unroll=True)
        grad_copy.wait()

    for copy in copies(step):
        copy.wait()
    columns = rows_at(step, tile)
    gate = dot_nn(h_ref[...], wide[0, :, columns])
    up = dot_nn(h_ref[...], wide[1, :, columns])
    dhid = early_ref[...]
    for k in range(2):
        at = (2 * k + 1) * block
        dhid += dot_nt(grad[:, at : at + block], tall[step, k])
    sigma = jax.nn.sigmoid(gate)
    active = gate * sigma
    hidden_ref[...] = (active * up).astype(BF)
    dgate = (dhid * up * sigma * (1.0 + gate * (1.0 - sigma))).astype(BF)
    dup = (dhid * active).astype(BF)
    dgate_ref[...] = dgate
    dup_ref[...] = dup
    dgates[:, columns] = dgate
    dups[:, columns] = dup

    @pl.when(step == steps - 1)
    def _():
        def block_of(r, unused):
            at = rows_at(r, block)
            term = dot_nt(dgates[...], wide[0, at, :]) + dot_nt(dups[...], wide[1, at, :])
            dh_ref[:, at] = term.astype(BF)
            return unused

        lax.fori_loop(0, 4, block_of, 0)


def mlp(tokens, branch, gain, grad, early, index, gates, ups, downs):
    rows, model = tokens.shape
    hidden = downs[0].shape[0]
    tile = 512
    block = model // 4
    bases = ((0, 0), (block, 0), (2 * block, 0), (3 * block, 0))
    if len(gates) > 4:
        bases = ((0, 0), (block, 1), (block, -1), (2 * block, 0), (3 * block, 1), (3 * block, -1))
    calls = []
    for side in (gates, ups):
        calls.append(tuple((at * size, size, *base) for (unused, size, at), base in zip(side, bases, strict=True)))
    whole = pl.BlockSpec((rows, model), lambda j, s: (0, 0))
    out = pl.BlockSpec((rows, tile), lambda j, s: (0, j))
    far = [downs[1], downs[3]]
    count = 2 * len(gates) + 2
    return pl.pallas_call(
        functools.partial(mlp_kernel, tuple(calls)),
        grid_spec=pltpu.PrefetchScalarGridSpec(
            num_scalar_prefetch=1,
            grid=(hidden // tile,),
            in_specs=[whole, whole, pl.BlockSpec((1, model), lambda j, s: (0, 0))]
            + [pl.BlockSpec(memory_space=pl.ANY), out]
            + [pl.BlockSpec(memory_space=pl.ANY)] * count,
            out_specs=[whole] + [out] * 3 + [whole],
            scratch_shapes=[
                pltpu.VMEM((rows, model), BF),
                pltpu.VMEM((rows, hidden), BF),
                pltpu.VMEM((rows, hidden), BF),
                pltpu.VMEM((2, model, hidden), BF),
                pltpu.VMEM((hidden // tile, 2, tile, block), BF),
                pltpu.SemaphoreType.DMA((hidden // tile, count)),
                pltpu.SemaphoreType.DMA,
            ],
        ),
        out_shape=[jax.ShapeDtypeStruct((rows, model), BF)]
        + [jax.ShapeDtypeStruct((rows, hidden), BF)] * 3
        + [jax.ShapeDtypeStruct((rows, model), BF)],
        compiler_params=pltpu.CompilerParams(vmem_limit_bytes=60 << 20),
        cost_estimate=LIGHT,
        name="mlp",
    )(index, tokens, branch, gain[None], grad, early, *[v[0] for v in gates + ups], *far)


def entry_kernel(dq_ref, own_ref, got_ref, cos_ref, sin_ref, *refs):
    queries, keys, (low_ref, dh_ref) = refs[:4], refs[4:8], refs[8:]
    block = dh_ref.shape[1] // 4
    width_q = dq_ref.shape[1]
    low_ref[:, :width_q] = dq_ref[...]
    sums = own_ref[...] + got_ref[...].astype(F32)
    dk = sums[:, :128]
    low_ref[:, width_q : width_q + 128] = (dk * cos_ref[...] - half_turn(dk) * sin_ref[...]).astype(BF)
    low_ref[:, width_q + 128 :] = sums[:, 128:].astype(BF)
    low = low_ref[:, width_q:]
    for r in range(4):
        term = dot_nt(dq_ref[...], queries[r][...]) + dot_nt(low, keys[r][:block, :])
        dh_ref[:, r * block : (r + 1) * block] = term.astype(BF)


def entry_grad(dq_low, own, got, cos_table, sin_table, query_pieces, key_pieces):
    rows, width_q = dq_low.shape
    block = query_pieces[0].shape[0]
    return pl.pallas_call(
        entry_kernel,
        out_shape=(
            jax.ShapeDtypeStruct((rows, width_q + key_pieces[0].shape[1]), BF),
            jax.ShapeDtypeStruct((rows, 4 * block), BF),
        ),
        compiler_params=pltpu.CompilerParams(vmem_limit_bytes=60 << 20),
        cost_estimate=LIGHT,
        name="entry_grad",
    )(dq_low, own, got, cos_table, sin_table, *query_pieces, *key_pieces)


def outer_kernel(n_adds, a_ref, b_ref, *refs):
    total = lax.dot_general(
        a_ref[...], b_ref[...], (((0,), (0,)), ((), ())), preferred_element_type=F32
    )
    for add in refs[:n_adds]:
        total += add[...].astype(F32)
    refs[n_adds][...] = total.astype(BF)


def outer(left, right, left_blocks, right_blocks, adds, name):
    rows = left.shape[0]
    size_m, size_n = left.shape[1] // 4, right.shape[1] // 4
    first_m, count_m = left_blocks
    first_n, count_n = right_blocks
    cut_rows = count_m < 4
    wide = size_n * count_n
    in_specs = [
        pl.BlockSpec((rows, size_m), lambda i: (0, first_m + i)),
        pl.BlockSpec((rows, wide), lambda i: (0, first_n // count_n)),
    ]
    for array, first in adds:
        if cut_rows:
            in_specs.append(pl.BlockSpec((size_m, wide), lambda i, first=first: (first + i, 0)))
        else:
            in_specs.append(pl.BlockSpec((size_m, wide), lambda i, first=first: (i, first)))
    return pl.pallas_call(
        functools.partial(outer_kernel, len(adds)),
        grid=(count_m,),
        in_specs=in_specs,
        out_specs=pl.BlockSpec((size_m, wide), lambda i: (i, 0)),
        out_shape=jax.ShapeDtypeStruct((size_m * count_m, wide), BF),
        compiler_params=pltpu.CompilerParams(vmem_limit_bytes=32 << 20),
        cost_estimate=LIGHT,
        name=name,
    )(left, right, *[array for array, unused in adds])


def lift_kernel(hidden_ref, d0, d1, d2, d3, out_ref, acc):
    step = pl.program_id(0)
    block = d0.shape[1]
    for r, piece in enumerate((d0, d1, d2, d3)):
        lanes = slice(r * block, (r + 1) * block)
        term = dot_nn(hidden_ref[...], piece[...])

        @pl.when(step == 0)
        def _():
            acc[:, lanes] = term

        @pl.when(step != 0)
        def _():
            acc[:, lanes] += term

    @pl.when(step == pl.num_programs(0) - 1)
    def _():
        out_ref[...] = acc[...].astype(BF)


def lift(hidden, downs):
    rows, width = hidden.shape
    block = downs[0].shape[1]
    tile = 512
    return pl.pallas_call(
        lift_kernel,
        grid=(width // tile,),
        in_specs=[pl.BlockSpec((rows, tile), lambda j: (0, j))]
        + [pl.BlockSpec((tile, block), lambda j: (j, 0))] * 4,
        out_specs=pl.BlockSpec((rows, 4 * block), lambda j: (0, 0)),
        out_shape=jax.ShapeDtypeStruct((rows, 4 * block), BF),
        scratch_shapes=[pltpu.VMEM((rows, 4 * block), F32)],
        compiler_params=pltpu.CompilerParams(vmem_limit_bytes=32 << 20),
        cost_estimate=LIGHT,
        name="lift",
    )(hidden, *downs)


def entry_outer_kernel(n_adds, attended_ref, branch_ref, normed_ref, low_ref, *refs):
    out_ref = refs[n_adds]
    width = attended_ref.shape[1]
    head = lax.dot_general(
        attended_ref[...], branch_ref[...], (((0,), (0,)), ((), ())), preferred_element_type=F32
    )
    tail = lax.dot_general(
        normed_ref[...], low_ref[...], (((0,), (0,)), ((), ())), preferred_element_type=F32
    )
    for add in refs[:n_adds]:
        head += add[:, : head.shape[1]].astype(F32)
        tail += add[:, head.shape[1] :].astype(F32)
    out_ref[:, : head.shape[1]] = head.astype(BF)
    out_ref[:, head.shape[1] :] = tail.astype(BF)


def entry_outer(attended, branch, normed, low, first, count, adds):
    rows, heads = attended.shape
    block = branch.shape[1] // 4
    width = block + low.shape[1]
    column = pl.BlockSpec((rows, block), lambda i: (0, first + i))
    in_specs = [
        pl.BlockSpec((rows, heads), lambda i: (0, 0)),
        column,
        column,
        pl.BlockSpec(low.shape, lambda i: (0, 0)),
    ]
    for array, at in adds:
        in_specs.append(pl.BlockSpec((block, width), lambda i, at=at: (at + i, 0)))
    return pl.pallas_call(
        functools.partial(entry_outer_kernel, len(adds)),
        grid=(count,),
        in_specs=in_specs,
        out_specs=pl.BlockSpec((block, width), lambda i: (i, 0)),
        out_shape=jax.ShapeDtypeStruct((block * count, width), BF),
        compiler_params=pltpu.CompilerParams(vmem_limit_bytes=24 << 20),
        cost_estimate=LIGHT,
        name="entry_outer",
    )(attended, branch, normed, low, *[array for array, unused in adds])


def exit_kernel(index_ref, middle_ref, dh_ref, x_ref, gain_ref, out_ref):
    x = x_ref[...].astype(F32)
    scale = lax.rsqrt(jnp.mean(x * x, axis=1, keepdims=True) + EPSILON)
    weighted = gain_ref[...] * dh_ref[...].astype(F32)
    inner = jnp.mean(weighted * x, axis=1, keepdims=True)
    total = middle_ref[...] + scale * weighted - x * (scale * scale * scale * inner)
    block = x.shape[1] // 4
    for k, owner in enumerate(OWNERS):
        place = pl.multiple_of((index_ref[0] ^ owner) * block, block)
        out_ref[:, pl.ds(place, block)] = total[:, k * block : (k + 1) * block].astype(BF)


def exit_grad(index, grad_middle, grad, tokens, gain):
    rows, model = tokens.shape
    height = 256
    part = pl.BlockSpec((height, model), lambda i, s: (i, 0))
    return pl.pallas_call(
        exit_kernel,
        grid_spec=pltpu.PrefetchScalarGridSpec(
            num_scalar_prefetch=1,
            grid=(rows // height,),
            in_specs=[part, part, part, pl.BlockSpec((1, model), lambda i, s: (0, 0))],
            out_specs=part,
        ),
        out_shape=jax.ShapeDtypeStruct((rows, model), BF),
        compiler_params=pltpu.CompilerParams(vmem_limit_bytes=60 << 20),
        cost_estimate=LIGHT,
        name="exit_grad",
    )(index, grad_middle, grad, tokens, gain[None])


def after(value, *others):
    if not others:
        return value
    return lax.optimization_barrier((value, *others))[0]


def sealed(step, *values):
    skipped = lambda *v: jax.tree.map(lambda a: jnp.zeros(a.shape, a.dtype), jax.eval_shape(step, *v))
    return lax.cond(lax.optimization_barrier(jnp.asarray(True)), step, skipped, *values)


def swap_core(value):
    return lax.ppermute(value, "dp", [(i, i ^ 1) for i in range(4)])


def swap_x(value):
    return lax.ppermute(value, "dp", [(i, i ^ 2) for i in range(4)])


def swap_both(value):
    return lax.ppermute(value, "dp", [(i, i ^ 3) for i in range(4)])


def swap_ctx(value):
    return lax.ppermute(value, "ctx", [(0, 1), (1, 0)])


def two_ctx():
    return lax.axis_size("ctx") == 2


def sum_ctx(total):
    low = total.astype(BF)
    if two_ctx():
        return low.astype(F32) + swap_ctx(low).astype(F32)
    return lax.psum(low, "ctx").astype(F32)


def far_halves(one, two):
    if not two_ctx():
        return jnp.concatenate([one, two])
    half = one.shape[0] // 2
    at = lax.axis_index("ctx") * half
    return jnp.concatenate([lax.dynamic_slice_in_dim(v, at, half) for v in (one, two)])


def psum_tensor(value):
    return lax.psum(value, "tensor")


def sum_everywhere(gains):
    gains = gains + swap_ctx(gains) if two_ctx() else lax.psum(gains, "ctx")
    near, far, other, both = split4(gains, 1)
    total = near + swap_x(far)
    total = total + swap_core(after(other, total))
    total = total + swap_both(after(both, total))
    if lax.axis_size("tensor") != 4:
        return lax.psum(total, "tensor")
    for bit in (1, 2):
        total = total + lax.ppermute(total, "tensor", [(i, i ^ bit) for i in range(4)])
    return total


def swap_bits(index):
    return ((index & 1) << 1) | (index >> 1)


def take_blocks(value, indices):
    size = value.shape[1] // 4
    return jnp.concatenate(
        [lax.dynamic_slice_in_dim(value, i * size, size, 1) for i in indices], axis=1
    )


OWNERS = (0, 2, 1, 3)


def relative(value):
    mine = lax.axis_index("dp")
    return take_blocks(value, [mine ^ k for k in OWNERS])


def absolute(value):
    mine = lax.axis_index("dp")
    return take_blocks(value, [swap_bits(mine ^ k) for k in range(4)])


def split4(value, axis):
    size = value.shape[axis] // 4
    return [lax.slice_in_dim(value, r * size, (r + 1) * size, axis=axis) for r in range(4)]


def token_places(row_ids, order_row, seen_row, prompt_len, block_rows, cont_len):
    block_total = order_row.shape[0]
    block_pick = (row_ids // block_rows)[:, None] == jnp.arange(block_total, dtype=jnp.int32)[
        None, :
    ]
    chosen = jnp.sum(jnp.where(block_pick, order_row[None, :], 0), axis=1)
    global_ids = chosen * block_rows + row_ids % block_rows
    in_prompt = global_ids < prompt_len
    segment = jnp.where(in_prompt, 0, 1 + (global_ids - prompt_len) // cont_len)
    cont_count = seen_row.shape[0]
    which_cont = (segment - 1)[:, None] == jnp.arange(cont_count, dtype=jnp.int32)[None, :]
    limit = jnp.sum(jnp.where(which_cont, seen_row[None, :], 0), axis=1)
    places = jnp.where(in_prompt, global_ids, limit + (global_ids - prompt_len) % cont_len)
    return (segment, places, limit)


def norm_scale(values):
    return lax.rsqrt(jnp.mean(values * values, axis=-1, keepdims=True) + EPSILON)


def norm_back(values, scale, gain, grad):
    weighted = gain * grad
    inner = jnp.mean(weighted * values, axis=-1, keepdims=True)
    return scale * weighted - values * (scale * scale * scale) * inner


def combine(low, peer):
    if two_ctx():
        return low.astype(F32) + peer.astype(F32)
    return peer.astype(F32)


class BlockSum:
    def __init__(self, term):
        self.term = term

    def begin(self):
        other = swap_core(self.term(2, 2, ()))
        return other, self.term(1, 1, ((other, 1),))

    def cross(self, begun, *wait):
        self.other, self.sent = begun
        self.got = swap_x(after(self.sent, *wait))
        return self

    def joined(self, other, got):
        self.other, self.got = other, got
        return self

    def fold(self, *wait):
        self.low = self.term(0, 1, ((self.other, 0), (after(self.got, *wait), 0)))
        return self

    def swap(self, *wait):
        low = after(self.low, *wait)
        self.peer = swap_ctx(low) if two_ctx() else lax.psum(low, "ctx")
        return self

    def result(self):
        return combine(self.low, self.peer)


def outer_sum(left, right, cut_left, name):
    def term(k, n, adds):
        cut, whole = (k, n), (0, 4)
        if cut_left:
            return outer(left, right, cut, whole, adds, name)
        return outer(left, right, whole, cut, adds, name)

    return BlockSum(term)


def shards(
    tokens,
    cotangent,
    first_gain,
    query_weight,
    key_weight,
    value_weight,
    output_weight,
    second_gain,
    gate_weight,
    up_weight,
    down_weight,
    block_order,
    prefix_seen,
):
    ctx_size = lax.axis_size("ctx")
    local_rows = tokens.shape[0]
    group_rows = local_rows * ctx_size
    offset = lax.axis_index("ctx") * local_rows
    width_q = query_weight.shape[1]
    width_kv = key_weight.shape[1]
    block_d = query_weight.shape[0]

    query_far = swap_x(query_weight)
    query_near = swap_core(query_weight)
    gain_rows = jnp.stack([first_gain, second_gain]).reshape(-1, 2 * width_kv)
    kv_shard = jnp.concatenate(
        [
            jnp.concatenate([after(key_weight, query_near), value_weight], axis=1),
            jnp.pad(gain_rows, ((0, 32 - gain_rows.shape[0]), (0, 0))),
        ],
        axis=0,
    )
    kv_far = swap_x(kv_shard)
    kv_near = swap_core(kv_shard)
    out_far = swap_x(after(output_weight, kv_near))
    out_near = swap_core(after(output_weight, kv_near))
    wide_sent = after(far_halves(*(after(v, query_near) for v in (gate_weight, up_weight))), query_near)
    wide_got = swap_x(after(wide_sent, kv_far))

    tokens, block_order = (after(v, query_near) for v in (tokens, block_order))
    all_ids = jnp.arange(group_rows, dtype=jnp.int32)
    if two_ctx():
        all_ids = jnp.where(all_ids < local_rows, all_ids + offset, all_ids - offset)
    key_seg, key_pos, key_lim = token_places(
        all_ids, block_order[0], prefix_seen[0], group_rows // 2, local_rows // 2, CLEN
    )
    if two_ctx():
        query_seg, query_pos, query_lim = key_seg[:local_rows], key_pos[:local_rows], key_lim[:local_rows]
    else:
        query_seg = lax.dynamic_slice_in_dim(key_seg, offset, local_rows)
        query_pos = lax.dynamic_slice_in_dim(key_pos, offset, local_rows)
        query_lim = lax.dynamic_slice_in_dim(key_lim, offset, local_rows)
    key_code = (key_seg * SEGMENT_STEP + key_pos)[:, None]
    in_prompt = query_seg == 0
    below = jnp.where(in_prompt, query_pos + 1, query_lim)
    low_code = jnp.where(in_prompt, 1, query_seg * SEGMENT_STEP)
    high_code = jnp.where(in_prompt, 0, query_seg * SEGMENT_STEP + query_pos)
    query_codes = jnp.stack([below, low_code, high_code] + [below] * 5)
    half_size = HD // 2
    freq = ROPE_BASE ** (-(jnp.arange(half_size, dtype=F32) * 2.0) / HD)
    angle_t = freq[:, None] * query_pos.astype(F32)[None, :]
    turn = jnp.concatenate([jnp.cos(angle_t), jnp.sin(angle_t)], axis=0)
    cosine, sine = turn[:half_size].T, turn[half_size:].T
    cos_table = jnp.concatenate([cosine] * 4, axis=1)
    sin_table = jnp.concatenate([-sine, sine] * 2, axis=1)

    tokens = relative(tokens)
    inputs = tokens.astype(F32)
    scale_one = norm_scale(inputs)
    kv_pieces = [kv_shard, kv_far, kv_near, swap_core(kv_far)]
    gain_at = block_d + block_d // (2 * width_kv)
    gain_one, gain_two = (
        jnp.concatenate([p[i : i + gain_at - block_d].reshape(-1) for p in kv_pieces]).astype(F32)
        for i in (block_d, gain_at)
    )
    normed, key_value = project_kv(
        tokens, after(scale_one, wide_sent), cos_table, sin_table, kv_pieces
    )
    if two_ctx():
        other_kv = swap_ctx(key_value)
    else:
        other_kv = lax.all_gather(key_value, "ctx", axis=0, tiled=True)
    query_pieces = [query_weight, query_far, query_near, swap_core(query_far)]
    queries = project_q(normed, cos_table, sin_table, query_pieces)
    other_kv = after(other_kv, queries)
    key_values = (key_value, other_kv) if two_ctx() else (other_kv,)
    attended, log_total = attend_forward(queries, key_values, key_code, query_codes)
    out_far = after(out_far, queries, key_values[-1])
    out_pieces = [output_weight, out_far, out_near, swap_core(out_far)]
    branch = out_project(attended, out_pieces)
    grad_out = relative(after(cotangent, log_total)).astype(F32)
    grad_mlp = (RESIDUAL * grad_out).astype(BF)
    branch = psum_tensor(branch)

    def spread_wide(got, gate, up, down, grad_mlp):
        gate_near = swap_core(gate)
        down_near = swap_core(after(down, gate_near))
        near = gate_near, swap_core(up), swap_core(after(got, gate_near)), down_near
        early = early_hidden(grad_mlp, down, down_near)
        return swap_ctx(got) if two_ctx() else got, *near, early

    def spread_last(*values):
        return tuple(swap_core(v) for v in values)

    down_far = swap_x(after(down_weight, log_total))
    wide_other, gate_near, up_near, last_got, down_near, early = sealed(
        spread_wide, after(wide_got, log_total), gate_weight, up_weight, down_weight, grad_mlp
    )
    last_other, down_last = sealed(spread_last, wide_other, down_far)
    downs = [down_weight, down_far, down_near, down_last]
    half = block_d // 2 if two_ctx() else block_d
    far = (wide_got, wide_other) if two_ctx() else (wide_got,)
    last = (last_got, last_other) if two_ctx() else (last_got,)
    gates, ups = (
        [(own, block_d, 0), *[(v, half, at) for v in far], (near, block_d, 0), *[(v, half, at) for v in last]]
        for own, near, at in ((gate_weight, gate_near, 0), (up_weight, up_near, 1))
    )
    wait = down_last
    branch = after(branch, wait)
    normed_two, hidden, grad_gate, grad_up, grad_two = mlp(
        tokens, branch, gain_two, grad_mlp, early, lax.axis_index("ctx")[None], gates, ups, downs
    )
    two_part = grad_two
    grad_two = psum_tensor(grad_two)
    middle = inputs + RESIDUAL * after(branch, hidden).astype(F32)
    scale_two = norm_scale(middle)

    def begin(hidden, normed_two, grad_mlp, grad_gate, grad_up, *downs):
        down_sum = outer_sum(hidden, grad_mlp, False, "down_outer")
        down_sum.cross(down_sum.begin())
        gate_begun = outer_sum(normed_two, grad_gate, True, "gate_outer").begin()
        up_begun = outer_sum(normed_two, grad_up, True, "up_outer").begin()
        part = lift(hidden, downs)
        return down_sum.fold(gate_begun[1], up_begun[1], part).low, gate_begun, up_begun, part

    down_sum = BlockSum(None)
    down_sum.low, gate_begun, up_begun, mlp_part = sealed(
        begin, hidden, normed_two, grad_mlp, grad_gate, grad_up, *downs
    )
    down_sum.swap()
    gate_sum = outer_sum(normed_two, grad_gate, True, "gate_outer").cross(gate_begun)
    up_sum = outer_sum(normed_two, grad_up, True, "up_outer")
    grad_two = after(grad_two, down_sum.low)
    mlp_sum = psum_tensor(after(mlp_part, grad_two))
    up_sum.cross(up_begun, grad_two)
    grad_two = grad_two.astype(F32)

    grad_middle = grad_out + norm_back(middle, scale_two, gain_two, grad_two)
    grad_branch = (RESIDUAL * grad_middle).astype(BF)
    query_low, key_value_parts = attend_backward(
        queries,
        key_values,
        key_code,
        query_codes,
        attended,
        grad_branch,
        log_total,
        turn,
        out_pieces,
    )
    if two_ctx():
        own_part = key_value_parts[:local_rows]
        got_part = swap_ctx(key_value_parts[local_rows:].astype(BF))
    else:
        own_part = lax.psum_scatter(
            key_value_parts.astype(BF), "ctx", scatter_dimension=0, tiled=True
        ).astype(F32)
        got_part = jnp.zeros(own_part.shape, BF)
    qkv_low, grad_one = entry_grad(
        query_low, own_part, got_part, cos_table, sin_table, query_pieces, kv_pieces
    )
    gate_sum.fold(query_low)
    gate_sum.swap(got_part)

    def entry_term(attended, grad_branch, normed, qkv_low):
        return BlockSum(
            lambda k, n, adds: entry_outer(attended, grad_branch, normed, qkv_low, k, n, adds)
        )

    entry_inputs = (attended, grad_branch, normed, qkv_low)
    begun = sealed(lambda *v: entry_term(*v).begin(), *entry_inputs)
    entry_sum = entry_term(*entry_inputs).cross(begun, gate_sum.low)
    mlp_sum = after(mlp_sum, qkv_low, down_sum.peer, gate_sum.low, up_sum.fold(qkv_low).low, entry_sum.sent)
    gains = jnp.stack(
        [
            jnp.sum(grad_one.astype(F32) * inputs * scale_one, axis=0),
            jnp.sum(two_part.astype(F32) * middle * scale_two, axis=0),
        ]
    )
    grad_one = psum_tensor(after(grad_one, mlp_sum))


    up_sum.swap()

    def finish(gains, middle, mlp_sum, *values):
        gains = sum_everywhere(gains)
        entry_sum = entry_term(*values[:4]).joined(*values[4:6]).fold().swap()
        layer_out = absolute((middle + RESIDUAL * mlp_sum.astype(F32)).astype(BF))
        totals = (combine(*values[i : i + 2]) for i in (6, 8, 10))
        parts = (
            combine(entry_sum.low[:, at], entry_sum.peer[:, at])
            for at in (slice(0, block_d), slice(block_d, None))
        )
        return gains, layer_out, *totals, *parts

    gain_grad, layer_out, down_grad, gate_grad, up_grad, output_grad, qkv_grad = sealed(
        finish,
        gains,
        middle,
        mlp_sum,
        *entry_inputs,
        entry_sum.other,
        entry_sum.got,
        down_sum.low,
        down_sum.peer,
        gate_sum.low,
        gate_sum.peer,
        up_sum.low,
        up_sum.peer,
    )
    tokens_grad = exit_grad(
        lax.axis_index("dp")[None],
        grad_middle,
        after(grad_one, down_grad),
        tokens,
        gain_one,
    )
    return (
        layer_out,
        tokens_grad,
        gain_grad[0],
        qkv_grad[:, :width_q],
        qkv_grad[:, width_q : width_q + width_kv],
        qkv_grad[:, width_q + width_kv :],
        output_grad,
        gain_grad[1],
        gate_grad,
        up_grad,
        down_grad,
    )


def solution(mesh):
    return jax.shard_map(
        shards,
        mesh=mesh,
        in_specs=(
            P(("dp", "ctx"), None),
            P(("dp", "ctx"), None),
            P("dp"),
            P("dp", "tensor"),
            P("dp", "tensor"),
            P("dp", "tensor"),
            P("tensor", "dp"),
            P("dp"),
            P("dp", "tensor"),
            P("dp", "tensor"),
            P("tensor", "dp"),
            P("dp", None),
            P("dp", None),
        ),
        out_specs=(
            P(("dp", "ctx"), None),
            P(("dp", "ctx"), None),
            P("dp"),
            P("dp", "tensor"),
            P("dp", "tensor"),
            P("dp", "tensor"),
            P("tensor", "dp"),
            P("dp"),
            P("dp", "tensor"),
            P("dp", "tensor"),
            P("tensor", "dp"),
        ),
        check_vma=False,
    )
```

```python
import functools

import jax
import jax.numpy as jnp
from jax import lax
from jax.experimental import pallas as pl
from jax.experimental.pallas import tpu as pltpu
from jax.sharding import PartitionSpec as P

HD = 64
CLEN = 512

EPSILON = 1e-05
ROPE_BASE = 10000000.0
ATTN_SCALE = 0.015625
RESIDUAL = 0.22
NEGATIVE = -1e30
SEGMENT_STEP = 1 << 16
BF = jnp.bfloat16
F32 = jnp.float32
LIGHT = pl.CostEstimate(flops=1, bytes_accessed=1, transcendentals=0)


def dot_nt(a, b):
    return lax.dot_general(a, b, (((1,), (1,)), ((), ())), preferred_element_type=F32)

def dot_nn(a, b):
    return lax.dot_general(a, b, (((1,), (0,)), ((), ())), preferred_element_type=F32)

def fill_bias(bias, key_code, query_codes):
    code = key_code[...]
    below = code < query_codes[0:1, :]
    own = (code >= query_codes[1:2, :]) & (code <= query_codes[2:3, :])
    bias[...] = jnp.where(below | own, 0.0, NEGATIVE)

def fill_padded(padded, sources, lane0):
    block = jnp.concatenate([v[:, lane0 : lane0 + 2 * HD] for v in sources], axis=0)
    lane = lax.broadcasted_iota(jnp.int32, block.shape, 1)
    low = jnp.where(lane < HD, block, jnp.zeros_like(block))
    high = jnp.where(lane < HD, jnp.zeros_like(block), block)
    padded[0, 0] = low
    padded[0, 1] = pltpu.roll(low.astype(F32), HD, 1).astype(BF)
    padded[1, 0] = pltpu.roll(high.astype(F32), HD, 1).astype(BF)
    padded[1, 1] = high

def fill_turned(turned, sources, lane0):
    at = 0
    for v in sources:
        turned[:, at : at + v.shape[0]] = v[:, lane0 : lane0 + 2 * HD].astype(F32).T.astype(BF)
        at += v.shape[0]


def forward_kernel(chunk, parts, q_ref, code_ref, codes_ref, *refs):
    kv_refs = refs[:parts]
    out_ref, lse_ref, bias, keys, vt_ref = refs[parts:]
    total = code_ref.shape[0]
    rows = q_ref.shape[0]
    fill_turned(vt_ref, kv_refs, 2 * HD)
    fill_bias(bias, code_ref, codes_ref)
    fill_padded(keys, kv_refs, 0)

    def pair_step(pair, unused):
        group = pair // 2
        lanes = pl.ds(pl.multiple_of(pair * 128, 128), 128)
        q_pair = q_ref[:, lanes]
        mixed = []
        for side in range(2):
            def chunk_step(part, carry):
                top, norm, acc = carry
                at = pl.ds(pl.multiple_of(part * chunk, chunk), chunk)
                scores = dot_nt(keys[group, side, at, :], q_pair) + bias[at, :]
                new_top = jnp.maximum(top, jnp.max(scores, axis=0, keepdims=True))
                weights = jnp.exp(scores - new_top)
                shrink = jnp.exp(top - new_top)
                norm = norm * shrink + jnp.sum(weights, axis=0, keepdims=True)
                values = vt_ref[pl.ds(pl.multiple_of(group * HD, HD), HD), at]
                acc = acc * shrink + dot_nn(values, weights.astype(BF))
                return new_top, norm, acc

            carry = (jnp.full((1, rows), NEGATIVE, F32), jnp.zeros((1, rows), F32), jnp.zeros((HD, rows), F32))
            if total == chunk:
                carry = chunk_step(0, carry)
            else:
                carry = lax.fori_loop(0, total // chunk, chunk_step, carry)
            top, norm, acc = carry
            mixed.append(acc / norm)
            lse_ref[pl.ds(pair * 2 + side, 1), :] = top + jnp.log(norm)
        out_ref[:, lanes] = jnp.concatenate(mixed, axis=0).T.astype(BF)
        return unused

    lax.fori_loop(0, q_ref.shape[1] // 128, pair_step, 0)


def attend_forward(queries, key_values, key_code, query_codes):
    rows, width = queries.shape
    total = key_code.shape[0]
    chunk = min(total, 1024)
    return pl.pallas_call(
        functools.partial(forward_kernel, chunk, len(key_values)),
        out_shape=(
            jax.ShapeDtypeStruct((rows, width), BF),
            jax.ShapeDtypeStruct((width // HD, rows), F32),
        ),
        scratch_shapes=[
            pltpu.VMEM((total, rows), F32),
            pltpu.VMEM((2, 2, total, 128), BF),
            pltpu.VMEM((128, total), BF),
        ],
        compiler_params=pltpu.CompilerParams(vmem_limit_bytes=(32 if total <= 1024 else 58) << 20),
        cost_estimate=LIGHT,
        name="attend_forward",
    )(queries, key_code, query_codes, *key_values)

def backward_kernel(
    chunk, parts, q_ref, code_ref, codes_ref, att_ref, branch_ref, lse_ref, rot_ref, o0, o1, o2, o3, *refs
):
    kv_refs = refs[:parts]
    dq_ref, dkv_ref, grad_ref, bias, keys, values, kt_ref, delta, dk_acc, dv_acc = refs[parts:]
    total = code_ref.shape[0]
    rows = q_ref.shape[0]
    width = q_ref.shape[1]
    heads = width // HD
    fill_turned(kt_ref, kv_refs, 0)
    fill_bias(bias, code_ref, codes_ref)
    fill_padded(keys, kv_refs, 0)
    fill_padded(values, kv_refs, 128)
    block = o0.shape[1]
    grad = jnp.zeros((rows, width), F32)
    for r, piece in enumerate((o0, o1, o2, o3)):
        grad += dot_nt(branch_ref[:, r * block : (r + 1) * block], piece[...])
    grad_ref[...] = grad.astype(BF)
    owner = lax.broadcasted_iota(jnp.int32, (heads, width), 1) // HD
    member = jnp.where(owner == lax.broadcasted_iota(jnp.int32, (heads, width), 0), 1.0, 0.0)
    product = att_ref[...].astype(F32) * grad_ref[...].astype(F32)
    delta[...] = lax.dot_general(member, product, (((1,), (1,)), ((), ())), precision=lax.Precision.HIGHEST, preferred_element_type=F32)
    dk_acc[...] = jnp.zeros_like(dk_acc)
    dv_acc[...] = jnp.zeros_like(dv_acc)
    half = HD // 2

    def pair_step(pair, unused):
        group = pair // 2
        lanes = pl.ds(pl.multiple_of(pair * 128, 128), 128)
        q_pair = q_ref[:, lanes]
        g_pair = grad_ref[:, lanes]
        turned = []
        for side in range(2):
            head = pl.ds(pair * 2 + side, 1)
            lse = lse_ref[head, :]
            dlt = delta[head, :]
            def chunk_step(part, acc):
                at = pl.ds(pl.multiple_of(part * chunk, chunk), chunk)
                scores = dot_nt(keys[group, side, at, :], q_pair) + bias[at, :]
                probs = jnp.exp(scores - lse)
                dprobs = dot_nt(values[group, side, at, :], g_pair)
                dscores = (probs * (dprobs - dlt)).astype(BF)
                dv_acc[group, side, at, :] += dot_nn(probs.astype(BF), g_pair)
                dk_acc[group, side, at, :] += dot_nn(dscores, q_pair)
                kt = kt_ref[pl.ds(pl.multiple_of(group * HD, HD), HD), at]
                return acc + dot_nn(kt, dscores)
            acc = jnp.zeros((HD, rows), F32)
            if total == chunk:
                acc = chunk_step(0, acc)
            else:
                acc = lax.fori_loop(0, total // chunk, chunk_step, acc)
            acc = acc * (1.0 / HD)
            first, second = acc[:half], acc[half:]
            cosine, sine = rot_ref[:half, :], rot_ref[half:, :]
            turned.append(first * cosine + second * sine)
            turned.append(second * cosine - first * sine)
        dq_ref[:, lanes] = jnp.concatenate(turned, axis=0).T.astype(BF)
        return unused

    lax.fori_loop(0, width // 128, pair_step, 0)
    lane = lax.broadcasted_iota(jnp.int32, (total, 128), 1)
    for which, acc in ((0, dk_acc), (1, dv_acc)):
        zero = acc[0, 0] + pltpu.roll(acc[0, 1], HD, 1)
        one = pltpu.roll(acc[1, 0], HD, 1) + acc[1, 1]
        dkv_ref[:, which * 128 : (which + 1) * 128] = jnp.where(lane < HD, zero, one)

def attend_backward(
    queries, key_values, key_code, query_codes, attended, grad_branch, lse, turn, out_pieces
):
    rows, width = queries.shape
    total = key_code.shape[0]
    chunk = min(total, 1024)
    return pl.pallas_call(
        functools.partial(backward_kernel, chunk, len(key_values)),
        out_shape=(jax.ShapeDtypeStruct((rows, width), BF), jax.ShapeDtypeStruct((total, 256), F32)),
        scratch_shapes=[
            pltpu.VMEM((rows, width), BF),
            pltpu.VMEM((total, rows), F32),
            pltpu.VMEM((2, 2, total, 128), BF),
            pltpu.VMEM((2, 2, total, 128), BF),
            pltpu.VMEM((128, total), BF),
            pltpu.VMEM((width // HD, rows), F32),
            pltpu.VMEM((2, 2, total, 128), F32),
            pltpu.VMEM((2, 2, total, 128), F32),
        ],
        compiler_params=pltpu.CompilerParams(vmem_limit_bytes=(32 if total <= 1024 else 58) << 20),
        cost_estimate=LIGHT,
        name="attend_backward",
    )(queries, key_code, query_codes, attended, grad_branch, lse, turn, *out_pieces, *key_values)


def out_kernel(attended_ref, o0, o1, o2, o3, branch_ref, built, sems):
    block = o0.shape[1]
    count = sems.shape[0]
    height = built.shape[0] // count
    copies = []
    for i in range(count):
        at = slice(i * height, (i + 1) * height)
        for r, piece in enumerate((o0, o1, o2, o3)):
            built[at, r * block : (r + 1) * block] = dot_nn(attended_ref[at, :], piece[...]).astype(BF)
        copies.append(pltpu.make_async_copy(built.at[at], branch_ref.at[at], sems.at[i]))
        copies[-1].start()
    for copy in copies:
        copy.wait()


def out_project(attended, out_pieces):
    out = jax.ShapeDtypeStruct((attended.shape[0], 4 * out_pieces[0].shape[1]), BF)
    return pl.pallas_call(
        out_kernel,
        out_shape=out,
        out_specs=pl.BlockSpec(memory_space=pltpu.HBM),
        scratch_shapes=[pltpu.VMEM(out.shape, BF), pltpu.SemaphoreType.DMA((2,))],
        compiler_params=pltpu.CompilerParams(vmem_limit_bytes=16 << 20),
        cost_estimate=LIGHT,
        name="out_project",
    )(attended, *out_pieces)


def rows_at(index, size):
    return pl.ds(pl.multiple_of(index * size, size), size)


def half_turn(block):
    lane = lax.broadcasted_iota(jnp.int32, block.shape, 1)
    return jnp.where(lane % HD < HD // 2, pltpu.roll(block, 128 - HD // 2, 1), pltpu.roll(block, HD // 2, 1))


def project_kv_kernel(x_ref, scale_ref, cos_ref, sin_ref, p0, p1, p2, p3, normed_ref, kv_ref):
    block = x_ref.shape[1] // 4
    total = jnp.zeros(kv_ref.shape, F32)
    for r, piece in enumerate((p0, p1, p2, p3)):
        lanes = slice(r * block, (r + 1) * block)
        rows = block // piece.shape[1]
        gain = jnp.concatenate([piece[block + i : block + i + 1, :] for i in range(rows)], axis=1)
        low = (x_ref[:, lanes].astype(F32) * scale_ref[...] * gain.astype(F32)).astype(BF)
        normed_ref[:, lanes] = low
        total += dot_nn(low, piece[:block, :])
    keys = total[:, :128]
    kv_ref[:, :128] = (keys * cos_ref[...] + half_turn(keys) * sin_ref[...]).astype(BF)
    kv_ref[:, 128:] = total[:, 128:].astype(BF)


def project_kv(tokens, scale, cos_table, sin_table, pieces):
    rows, model = tokens.shape
    return pl.pallas_call(
        project_kv_kernel,
        out_shape=(
            jax.ShapeDtypeStruct((rows, model), BF),
            jax.ShapeDtypeStruct((rows, pieces[0].shape[1]), BF),
        ),
        compiler_params=pltpu.CompilerParams(vmem_limit_bytes=24 << 20),
        cost_estimate=LIGHT,
        name="project_kv",
    )(tokens, scale, cos_table, sin_table, *pieces)


def project_q_kernel(normed_ref, cos_ref, sin_ref, p0, p1, p2, p3, q_ref):
    block = p0.shape[0]
    total = jnp.zeros(q_ref.shape, F32)
    for r, piece in enumerate((p0, p1, p2, p3)):
        total += dot_nn(normed_ref[:, r * block : (r + 1) * block], piece[...])
    for at in range(0, q_ref.shape[1], 128):
        part = total[:, at : at + 128]
        part = part * cos_ref[...] + half_turn(part) * sin_ref[...]
        q_ref[:, at : at + 128] = part.astype(BF) * jnp.asarray(ATTN_SCALE, BF)


def project_q(normed, cos_table, sin_table, pieces):
    return pl.pallas_call(
        project_q_kernel,
        out_shape=jax.ShapeDtypeStruct((normed.shape[0], pieces[0].shape[1]), BF),
        compiler_params=pltpu.CompilerParams(vmem_limit_bytes=24 << 20),
        cost_estimate=LIGHT,
        name="project_q",
    )(normed, cos_table, sin_table, *pieces)


def early_kernel(g_ref, d0, d2, out_ref):
    block = d0.shape[1]
    out_ref[...] = dot_nt(g_ref[:, :block], d0[...]) + dot_nt(g_ref[:, 2 * block : 3 * block], d2[...])


def early_hidden(grad, own, near):
    rows, model = grad.shape
    hidden, block = own.shape
    tile = 512
    return pl.pallas_call(
        early_kernel,
        grid=(hidden // tile,),
        in_specs=[pl.BlockSpec((rows, model), lambda j: (0, 0))]
        + [pl.BlockSpec((tile, block), lambda j: (j, 0))] * 2,
        out_specs=pl.BlockSpec((rows, tile), lambda j: (0, j)),
        out_shape=jax.ShapeDtypeStruct((rows, hidden), F32),
        compiler_params=pltpu.CompilerParams(vmem_limit_bytes=60 << 20),
        cost_estimate=LIGHT,
        name="early_hidden",
    )(grad, own, near)


def mlp_kernel(side_places, index_ref, x_hbm, branch_hbm, gain_ref, g_ref, early_ref, *refs):
    count = len(side_places[0])
    sides, downs = (refs[:count], refs[count : 2 * count]), refs[2 * count : 2 * count + 2]
    h_ref, hidden_ref, dgate_ref, dup_ref, dh_ref = refs[2 * count + 2 : 2 * count + 7]
    grad, dgates, dups, built, wide, tall, sems, grad_sem, out_sems, x_ref, branch_ref, in_sems = refs[
        2 * count + 7 :
    ]
    step, steps = pl.program_id(0), pl.num_programs(0)
    block = h_ref.shape[1] // 4
    tile = tall.shape[2]
    index = index_ref[0]

    def copies(at_step):
        columns = rows_at(at_step, tile)
        made = []
        for which, pieces in enumerate(sides):
            for piece, (first, size, base, sign) in zip(pieces, side_places[which], strict=True):
                if sign:
                    base = pl.multiple_of(base + (index if sign > 0 else 1 - index) * size, size)
                made.append((piece.at[pl.ds(first, size), columns], wide.at[which, pl.ds(base, size), columns]))
        for k, piece in enumerate(downs):
            made.append((piece.at[columns], tall.at[at_step, k]))
        return [pltpu.make_async_copy(*ends, sems.at[at_step, n]) for n, ends in enumerate(made)]

    grad_copy = pltpu.make_async_copy(g_ref, grad, grad_sem)

    def out_copy(r):
        at = rows_at(r, block)
        return pltpu.make_async_copy(built.at[:, at], dh_ref.at[:, at], out_sems.at[r])

    height = 128

    def in_copies(i):
        at = rows_at(i, height)
        return [
            pltpu.make_async_copy(there.at[at], here.at[at], in_sems.at[k, i])
            for k, (there, here) in enumerate(((x_hbm, x_ref), (branch_hbm, branch_ref)))
        ]

    @pl.when(step == 0)
    def _():
        for i in range(in_sems.shape[1]):
            for copy in in_copies(i):
                copy.start()
        for copy in copies(0):
            copy.start()
        grad_copy.start()

        def begin(j, unused):
            for copy in copies(j):
                copy.start()
            return unused

        lax.fori_loop(1, steps, begin, 0)

    @pl.when(step == 0)
    def _():
        def norm(i, unused):
            at = rows_at(i, height)
            for copy in in_copies(i):
                copy.wait()
            middle = x_ref[at, :].astype(F32) + RESIDUAL * branch_ref[at, :].astype(F32)
            square = jnp.mean(middle * middle, axis=1, keepdims=True)
            h_ref[at, :] = (middle * lax.rsqrt(square + EPSILON) * gain_ref[...]).astype(BF)
            return unused

        lax.fori_loop(0, h_ref.shape[0] // height, norm, 0, unroll=True)
        grad_copy.wait()

    for copy in copies(step):
        copy.wait()
    columns = rows_at(step, tile)
    gate = dot_nn(h_ref[...], wide[0, :, columns])
    up = dot_nn(h_ref[...], wide[1, :, columns])
    dhid = early_ref[...]
    for k in range(2):
        at = (2 * k + 1) * block
        dhid += dot_nt(grad[:, at : at + block], tall[step, k])
    sigma = jax.nn.sigmoid(gate)
    active = gate * sigma
    hidden_ref[...] = (active * up).astype(BF)
    dgate = (dhid * up * sigma * (1.0 + gate * (1.0 - sigma))).astype(BF)
    dup = (dhid * active).astype(BF)
    dgate_ref[...] = dgate
    dup_ref[...] = dup
    dgates[:, columns] = dgate
    dups[:, columns] = dup

    @pl.when(step == steps - 1)
    def _():
        def block_of(r, unused):
            at = rows_at(r, block)
            term = dot_nt(dgates[...], wide[0, at, :]) + dot_nt(dups[...], wide[1, at, :])
            built[:, at] = term.astype(BF)
            out_copy(r).start()
            return unused

        def end(r, unused):
            out_copy(r).wait()
            return unused

        lax.fori_loop(0, 4, block_of, 0)
        lax.fori_loop(0, 4, end, 0)


def mlp(tokens, branch, gain, grad, early, index, gates, ups, downs):
    rows, model = tokens.shape
    hidden = downs[0].shape[0]
    tile = 512
    block = model // 4
    bases = ((0, 0), (block, 0), (2 * block, 0), (3 * block, 0))
    if len(gates) > 4:
        bases = ((0, 0), (block, 1), (block, -1), (2 * block, 0), (3 * block, 1), (3 * block, -1))
    calls = []
    for side in (gates, ups):
        calls.append(tuple((at * size, size, *base) for (unused, size, at), base in zip(side, bases, strict=True)))
    whole = pl.BlockSpec((rows, model), lambda j, s: (0, 0))
    out = pl.BlockSpec((rows, tile), lambda j, s: (0, j))
    far = [downs[1], downs[3]]
    count = 2 * len(gates) + 2
    return pl.pallas_call(
        functools.partial(mlp_kernel, tuple(calls)),
        grid_spec=pltpu.PrefetchScalarGridSpec(
            num_scalar_prefetch=1,
            grid=(hidden // tile,),
            in_specs=[pl.BlockSpec(memory_space=pl.ANY)] * 2
            + [pl.BlockSpec((1, model), lambda j, s: (0, 0))]
            + [pl.BlockSpec(memory_space=pl.ANY), out]
            + [pl.BlockSpec(memory_space=pl.ANY)] * count,
            out_specs=[whole] + [out] * 3 + [pl.BlockSpec(memory_space=pltpu.HBM)],
            scratch_shapes=[
                pltpu.VMEM((rows, model), BF),
                pltpu.VMEM((rows, hidden), BF),
                pltpu.VMEM((rows, hidden), BF),
                pltpu.VMEM((rows, model), BF),
                pltpu.VMEM((2, model, hidden), BF),
                pltpu.VMEM((hidden // tile, 2, tile, block), BF),
                pltpu.SemaphoreType.DMA((hidden // tile, count)),
                pltpu.SemaphoreType.DMA,
                pltpu.SemaphoreType.DMA((4,)),
                pltpu.VMEM((rows, model), BF),
                pltpu.VMEM((rows, model), BF),
                pltpu.SemaphoreType.DMA((2, rows // 128)),
            ],
        ),
        out_shape=[jax.ShapeDtypeStruct((rows, model), BF)]
        + [jax.ShapeDtypeStruct((rows, hidden), BF)] * 3
        + [jax.ShapeDtypeStruct((rows, model), BF)],
        compiler_params=pltpu.CompilerParams(vmem_limit_bytes=60 << 20),
        cost_estimate=LIGHT,
        name="mlp",
    )(index, tokens, branch, gain[None], grad, early, *[v[0] for v in gates + ups], *far)


def entry_kernel(dq_ref, own_ref, got_ref, cos_ref, sin_ref, *refs):
    queries, keys, (low_ref, dh_ref) = refs[:4], refs[4:8], refs[8:]
    block = dh_ref.shape[1] // 4
    width_q = dq_ref.shape[1]
    low_ref[:, :width_q] = dq_ref[...]
    sums = own_ref[...] + got_ref[...].astype(F32)
    dk = sums[:, :128]
    low_ref[:, width_q : width_q + 128] = (dk * cos_ref[...] - half_turn(dk) * sin_ref[...]).astype(BF)
    low_ref[:, width_q + 128 :] = sums[:, 128:].astype(BF)
    low = low_ref[:, width_q:]
    for r in range(4):
        term = dot_nt(dq_ref[...], queries[r][...]) + dot_nt(low, keys[r][:block, :])
        dh_ref[:, r * block : (r + 1) * block] = term.astype(BF)


def entry_grad(dq_low, own, got, cos_table, sin_table, query_pieces, key_pieces):
    rows, width_q = dq_low.shape
    block = query_pieces[0].shape[0]
    return pl.pallas_call(
        entry_kernel,
        out_shape=(
            jax.ShapeDtypeStruct((rows, width_q + key_pieces[0].shape[1]), BF),
            jax.ShapeDtypeStruct((rows, 4 * block), BF),
        ),
        compiler_params=pltpu.CompilerParams(vmem_limit_bytes=60 << 20),
        cost_estimate=LIGHT,
        name="entry_grad",
    )(dq_low, own, got, cos_table, sin_table, *query_pieces, *key_pieces)


def outer_kernel(n_adds, a_ref, b_ref, *refs):
    total = lax.dot_general(
        a_ref[...], b_ref[...], (((0,), (0,)), ((), ())), preferred_element_type=F32
    )
    for add in refs[:n_adds]:
        total += add[...].astype(F32)
    refs[n_adds][...] = total.astype(BF)


def outer(left, right, left_blocks, right_blocks, adds, name):
    rows = left.shape[0]
    size_m, size_n = left.shape[1] // 4, right.shape[1] // 4
    first_m, count_m = left_blocks
    first_n, count_n = right_blocks
    cut_rows = count_m < 4
    wide = size_n * count_n
    in_specs = [
        pl.BlockSpec((rows, size_m), lambda i: (0, first_m + i)),
        pl.BlockSpec((rows, wide), lambda i: (0, first_n // count_n)),
    ]
    for array, first in adds:
        if cut_rows:
            in_specs.append(pl.BlockSpec((size_m, wide), lambda i, first=first: (first + i, 0)))
        else:
            in_specs.append(pl.BlockSpec((size_m, wide), lambda i, first=first: (i, first)))
    return pl.pallas_call(
        functools.partial(outer_kernel, len(adds)),
        grid=(count_m,),
        in_specs=in_specs,
        out_specs=pl.BlockSpec((size_m, wide), lambda i: (i, 0)),
        out_shape=jax.ShapeDtypeStruct((size_m * count_m, wide), BF),
        compiler_params=pltpu.CompilerParams(vmem_limit_bytes=32 << 20),
        cost_estimate=LIGHT,
        name=name,
    )(left, right, *[array for array, unused in adds])


def lift_kernel(hidden_ref, d0, d1, d2, d3, out_ref, acc):
    step = pl.program_id(0)
    block = d0.shape[1]
    for r, piece in enumerate((d0, d1, d2, d3)):
        lanes = slice(r * block, (r + 1) * block)
        term = dot_nn(hidden_ref[...], piece[...])

        @pl.when(step == 0)
        def _():
            acc[:, lanes] = term

        @pl.when(step != 0)
        def _():
            acc[:, lanes] += term

    @pl.when(step == pl.num_programs(0) - 1)
    def _():
        out_ref[...] = acc[...].astype(BF)


def lift(hidden, downs):
    rows, width = hidden.shape
    block = downs[0].shape[1]
    tile = 512
    return pl.pallas_call(
        lift_kernel,
        grid=(width // tile,),
        in_specs=[pl.BlockSpec((rows, tile), lambda j: (0, j))]
        + [pl.BlockSpec((tile, block), lambda j: (j, 0))] * 4,
        out_specs=pl.BlockSpec((rows, 4 * block), lambda j: (0, 0)),
        out_shape=jax.ShapeDtypeStruct((rows, 4 * block), BF),
        scratch_shapes=[pltpu.VMEM((rows, 4 * block), F32)],
        compiler_params=pltpu.CompilerParams(vmem_limit_bytes=32 << 20),
        cost_estimate=LIGHT,
        name="lift",
    )(hidden, *downs)


def entry_outer_kernel(n_adds, attended_ref, branch_ref, normed_ref, low_ref, *refs):
    out_ref = refs[n_adds]
    width = attended_ref.shape[1]
    head = lax.dot_general(
        attended_ref[...], branch_ref[...], (((0,), (0,)), ((), ())), preferred_element_type=F32
    )
    tail = lax.dot_general(
        normed_ref[...], low_ref[...], (((0,), (0,)), ((), ())), preferred_element_type=F32
    )
    for add in refs[:n_adds]:
        head += add[:, : head.shape[1]].astype(F32)
        tail += add[:, head.shape[1] :].astype(F32)
    out_ref[:, : head.shape[1]] = head.astype(BF)
    out_ref[:, head.shape[1] :] = tail.astype(BF)


def entry_outer(attended, branch, normed, low, first, count, adds):
    rows, heads = attended.shape
    block = branch.shape[1] // 4
    width = block + low.shape[1]
    column = pl.BlockSpec((rows, block), lambda i: (0, first + i))
    in_specs = [
        pl.BlockSpec((rows, heads), lambda i: (0, 0)),
        column,
        column,
        pl.BlockSpec(low.shape, lambda i: (0, 0)),
    ]
    for array, at in adds:
        in_specs.append(pl.BlockSpec((block, width), lambda i, at=at: (at + i, 0)))
    return pl.pallas_call(
        functools.partial(entry_outer_kernel, len(adds)),
        grid=(count,),
        in_specs=in_specs,
        out_specs=pl.BlockSpec((block, width), lambda i: (i, 0)),
        out_shape=jax.ShapeDtypeStruct((block * count, width), BF),
        compiler_params=pltpu.CompilerParams(vmem_limit_bytes=24 << 20),
        cost_estimate=LIGHT,
        name="entry_outer",
    )(attended, branch, normed, low, *[array for array, unused in adds])


def exit_kernel(index_ref, middle_ref, dh_ref, x_ref, gain_ref, out_ref):
    x = x_ref[...].astype(F32)
    scale = lax.rsqrt(jnp.mean(x * x, axis=1, keepdims=True) + EPSILON)
    weighted = gain_ref[...] * dh_ref[...].astype(F32)
    inner = jnp.mean(weighted * x, axis=1, keepdims=True)
    total = middle_ref[...] + scale * weighted - x * (scale * scale * scale * inner)
    block = x.shape[1] // 4
    for k, owner in enumerate(OWNERS):
        place = pl.multiple_of((index_ref[0] ^ owner) * block, block)
        out_ref[:, pl.ds(place, block)] = total[:, k * block : (k + 1) * block].astype(BF)


def exit_grad(index, grad_middle, grad, tokens, gain):
    rows, model = tokens.shape
    height = 256
    part = pl.BlockSpec((height, model), lambda i, s: (i, 0))
    return pl.pallas_call(
        exit_kernel,
        grid_spec=pltpu.PrefetchScalarGridSpec(
            num_scalar_prefetch=1,
            grid=(rows // height,),
            in_specs=[part, part, part, pl.BlockSpec((1, model), lambda i, s: (0, 0))],
            out_specs=part,
        ),
        out_shape=jax.ShapeDtypeStruct((rows, model), BF),
        compiler_params=pltpu.CompilerParams(vmem_limit_bytes=60 << 20),
        cost_estimate=LIGHT,
        name="exit_grad",
    )(index, grad_middle, grad, tokens, gain[None])


def after(value, *others):
    if not others:
        return value
    return lax.optimization_barrier((value, *others))[0]


def sealed(step, *values):
    skipped = lambda *v: jax.tree.map(lambda a: jnp.zeros(a.shape, a.dtype), jax.eval_shape(step, *v))
    return lax.cond(lax.optimization_barrier(jnp.asarray(True)), step, skipped, *values)


def swap_core(value):
    return lax.ppermute(value, "dp", [(i, i ^ 1) for i in range(4)])


def swap_x(value):
    return lax.ppermute(value, "dp", [(i, i ^ 2) for i in range(4)])


def swap_both(value):
    return lax.ppermute(value, "dp", [(i, i ^ 3) for i in range(4)])


def swap_ctx(value):
    return lax.ppermute(value, "ctx", [(0, 1), (1, 0)])


def two_ctx():
    return lax.axis_size("ctx") == 2


def sum_ctx(total):
    low = total.astype(BF)
    if two_ctx():
        return low.astype(F32) + swap_ctx(low).astype(F32)
    return lax.psum(low, "ctx").astype(F32)


def far_halves(one, two):
    if not two_ctx():
        return jnp.concatenate([one, two])
    half = one.shape[0] // 2
    at = lax.axis_index("ctx") * half
    return jnp.concatenate([lax.dynamic_slice_in_dim(v, at, half) for v in (one, two)])


def psum_tensor(value):
    return lax.psum(value, "tensor")


def sum_everywhere(gains):
    gains = gains + swap_ctx(gains) if two_ctx() else lax.psum(gains, "ctx")
    near, far, other, both = split4(gains, 1)
    total = near + swap_x(far)
    total = total + swap_core(after(other, total))
    total = total + swap_both(after(both, total))
    if lax.axis_size("tensor") != 4:
        return lax.psum(total, "tensor")
    for bit in (1, 2):
        total = total + lax.ppermute(total, "tensor", [(i, i ^ bit) for i in range(4)])
    return total


def swap_bits(index):
    return ((index & 1) << 1) | (index >> 1)


def take_blocks(value, indices):
    size = value.shape[1] // 4
    return jnp.concatenate(
        [lax.dynamic_slice_in_dim(value, i * size, size, 1) for i in indices], axis=1
    )


OWNERS = (0, 2, 1, 3)


def relative(value):
    mine = lax.axis_index("dp")
    return take_blocks(value, [mine ^ k for k in OWNERS])


def absolute(value):
    mine = lax.axis_index("dp")
    return take_blocks(value, [swap_bits(mine ^ k) for k in range(4)])


def split4(value, axis):
    size = value.shape[axis] // 4
    return [lax.slice_in_dim(value, r * size, (r + 1) * size, axis=axis) for r in range(4)]


def token_places(row_ids, order_row, seen_row, prompt_len, block_rows, cont_len):
    block_total = order_row.shape[0]
    block_pick = (row_ids // block_rows)[:, None] == jnp.arange(block_total, dtype=jnp.int32)[
        None, :
    ]
    chosen = jnp.sum(jnp.where(block_pick, order_row[None, :], 0), axis=1)
    global_ids = chosen * block_rows + row_ids % block_rows
    in_prompt = global_ids < prompt_len
    segment = jnp.where(in_prompt, 0, 1 + (global_ids - prompt_len) // cont_len)
    cont_count = seen_row.shape[0]
    which_cont = (segment - 1)[:, None] == jnp.arange(cont_count, dtype=jnp.int32)[None, :]
    limit = jnp.sum(jnp.where(which_cont, seen_row[None, :], 0), axis=1)
    places = jnp.where(in_prompt, global_ids, limit + (global_ids - prompt_len) % cont_len)
    return (segment, places, limit)


def norm_scale(values):
    return lax.rsqrt(jnp.mean(values * values, axis=-1, keepdims=True) + EPSILON)


def norm_back(values, scale, gain, grad):
    weighted = gain * grad
    inner = jnp.mean(weighted * values, axis=-1, keepdims=True)
    return scale * weighted - values * (scale * scale * scale) * inner


def combine(low, peer):
    if two_ctx():
        return low.astype(F32) + peer.astype(F32)
    return peer.astype(F32)


class BlockSum:
    def __init__(self, term):
        self.term = term

    def begin(self):
        other = swap_core(self.term(2, 2, ()))
        return other, self.term(1, 1, ((other, 1),))

    def cross(self, begun, *wait):
        self.other, self.sent = begun
        self.got = swap_x(after(self.sent, *wait))
        return self

    def joined(self, other, got):
        self.other, self.got = other, got
        return self

    def fold(self, *wait):
        self.low = self.term(0, 1, ((self.other, 0), (after(self.got, *wait), 0)))
        return self

    def swap(self, *wait):
        low = after(self.low, *wait)
        self.peer = swap_ctx(low) if two_ctx() else lax.psum(low, "ctx")
        return self

    def result(self):
        return combine(self.low, self.peer)


def outer_sum(left, right, cut_left, name):
    def term(k, n, adds):
        cut, whole = (k, n), (0, 4)
        if cut_left:
            return outer(left, right, cut, whole, adds, name)
        return outer(left, right, whole, cut, adds, name)

    return BlockSum(term)


def shards(
    tokens,
    cotangent,
    first_gain,
    query_weight,
    key_weight,
    value_weight,
    output_weight,
    second_gain,
    gate_weight,
    up_weight,
    down_weight,
    block_order,
    prefix_seen,
):
    ctx_size = lax.axis_size("ctx")
    local_rows = tokens.shape[0]
    group_rows = local_rows * ctx_size
    offset = lax.axis_index("ctx") * local_rows
    width_q = query_weight.shape[1]
    width_kv = key_weight.shape[1]
    block_d = query_weight.shape[0]

    query_far = swap_x(query_weight)
    query_near = swap_core(query_weight)
    gain_rows = jnp.stack([first_gain, second_gain]).reshape(-1, 2 * width_kv)
    kv_shard = jnp.concatenate(
        [
            jnp.concatenate([after(key_weight, query_near), value_weight], axis=1),
            jnp.pad(gain_rows, ((0, 32 - gain_rows.shape[0]), (0, 0))),
        ],
        axis=0,
    )
    kv_far = swap_x(kv_shard)
    kv_near = swap_core(kv_shard)
    out_far = swap_x(after(output_weight, kv_near))
    out_near = swap_core(after(output_weight, kv_near))
    wide_sent = after(far_halves(*(after(v, query_near) for v in (gate_weight, up_weight))), query_near)
    wide_got = swap_x(after(wide_sent, kv_far))

    tokens, block_order = (after(v, query_near) for v in (tokens, block_order))
    all_ids = jnp.arange(group_rows, dtype=jnp.int32)
    if two_ctx():
        all_ids = jnp.where(all_ids < local_rows, all_ids + offset, all_ids - offset)
    key_seg, key_pos, key_lim = token_places(
        all_ids, block_order[0], prefix_seen[0], group_rows // 2, local_rows // 2, CLEN
    )
    if two_ctx():
        query_seg, query_pos, query_lim = key_seg[:local_rows], key_pos[:local_rows], key_lim[:local_rows]
    else:
        query_seg = lax.dynamic_slice_in_dim(key_seg, offset, local_rows)
        query_pos = lax.dynamic_slice_in_dim(key_pos, offset, local_rows)
        query_lim = lax.dynamic_slice_in_dim(key_lim, offset, local_rows)
    key_code = (key_seg * SEGMENT_STEP + key_pos)[:, None]
    in_prompt = query_seg == 0
    below = jnp.where(in_prompt, query_pos + 1, query_lim)
    low_code = jnp.where(in_prompt, 1, query_seg * SEGMENT_STEP)
    high_code = jnp.where(in_prompt, 0, query_seg * SEGMENT_STEP + query_pos)
    query_codes = jnp.stack([below, low_code, high_code] + [below] * 5)
    half_size = HD // 2
    freq = ROPE_BASE ** (-(jnp.arange(half_size, dtype=F32) * 2.0) / HD)
    angle_t = freq[:, None] * query_pos.astype(F32)[None, :]
    turn = jnp.concatenate([jnp.cos(angle_t), jnp.sin(angle_t)], axis=0)
    cosine, sine = turn[:half_size].T, turn[half_size:].T
    cos_table = jnp.concatenate([cosine] * 4, axis=1)
    sin_table = jnp.concatenate([-sine, sine] * 2, axis=1)

    tokens = relative(tokens)
    inputs = tokens.astype(F32)
    scale_one = norm_scale(inputs)
    kv_pieces = [kv_shard, kv_far, kv_near, swap_core(kv_far)]
    gain_at = block_d + block_d // (2 * width_kv)
    gain_one, gain_two = (
        jnp.concatenate([p[i : i + gain_at - block_d].reshape(-1) for p in kv_pieces]).astype(F32)
        for i in (block_d, gain_at)
    )
    normed, key_value = project_kv(
        tokens, after(scale_one, wide_sent), cos_table, sin_table, kv_pieces
    )
    if two_ctx():
        other_kv = swap_ctx(key_value)
    else:
        other_kv = lax.all_gather(key_value, "ctx", axis=0, tiled=True)
    query_pieces = [query_weight, query_far, query_near, swap_core(query_far)]
    queries = project_q(normed, cos_table, sin_table, query_pieces)
    other_kv = after(other_kv, queries)
    key_values = (key_value, other_kv) if two_ctx() else (other_kv,)
    attended, log_total = attend_forward(queries, key_values, key_code, query_codes)
    out_far = after(out_far, queries, key_values[-1])
    out_pieces = [output_weight, out_far, out_near, swap_core(out_far)]
    branch = out_project(attended, out_pieces)
    grad_out = relative(after(cotangent, log_total)).astype(F32)
    grad_mlp = (RESIDUAL * grad_out).astype(BF)
    branch = psum_tensor(branch)

    def spread_wide(got, gate, up, down, grad_mlp):
        gate_near = swap_core(gate)
        down_near = swap_core(after(down, gate_near))
        near = gate_near, swap_core(up), swap_core(after(got, gate_near)), down_near
        early = early_hidden(grad_mlp, down, down_near)
        return swap_ctx(got) if two_ctx() else got, *near, early

    def spread_last(*values):
        return tuple(swap_core(v) for v in values)

    down_far = swap_x(after(down_weight, log_total))
    wide_other, gate_near, up_near, last_got, down_near, early = sealed(
        spread_wide, after(wide_got, log_total), gate_weight, up_weight, down_weight, grad_mlp
    )
    last_other, down_last = sealed(spread_last, wide_other, down_far)
    downs = [down_weight, down_far, down_near, down_last]
    half = block_d // 2 if two_ctx() else block_d
    far = (wide_got, wide_other) if two_ctx() else (wide_got,)
    last = (last_got, last_other) if two_ctx() else (last_got,)
    gates, ups = (
        [(own, block_d, 0), *[(v, half, at) for v in far], (near, block_d, 0), *[(v, half, at) for v in last]]
        for own, near, at in ((gate_weight, gate_near, 0), (up_weight, up_near, 1))
    )
    wait = down_last
    branch = after(branch, wait)
    normed_two, hidden, grad_gate, grad_up, grad_two = mlp(
        tokens, branch, gain_two, grad_mlp, early, lax.axis_index("ctx")[None], gates, ups, downs
    )
    two_part = grad_two
    grad_two = psum_tensor(grad_two)
    middle = inputs + RESIDUAL * after(branch, hidden).astype(F32)
    scale_two = norm_scale(middle)

    def begin(hidden, normed_two, grad_mlp, grad_gate, grad_up, *downs):
        down_sum = outer_sum(hidden, grad_mlp, False, "down_outer")
        down_sum.cross(down_sum.begin())
        gate_begun = outer_sum(normed_two, grad_gate, True, "gate_outer").begin()
        up_begun = outer_sum(normed_two, grad_up, True, "up_outer").begin()
        part = lift(hidden, downs)
        return down_sum.fold(gate_begun[1], up_begun[1], part).low, gate_begun, up_begun, part

    down_sum = BlockSum(None)
    down_sum.low, gate_begun, up_begun, mlp_part = sealed(
        begin, hidden, normed_two, grad_mlp, grad_gate, grad_up, *downs
    )
    down_sum.swap()
    gate_sum = outer_sum(normed_two, grad_gate, True, "gate_outer").cross(gate_begun)
    up_sum = outer_sum(normed_two, grad_up, True, "up_outer")
    grad_two = after(grad_two, down_sum.low)
    mlp_sum = psum_tensor(after(mlp_part, grad_two))
    up_sum.cross(up_begun, grad_two)
    grad_two = grad_two.astype(F32)

    grad_middle = grad_out + norm_back(middle, scale_two, gain_two, grad_two)
    grad_branch = (RESIDUAL * grad_middle).astype(BF)
    query_low, key_value_parts = attend_backward(
        queries,
        key_values,
        key_code,
        query_codes,
        attended,
        grad_branch,
        log_total,
        turn,
        out_pieces,
    )
    if two_ctx():
        own_part = key_value_parts[:local_rows]
        got_part = swap_ctx(key_value_parts[local_rows:].astype(BF))
    else:
        own_part = lax.psum_scatter(
            key_value_parts.astype(BF), "ctx", scatter_dimension=0, tiled=True
        ).astype(F32)
        got_part = jnp.zeros(own_part.shape, BF)
    qkv_low, grad_one = entry_grad(
        query_low, own_part, got_part, cos_table, sin_table, query_pieces, kv_pieces
    )
    gate_sum.fold(query_low)
    gate_sum.swap(got_part)

    def entry_term(attended, grad_branch, normed, qkv_low):
        return BlockSum(
            lambda k, n, adds: entry_outer(attended, grad_branch, normed, qkv_low, k, n, adds)
        )

    entry_inputs = (attended, grad_branch, normed, qkv_low)
    begun = sealed(lambda *v: entry_term(*v).begin(), *entry_inputs)
    entry_sum = entry_term(*entry_inputs).cross(begun, gate_sum.low)
    mlp_sum = after(mlp_sum, qkv_low, down_sum.peer, gate_sum.low, up_sum.fold(qkv_low).low, entry_sum.sent)
    gains = jnp.stack(
        [
            jnp.sum(grad_one.astype(F32) * inputs * scale_one, axis=0),
            jnp.sum(two_part.astype(F32) * middle * scale_two, axis=0),
        ]
    )
    grad_one = psum_tensor(after(grad_one, mlp_sum))


    up_sum.swap()

    def finish(gains, middle, mlp_sum, *values):
        gains = sum_everywhere(gains)
        entry_sum = entry_term(*values[:4]).joined(*values[4:6]).fold().swap()
        layer_out = absolute((middle + RESIDUAL * mlp_sum.astype(F32)).astype(BF))
        totals = (combine(*values[i : i + 2]) for i in (6, 8, 10))
        parts = (
            combine(entry_sum.low[:, at], entry_sum.peer[:, at])
            for at in (slice(0, block_d), slice(block_d, None))
        )
        return gains, layer_out, *totals, *parts

    gain_grad, layer_out, down_grad, gate_grad, up_grad, output_grad, qkv_grad = sealed(
        finish,
        gains,
        middle,
        mlp_sum,
        *entry_inputs,
        entry_sum.other,
        entry_sum.got,
        down_sum.low,
        down_sum.peer,
        gate_sum.low,
        gate_sum.peer,
        up_sum.low,
        up_sum.peer,
    )
    tokens_grad = exit_grad(
        lax.axis_index("dp")[None],
        grad_middle,
        after(grad_one, down_grad),
        tokens,
        gain_one,
    )
    return (
        layer_out,
        tokens_grad,
        gain_grad[0],
        qkv_grad[:, :width_q],
        qkv_grad[:, width_q : width_q + width_kv],
        qkv_grad[:, width_q + width_kv :],
        output_grad,
        gain_grad[1],
        gate_grad,
        up_grad,
        down_grad,
    )


def solution(mesh):
    return jax.shard_map(
        shards,
        mesh=mesh,
        in_specs=(
            P(("dp", "ctx"), None),
            P(("dp", "ctx"), None),
            P("dp"),
            P("dp", "tensor"),
            P("dp", "tensor"),
            P("dp", "tensor"),
            P("tensor", "dp"),
            P("dp"),
            P("dp", "tensor"),
            P("dp", "tensor"),
            P("tensor", "dp"),
            P("dp", None),
            P("dp", None),
        ),
        out_specs=(
            P(("dp", "ctx"), None),
            P(("dp", "ctx"), None),
            P("dp"),
            P("dp", "tensor"),
            P("dp", "tensor"),
            P("dp", "tensor"),
            P("tensor", "dp"),
            P("dp"),
            P("dp", "tensor"),
            P("dp", "tensor"),
            P("tensor", "dp"),
        ),
        check_vma=False,
    )
```
